32 devices in a mesh: dp: 16 (over z, x, core), tensor: 2 (over y).
Axes of the slice: x: 2, y: 2, z: 4, core: 2. Of those that a mesh axis runs over, the one named last changes fastest.
Arguments:
- tokens: bfloat16 [19712, 512], P('dp'), may hold values from -6 to 6
- lengths: int32 [256], P('dp'), may hold values from 5 to 77, as said below
- qkv_weight: bfloat16 [3, 512, 512], P(None, None, 'tensor'), may hold values from -0.375 to 0.375
- qv_bias: bfloat16 [2, 512], P(None, 'tensor'), may hold values from -3 to 3
- out_weight: bfloat16 [512, 512], P('tensor'), may hold values from -0.75 to 0.75
- out_bias: bfloat16 [512], replicated, may hold values from -3 to 3
- up_weight: bfloat16 [512, 2048], P(None, 'tensor'), may hold values from -0.25 to 0.25
- up_bias: bfloat16 [2048], P('tensor'), may hold values from -3 to 3
- down_weight: bfloat16 [2048, 512], P('tensor'), may hold values from -0.1875 to 0.1875
- down_bias: bfloat16 [512], replicated, may hold values from -3 to 3
- norm_gain: bfloat16 [2, 512], replicated, may hold values from 0.099609375 to 1.8984375
- norm_shift: bfloat16 [2, 512], replicated, may hold values from -3 to 3
- cotangent: bfloat16 [19712, 512], P('dp'), may hold values from -6 to 6
Outputs:
- layer_out: bfloat16 [19712, 512], P(('dp', 'tensor'))
- input_grad: float32 [19712, 512], P(('dp', 'tensor'))
- qkv_grad: float32 [3, 512, 512], P(None, None, 'tensor')
- qv_bias_grad: float32 [2, 512], P(None, 'tensor')
- out_weight_grad: float32 [512, 512], P('tensor')
- out_bias_grad: float32 [512], replicated
- up_weight_grad: float32 [512, 2048], P(None, 'tensor')
- up_bias_grad: float32 [2048], P('tensor')
- down_weight_grad: float32 [2048, 512], P('tensor')
- down_bias_grad: float32 [512], replicated
- norm_gain_grad: float32 [2, 512], replicated
- norm_shift_grad: float32 [2, 512], replicated
The draws below stay inside these ranges and needn't reach their ends.
Inputs may be any that keep to these rules, and one draw needn't show every extreme that they name: `lengths`: in each aligned block of 16 captions one caption has exactly 77 tokens.
All inputs are finite; a program needn't handle non-finite values.
Results may differ from the reference program's by a relative error of at most 0.02.
Values may be sent and summed in bfloat16 or wider, within the bound.
A program may use at most 128 MiB of HBM per device.

```python
import jax
import jax.numpy as jnp
from jax import lax

D = 512
H = 8
HD = 64
FF = 2048
SLOTS = 77
CAP_DEV = 16
CAPTIONS = 256
TOKENS = 19712


def draw_lengths(key, part):
    key_one, key_two, key_three = jax.random.split(key, 3)
    reach = SLOTS - 5
    first = jax.random.randint(key_one, (CAPTIONS,), 0, reach + 1)
    second = jax.random.randint(key_two, (CAPTIONS,), 0, reach + 1)
    shorter = SLOTS - first * second // max(reach, 1)
    chosen = jax.random.randint(key_three, (CAPTIONS // CAP_DEV,), 0, CAP_DEV)
    position = jnp.arange(CAPTIONS) % CAP_DEV
    longest = position == jnp.repeat(chosen, CAP_DEV)
    return jnp.where(longest, SLOTS, shorter).astype(jnp.int32)


def shard_levels(stream_key, shape, pieces, least, largest):
    factor_of = 1.0
    for dim, blocks in pieces:
        heights = jax.random.uniform(jax.random.fold_in(jax.random.fold_in(stream_key, 6), dim), (blocks,), jnp.float32, least / len(pieces), largest / len(pieces))
        factor_of = factor_of * jnp.repeat(jnp.exp(heights), shape[dim] // blocks).reshape((-1,) + (1,) * (len(shape) - 1 - dim))
    return factor_of


def noise(rng, dims, spread, bound, cuts=(), kind=jnp.bfloat16):
    values = spread * jax.random.normal(rng, dims, jnp.float32)
    if cuts:
        values = values * shard_levels(rng, dims, cuts, -0.22, 0.18)
    return jnp.clip(values, -bound, bound).astype(kind)


def setup_inputs(seed: int = 0) -> dict:
    streams_of = jax.random.split(jax.random.key(seed), 14)
    tokens = noise(streams_of[0], (TOKENS, D), 1.0, 6.0, ((0, 16),))
    lengths = draw_lengths(jax.random.fold_in(streams_of[13], 71), 0)
    qkv_weight = noise(streams_of[2], (3, D, D), (D // 2) ** -0.5, 0.375, ((2, 2),))
    qv_bias = noise(streams_of[3], (2, D), 0.3, 3.0, ((1, 2),))
    out_weight = noise(streams_of[4], (D, D), (D // 8) ** -0.5, 0.75, ((0, 2),))
    out_bias = noise(streams_of[5], (D,), 0.3, 3.0)
    up_weight = noise(streams_of[6], (D, FF), D ** -0.5, 0.25, ((1, 2),))
    up_bias = noise(streams_of[7], (FF,), 0.3, 3.0, ((0, 2),))
    down_weight = noise(streams_of[8], (FF, D), (FF // 2) ** -0.5, 0.1875, ((0, 2),))
    down_bias = noise(streams_of[9], (D,), 0.3, 3.0)
    norm_gain = jnp.clip(1.0 + 0.18 * jax.random.normal(streams_of[10], (2, D), jnp.float32), 0.099609375, 1.8984375).astype(jnp.bfloat16)
    norm_shift = noise(streams_of[11], (2, D), 0.3, 3.0)
    cotangent = noise(streams_of[12], (TOKENS, D), 1.0, 6.0, ((0, 16),))
    return dict(tokens=tokens, lengths=lengths, qkv_weight=qkv_weight, qv_bias=qv_bias, out_weight=out_weight, out_bias=out_bias, up_weight=up_weight, up_bias=up_bias, down_weight=down_weight, down_bias=down_bias, norm_gain=norm_gain, norm_shift=norm_shift, cotangent=cotangent)


@jax.custom_vjp
def low(v):
    return lax.optimization_barrier(v.astype(jnp.bfloat16)).astype(jnp.float32)

@jax.custom_vjp
def low_back(v):
    return v

def low_keep(v):
    return (low(v), None)

def low_pass(kept, grad):
    return (grad,)

def back_keep(v):
    return (v, None)

def back_low(kept, grad):
    return (low(grad),)
low.defvjp(low_keep, low_pass)
low_back.defvjp(back_keep, back_low)

def matmul_high(left, right):
    return jnp.dot(left, right, precision=lax.Precision.HIGHEST)

def layer_norm(values, gain_vec, shift_vec):
    center = values - lax.optimization_barrier(jnp.mean(values, axis=-1, keepdims=True))
    variance = lax.optimization_barrier(jnp.mean(center * center, axis=-1, keepdims=True))
    return center * lax.rsqrt(variance + 1e-05) * gain_vec + shift_vec

def caption_block(rows, lengths, params):
    qkv_w, qv_b, out_w, out_b, up_w, up_b, down_w, down_b, gains, shifts = params
    count = lengths.shape[0]
    first_in = low(layer_norm(rows, gains[0], shifts[0]))
    queries = low_back(low(matmul_high(first_in, qkv_w[0]) + qv_b[0]))
    keys_all = low_back(low(matmul_high(first_in, qkv_w[1])))
    values_all = low_back(low(matmul_high(first_in, qkv_w[2]) + qv_b[1]))
    shape4 = (count, SLOTS, H, HD)
    scores = jnp.einsum('cihd,cjhd->chij', queries.reshape(shape4), keys_all.reshape(shape4), precision=lax.Precision.HIGHEST) * HD ** (-0.5)
    scores = low_back(scores)
    position = jnp.arange(SLOTS)
    allowed = (position[None, :] <= position[:, None])[None, :, :] & (position[None, None, :] < lengths[:, None, None])
    scores = jnp.where(allowed[:, None, :, :], scores, -1e+30)
    probs = low(jax.nn.softmax(scores, axis=-1))
    context = jnp.einsum('chij,cjhd->cihd', probs, values_all.reshape(shape4), precision=lax.Precision.HIGHEST)
    context = low_back(low(context.reshape(count * SLOTS, D)))
    attn_out = low_back(matmul_high(context, out_w) + out_b)
    hidden_res = rows + attn_out
    second_in = low(layer_norm(hidden_res, gains[1], shifts[1]))
    upper = low_back(matmul_high(second_in, up_w) + up_b)
    hidden = low(upper * jax.nn.sigmoid(1.702 * upper))
    mlp_out = low_back(matmul_high(hidden, down_w) + down_b)
    return hidden_res + mlp_out

def reference(tokens, lengths, qkv_weight, qv_bias, out_weight, out_bias, up_weight, up_bias, down_weight, down_bias, norm_gain, norm_shift, cotangent):
    blocks = CAPTIONS // CAP_DEV
    length_blocks = lengths.reshape(blocks, CAP_DEV)

    def forward(token_rows, *params):
        row_blocks = token_rows.reshape(blocks, CAP_DEV * SLOTS, D)
        step_fn = jax.checkpoint(lambda pair: caption_block(pair[0], pair[1], params))
        outputs = lax.map(step_fn, (row_blocks, length_blocks))
        return outputs.reshape(TOKENS, D)
    float_params = tuple((item.astype(jnp.float32) for item in (qkv_weight, qv_bias, out_weight, out_bias, up_weight, up_bias, down_weight, down_bias, norm_gain, norm_shift)))
    result, pullback = jax.vjp(forward, tokens.astype(jnp.float32), *float_params)
    grads = pullback(cotangent.astype(jnp.float32))
    return (result.astype(jnp.bfloat16), grads[0], grads[1], grads[2], grads[3], grads[4], grads[5], grads[6], grads[7], grads[8], grads[9], grads[10])
```

```python
import functools

import jax
import jax.numpy as jnp
from jax import lax
from jax.experimental import pallas as pl
from jax.experimental.pallas import tpu as pltpu
from jax.sharding import PartitionSpec as P

HD = 64
EPSILON = 1e-05
F32 = jnp.float32
BF16 = jnp.bfloat16
LOG2E = 1.4426950408889634
UNITS = 12
MESH = pl.DeviceIdType.MESH


def nn(left, right):
    return lax.dot_general(left, right, (((1,), (0,)), ((), ())), preferred_element_type=F32)


def nt(left, right):
    return lax.dot_general(left, right, (((1,), (1,)), ((), ())), preferred_element_type=F32)


def tn(left, right):
    return lax.dot_general(left, right, (((0,), (0,)), ((), ())), preferred_element_type=F32)


def loop(count, body):
    lax.fori_loop(0, count, lambda i, c: (body(i), c)[1], 0)


def norm(rows):
    center = rows - jnp.mean(rows, axis=-1, keepdims=True)
    inv = lax.rsqrt(jnp.mean(center * center, axis=-1, keepdims=True) + EPSILON)
    return center * inv, inv


def norm_back(grad, normed, inv, gain):
    t = grad * gain
    inner = jnp.mean(t * normed, axis=-1, keepdims=True)
    return inv * (t - jnp.mean(t, axis=-1, keepdims=True) - normed * inner)


def colsum(x):
    return jnp.sum(x, axis=0, keepdims=True)


class Layer:
    def __init__(self, caps, slots, pad, refs):
        self.caps, self.slots, self.pad = caps, slots, pad
        self.rows = caps * pad
        self.__dict__.update(refs)

    def head_mask(self, h, rows):
        lane = lax.broadcasted_iota(jnp.int32, (rows, 256), 1)
        return (lane >= h * HD) & (lane < (h + 1) * HD)

    def stack(self, block):
        parts = []
        for h in range(4):
            parts.append(jnp.where(self.head_mask(h, self.pad), block, jnp.zeros_like(block)))
        return jnp.concatenate(parts, axis=0)

    def unstack(self, block):
        out = None
        for h in range(4):
            part = block[h * self.pad : (h + 1) * self.pad]
            out = part if out is None else jnp.where(self.head_mask(h, self.pad), part, out)
        return out

    def widen(self, src, base, dst):
        total = src.shape[0]
        tile = self.slots * 2 if total % (self.slots * 2) == 0 else self.slots
        tile = 176 if total % 176 == 0 else total
        def conv(i):
            r = pl.ds(pl.multiple_of(i * tile, 16), tile)
            self.stage[r, :] = src[r, :].astype(F32)
        loop(total // tile, conv)
        self.stage[total : total + 16, :] = jnp.zeros((16, self.stage.shape[1]), F32)
        for c in range(self.caps):
            off = c * self.slots
            low = off // 8 * 8
            v = self.stage[pl.ds(pl.multiple_of(base + low, 8), self.pad + 8), :]
            v = v[off - low : off - low + self.pad]
            row = lax.broadcasted_iota(jnp.int32, v.shape, 0)
            v = jnp.where(row < self.slots, v, 0.0)
            dst[c * self.pad : (c + 1) * self.pad, :] = v.astype(BF16)

    def crows(self, c):
        return pl.ds(pl.multiple_of(c * self.pad, self.pad), self.pad)

    def norm_one(self):
        gain, shift = self.gains[0:1, :].astype(F32), self.shifts[0:1, :].astype(F32)
        def cap(c):
            r = self.crows(c)
            n, inv = norm(self.xs[r, :].astype(F32))
            self.n1[r, :] = n
            self.r1[r, :] = jnp.broadcast_to(inv, (self.pad, 128))
            self.a1[r, :] = (n * gain + shift).astype(BF16)
        loop(self.caps, cap)

    def qkv(self, i):
        s, j = i // 3, lax.rem(i, 3)
        out = nn(self.a1[...], self.w[s * UNITS + j]) + self.bias_qkv[i]
        self.pqkv[i] = out.astype(BF16)

    def attention(self, i):
        s, c = i // self.caps, lax.rem(i, self.caps)
        r = self.crows(c)
        q = self.pqkv[s * 3, r, :]
        km = self.stack(self.pqkv[s * 3 + 1, r, :])
        vm = self.stack(self.pqkv[s * 3 + 2, r, :])
        st = nt(km, q)
        length = self.lengths[self.cap_base + c]
        jj = lax.broadcasted_iota(jnp.int32, (self.pad, self.pad), 0)
        ii = lax.broadcasted_iota(jnp.int32, (self.pad, self.pad), 1)
        allowed = (jj <= ii) & (jj < length)
        blocks = []
        for h in range(4):
            blk = jnp.where(allowed, st[h * self.pad : (h + 1) * self.pad], -1e30)
            top = jnp.max(blk, axis=0, keepdims=True)
            e = jnp.exp2((blk - top) * (HD**-0.5 * LOG2E))
            blocks.append(e * (1.0 / jnp.sum(e, axis=0, keepdims=True)))
        p = jnp.concatenate(blocks, axis=0)
        self.probs[i] = p
        self.ctx[s, r, :] = tn(p.astype(BF16), vm).astype(BF16)

    def attention_back(self, i):
        s, c = i // self.caps, lax.rem(i, self.caps)
        r = self.crows(c)
        q = self.pqkv[s * 3, r, :]
        k = self.pqkv[s * 3 + 1, r, :]
        v = self.pqkv[s * 3 + 2, r, :]
        d = self.dctx[s, r, :]
        p = self.probs[i]
        self.dqkv[s * 3 + 2, r, :] = self.unstack(nn(p.astype(BF16), d)).astype(BF16)
        dp = nt(self.stack(v), d)
        blocks = []
        for h in range(4):
            rr = slice(h * self.pad, (h + 1) * self.pad)
            blocks.append(p[rr] * (dp[rr] - jnp.sum(dp[rr] * p[rr], axis=0, keepdims=True)))
        ds = jnp.concatenate(blocks, axis=0).astype(BF16)
        self.dqkv[s * 3 + 1, r, :] = (self.unstack(nn(ds, q)) * HD**-0.5).astype(BF16)
        self.dqkv[s * 3, r, :] = (tn(ds, self.stack(k)) * HD**-0.5).astype(BF16)

    def project(self, i):
        tile = self.rows // 4
        r = pl.ds(pl.multiple_of(i * tile, 16), tile)
        gain, shift = self.gains[1:2, :].astype(F32), self.shifts[1:2, :].astype(F32)
        c0, c1 = self.ctx[0, r, :], self.ctx[1, r, :]
        halves = []
        for n in range(2):
            w = slice(n * 256, (n + 1) * 256)
            halves.append(nn(c0, self.w[3, w, :]) + nn(c1, self.w[UNITS + 3, w, :]))
        o = jnp.concatenate(halves, axis=1)
        h1 = self.xs[r, :].astype(F32) + o + self.ob[...].astype(F32)
        self.h1[r, :] = h1
        n, inv = norm(h1)
        self.n2[r, :] = n
        self.r2[r, :] = jnp.broadcast_to(inv, (tile, 128))
        self.a2[r, :] = (n * gain + shift).astype(BF16)

    def wup(self, m):
        return (m // 4) * UNITS + 4 + lax.rem(m, 4)

    def wdown(self, m):
        return (m // 4) * UNITS + 8 + lax.rem(m, 4)

    def up(self, m):
        u = nn(self.a2[...], self.w[self.wup(m)]) + self.bias_up[m]
        sg = 0.5 * jnp.tanh(0.851 * u) + 0.5
        h = u * sg
        self.hid[m] = h.astype(BF16)
        self.act[m] = sg + 1.702 * h * (1.0 - sg)

    def down_grad(self, m):
        w = tn(self.hid[m], self.g[...]).astype(BF16)
        s, n = m // 4, lax.rem(m, 4)
        self.grads[n, s, 0:256, :] = w[:, :256]
        self.grads[n, s, 256:512, :] = w[:, 256:]

    def hidden_back(self, m):
        w = self.wdown(m)
        back = nt(self.g[:, 0:256], self.w[w, 0:256, :]) + nt(self.g[:, 256:512], self.w[w, 256:512, :])
        du = (back * self.act[m]).astype(BF16)
        self.du[m] = du
        self.small_up[m] = colsum(du.astype(F32))

    def up_grad(self, m):
        s, n = m // 4, lax.rem(m, 4)
        self.grads[4 + n, s] = tn(self.a2[...], self.du[m]).astype(BF16)

    def half_tile(self, i):
        tile = self.rows // 2
        r = pl.ds(pl.multiple_of((i // 2) * tile, 16), tile)
        return r, lax.rem(i, 2)

    def second_grad(self, i):
        r, n = self.half_tile(i)
        w = pl.ds(pl.multiple_of(n * 256, 256), 256)
        acc = None
        for m in range(8):
            part = nt(self.du[m, r, :], self.w[(m // 4) * UNITS + 4 + m % 4, w, :])
            acc = part if acc is None else acc + part
        self.e[r, w] = acc

    def mlp_out(self, i):
        r, n = self.half_tile(i)
        w = pl.ds(pl.multiple_of(n * 256, 256), 256)
        acc = self.h1[r, w] + self.db[:, w].astype(F32)
        for m in range(8):
            acc = acc + nn(self.hid[m, r, :], self.w[(m // 4) * UNITS + 8 + m % 4, w, :])
        self.h1[r, w] = acc

    def norm_two_back(self):
        gain = self.gains[1:2, :].astype(F32)
        zero = jnp.zeros((1, gain.shape[1]), F32)
        def cap(c, carry):
            gg, sg, ob, db = carry
            r = self.crows(c)
            e, n, g = self.e[r, :], self.n2[r, :], self.g[r, :].astype(F32)
            dh = g + norm_back(e, n, self.r2[r, 0:1], gain)
            self.dh1[r, :] = dh
            dob = dh.astype(BF16)
            self.dob[r, :] = dob
            return (gg + colsum(e * n), sg + colsum(e), ob + colsum(dob.astype(F32)), db + colsum(g))
        gg, sg, ob, db = lax.fori_loop(0, self.caps, cap, (zero, zero, zero, zero))
        self.small[1:2, :], self.small[3:4, :], self.small[4:5, :], self.small[5:6, :] = gg, sg, ob, db

    def out_back(self, s):
        w = tn(self.ctx[s], self.dob[...]).astype(BF16)
        self.grads[8, s, 0:256, :] = w[:, :256]
        self.grads[8, s, 256:512, :] = w[:, 256:]
        wo = s * UNITS + 3
        back = nt(self.dob[:, 0:256], self.w[wo, 0:256, :]) + nt(self.dob[:, 256:512], self.w[wo, 256:512, :])
        self.dctx[s] = back.astype(BF16)

    def qkv_grad(self, i):
        s, j = i // 3, lax.rem(i, 3)
        d = self.dqkv[i]
        self.grads[9 + j, s] = tn(self.a1[...], d).astype(BF16)
        self.small_qkv[i] = colsum(d.astype(F32))

    def first_grad(self, i):
        r, n = self.half_tile(i)
        w = pl.ds(pl.multiple_of(n * 256, 256), 256)
        acc = None
        for m in range(6):
            part = nt(self.dqkv[m, r, :], self.w[(m // 3) * UNITS + m % 3, w, :])
            acc = part if acc is None else acc + part
        self.e[r, w] = acc

    def norm_one_back(self, out, base):
        gain = self.gains[0:1, :].astype(F32)
        zero = jnp.zeros((1, gain.shape[1]), F32)
        gg, sg = zero, zero
        for c in range(self.caps):
            r = slice(c * self.pad, (c + 1) * self.pad)
            e, n = self.e[r, :], self.n1[r, :]
            dx = self.dh1[r, :] + norm_back(e, n, self.r1[r, 0:1], gain)
            out[base + c * self.slots : base + (c + 1) * self.slots, :] = dx[: self.slots]
            gg, sg = gg + colsum(e * n), sg + colsum(e)
        self.small[0:1, :], self.small[2:3, :] = gg, sg

    def layer_out(self, flat, out):
        for c in range(self.caps):
            flat[c * self.slots : (c + 1) * self.slots, :] = self.h1[c * self.pad : c * self.pad + self.slots, :]
        out[...] = flat[0 : self.caps * self.slots, :].astype(BF16)

    def pack_small(self, out):
        def put(slot, row, value):
            for i in range(value.shape[1] // 128):
                out[slot, row + i : row + i + 1, :] = value[:, i * 128 : (i + 1) * 128]
        for slot in range(2):
            out[slot] = jnp.zeros(out.shape[1:], F32)
            put(slot, 0, self.small_qkv[slot * 3])
            put(slot, 2, self.small_qkv[slot * 3 + 2])
            for n in range(4):
                put(slot, 4 + 2 * n, self.small_up[slot * 4 + n])
            for i, k in enumerate((4, 5, 0, 1, 2, 3)):
                put(slot, 12 + 4 * i, self.small[k : k + 1, :])


class Peers:
    def __init__(self):
        dp, t = lax.axis_index("dp"), lax.axis_index("tensor")
        depth = lax.axis_size("dp") // 4
        self.core = lax.rem(dp, 2)
        self.x = lax.rem(dp // 2, 2)
        self.z = dp // 4
        self.t = t
        self.to_y = (dp, 1 - t)
        self.to_x = (dp + 2 - 4 * self.x, t)
        self.to_core = (dp + 1 - 2 * self.core, t)
        self.depth = depth
        self.to_z = [(lax.rem(self.z + k, depth) * 4 + lax.rem(dp, 4), t) for k in range(1, depth)]
        self.z_of = [lax.rem(self.z + k, depth) for k in range(1, depth)]

    def all(self):
        return [self.to_y, self.to_x, self.to_core] + self.to_z

    def meet(self):
        barrier = pltpu.get_barrier_semaphore()
        peers = self.all()
        for peer in peers:
            pl.semaphore_signal(barrier, inc=1, device_id=peer, device_id_type=MESH)
        pl.semaphore_wait(barrier, len(peers))


def rows(index, size):
    return pl.ds(pl.multiple_of(index * size, size), size)


def remote(src, dst, send, recv, peer):
    return pltpu.make_async_remote_copy(src_ref=src, dst_ref=dst, send_sem=send, recv_sem=recv, device_id=peer, device_id_type=MESH)


class Weights:
    def __init__(self, peers, w, send, recv):
        self.p, self.w, self.send, self.recv = peers, w, send, recv
        self.quarter = peers.core * 2 + peers.x
        self.size = w.shape[1] // 4

    def y(self, u):
        r = rows(self.quarter, self.size)
        return remote(self.w.at[u, r], self.w.at[UNITS + u, r], self.send.at[u, 0], self.recv.at[u, 0], self.p.to_y)

    def x(self, u):
        part = self.w.at[UNITS + u, rows(self.quarter, self.size)]
        return remote(part, part, self.send.at[u, 1], self.recv.at[u, 1], self.p.to_x)

    def c(self, u):
        part = self.w.at[UNITS + u, rows(self.p.core, self.size * 2)]
        return remote(part, part, self.send.at[u, 2], self.recv.at[u, 2], self.p.to_core)

    def relay_x(self, u):
        self.y(u).wait_recv()
        self.x(u).start()

    def relay_c(self, u):
        self.x(u).wait_recv()
        self.c(u).start()

    def ready(self, u):
        self.c(u).wait_recv()

    def drain(self, u):
        self.y(u).wait_send()
        self.x(u).wait_send()
        self.c(u).wait_send()


class Reduce:
    def __init__(self, peers, refs, sem0, send, recv):
        self.p = peers
        self.g, self.cr, self.yr, self.xr, self.zr, self.f = refs
        self.sem0, self.send, self.recv = sem0, send, recv
        self.count = self.g.shape[0]
        self.full = self.g.shape[2]
        self.half, self.quarter = self.full // 2, self.full // 4
        self.shard = self.quarter // peers.depth

    def sems(self, n, k):
        return self.send.at[self.sem0 + n, k], self.recv.at[self.sem0 + n, k]

    def c(self, n):
        return remote(self.g.at[n, :, rows(1 - self.p.core, self.half)], self.cr.at[n], *self.sems(n, 0), self.p.to_core)

    def y(self, n):
        return remote(self.cr.at[n, 1], self.yr.at[n], *self.sems(n, 1), self.p.to_y)

    def x(self, n):
        return remote(self.cr.at[n, 0, rows(1 - self.p.x, self.quarter)], self.xr.at[n], *self.sems(n, 2), self.p.to_x)

    def z(self, n):
        return [
            remote(
                self.cr.at[n, 0, pl.ds(pl.multiple_of(self.p.x * self.quarter + self.p.z_of[k] * self.shard, self.shard), self.shard)],
                self.zr.at[n, k],
                *self.sems(n, 5 + k),
                self.p.to_z[k],
            )
            for k in range(self.p.depth - 1)
        ]

    def own_shard(self):
        p = self.p
        return pl.ds(pl.multiple_of(p.core * self.half + p.x * self.quarter + p.z * self.shard, self.shard), self.shard)

    def za(self, n):
        part = self.f.at[n, self.own_shard()]
        return [
            remote(part, part, *self.sems(n, 4 + self.p.depth + k), self.p.to_z[k]) for k in range(self.p.depth - 1)
        ]

    def xa(self, n):
        part = self.f.at[n, pl.ds(pl.multiple_of(self.p.core * self.half + self.p.x * self.quarter, self.quarter), self.quarter)]
        return remote(part, part, *self.sems(n, 3), self.p.to_x)

    def ca(self, n):
        part = self.f.at[n, rows(self.p.core, self.half)]
        return remote(part, part, *self.sems(n, 4), self.p.to_core)

    def c_start(self, n):
        self.c(n).start()

    def c_done(self, n):
        self.c(n).wait_recv()
        self.cr[n] = self.cr[n] + self.g[n, :, rows(self.p.core, self.half), :]
        self.y(n).start()

    def y_done(self, n):
        self.y(n).wait_recv()
        self.cr[n, 0] = self.cr[n, 0] + self.yr[n]
        self.x(n).start()

    def x_done(self, n):
        self.x(n).wait_recv()
        r = rows(self.p.x, self.quarter)
        self.cr[n, 0, r, :] = self.cr[n, 0, r, :] + self.xr[n]
        for copy in self.z(n):
            copy.start()

    def z_done(self, n):
        for copy in self.z(n):
            copy.wait_recv()
        mine = pl.ds(pl.multiple_of(self.p.x * self.quarter + self.p.z * self.shard, self.shard), self.shard)
        total = self.cr[n, 0, mine, :].astype(F32)
        for k in range(self.p.depth - 1):
            total = total + self.zr[n, k].astype(F32)
        self.f[n, self.own_shard(), :] = total.astype(self.f.dtype)
        for copy in self.za(n):
            copy.start()

    def za_done(self, n):
        for copy in self.za(n):
            copy.wait_recv()
        self.xa(n).start()

    def xa_done(self, n):
        self.xa(n).wait_recv()
        self.ca(n).start()

    def ca_done(self, n):
        self.ca(n).wait_recv()

    def drain(self, n):
        for copy in [self.c(n), self.y(n), self.x(n), self.xa(n), self.ca(n)] + self.z(n) + self.za(n):
            copy.wait_send()


STAGES = ("y_done", "x_done", "z_done", "za_done", "xa_done", "ca_done")


def step(big, small, outs, tick):
    for lag, name in enumerate(STAGES):
        unit = tick - lag

        @pl.when((unit >= 0) & (unit < UNITS))
        def _():
            getattr(big, name)(unit)
            if name == "ca_done":
                outs(unit).start()

        if small is not None:

            @pl.when(unit == UNITS)
            def _():
                getattr(small, name)(0)


def kernel(caps, slots, pad, names_in, *all_refs):
    L = Layer(caps, slots, pad, dict(zip(names_in, all_refs)))
    peers = Peers()
    L.cap_base = peers.t * caps
    weights = Weights(peers, L.w, L.wsend, L.wrecv)
    big = Reduce(peers, (L.grads, L.cr, L.yr, L.xr, L.zr, L.f), 0, L.gsend, L.grecv)
    small = Reduce(peers, (L.sg, L.scr, L.syr, L.sxr, L.szr, L.sf), UNITS, L.gsend, L.grecv)

    local = []

    def load(a, b):
        copy = pltpu.make_async_copy(a, b, L.lsem.at[len(local)])
        copy.start()
        local.append(copy)

    for j in range(3):
        load(L.wqkv_a.at[j], L.w.at[j])
    for n in range(2):
        load(L.wo_a.at[:, pl.ds(n * 256, 256)], L.w.at[3, pl.ds(n * 256, 256)])
    load(L.tok, L.tok_v)
    for n in range(4):
        load(L.wu_a.at[:, pl.ds(n * 256, 256)], L.w.at[4 + n])
    for n in range(4):
        for k in range(2):
            load(L.wd_a.at[pl.ds(n * 256, 256), pl.ds(k * 256, 256)], L.w.at[8 + n, pl.ds(k * 256, 256)])
    load(L.cot, L.cot_v)
    peers.meet()
    bias_send = [
        remote(L.qvb, L.qvb_b, L.bsem.at[0], L.bsem.at[1], peers.to_y),
        remote(L.ub, L.ub_b, L.bsem.at[2], L.bsem.at[3], peers.to_y),
    ]
    for copy in bias_send:
        copy.start()
    for copy in local:
        copy.wait()
    loop(UNITS, lambda u: weights.y(u).start())
    L.widen(L.tok_v, peers.t * caps * slots, L.xs)
    L.norm_one()
    for copy in bias_send:
        copy.wait()
    for s, (qvb, ub) in enumerate(((L.qvb, L.ub), (L.qvb_b, L.ub_b))):
        for j in range(3):
            if j == 1:
                L.bias_qkv[s * 3 + j] = jnp.zeros((1, 256), F32)
            else:
                L.bias_qkv[s * 3 + j] = qvb[j // 2 : j // 2 + 1, :].astype(F32)
        for n in range(4):
            L.bias_up[s * 4 + n] = ub[:, n * 256 : (n + 1) * 256].astype(F32)
    loop(3, L.qkv)
    loop(2, weights.relay_x)

    def attend_own(i):
        L.attention(i)

        @pl.when(i < 7)
        def _():
            weights.relay_x(2 + i)

        @pl.when(i < 8)
        def _():
            weights.relay_c(i)

    loop(caps, attend_own)
    L.widen(L.cot_v, peers.t * caps * slots, L.g)
    loop(3, lambda i: (weights.ready(i), L.qkv(3 + i)))

    def attend_other(i):
        L.attention(caps + i)

        @pl.when(i < 3)
        def _():
            weights.relay_x(9 + i)

        @pl.when(i < 4)
        def _():
            weights.relay_c(8 + i)

    loop(caps, attend_other)
    weights.ready(3)
    loop(4, L.project)
    loop(4, L.up)
    loop(4, lambda i: (weights.ready(4 + i), L.up(4 + i)))

    def down(i):
        L.down_grad(i)
        L.down_grad(4 + i)
        big.c_start(i)

        @pl.when(i > 0)
        def _():
            big.c_done(i - 1)

    loop(4, down)
    loop(4, L.hidden_back)
    big.c_done(3)
    loop(4, lambda i: (weights.ready(8 + i), L.hidden_back(4 + i)))

    outs = lambda n: pltpu.make_async_copy(L.f.at[n], L.f_out.at[n], L.osem.at[n])
    tick = functools.partial(step, big, None, outs)

    def ups(i):
        L.up_grad(i)
        L.up_grad(4 + i)
        big.c_start(4 + i)

        @pl.when(i > 0)
        def _():
            big.c_done(3 + i)

        @pl.when(lax.rem(i, 2) == 1)
        def _():
            tick(i // 2)

    loop(4, ups)
    loop(4, L.second_grad)
    big.c_done(7)
    tick(2)
    L.norm_two_back()
    loop(2, L.out_back)
    big.c_start(8)
    tick(3)

    def attend_back(i):
        L.attention_back(i)

        @pl.when(i == 1)
        def _():
            big.c_done(8)

        @pl.when(lax.rem(i, 6) == 5)
        def _():
            tick(4 + i // 6)

    loop(2 * caps, attend_back)

    def qkvs(i):
        L.qkv_grad(i)
        L.qkv_grad(3 + i)
        big.c_start(9 + i)

        @pl.when(i > 0)
        def _():
            big.c_done(8 + i)

    loop(3, qkvs)
    tick(6)
    loop(4, L.first_grad)
    big.c_done(11)
    size = caps * slots
    base = (size + 7) // 8 * 8
    L.norm_one_back(L.stage, base)
    dx_copy = pltpu.make_async_copy(L.stage.at[pl.ds(base, size)], L.dx_out, L.osem.at[UNITS])
    dx_copy.start()
    L.pack_small(L.sg.at[0])
    small.c_start(0)
    tick(7)
    loop(4, L.mlp_out)
    L.layer_out(L.stage, L.yb)
    y_copy = pltpu.make_async_copy(L.yb, L.y_out, L.osem.at[UNITS + 1])
    y_copy.start()
    small.c_done(0)
    loop(UNITS + len(STAGES) - 8, lambda i: step(big, small, outs, 8 + i))
    s_copy = pltpu.make_async_copy(L.sf.at[0], L.s_out, L.osem.at[UNITS + 2])
    s_copy.start()

    def drain(n):
        weights.drain(n)
        big.drain(n)
        outs(n).wait()

    loop(UNITS, drain)
    small.drain(0)
    dx_copy.wait()
    y_copy.wait()
    s_copy.wait()


def finish(f, s, y, dx, y_out, dx_out, qkv, out, up, down, qvb, ob, ub, db, gg, sh, f_v, wide, sem_in, sem_out, sem_io):
    ins = [pltpu.make_async_copy(f.at[n], f_v.at[n], sem_in.at[n]) for n in range(UNITS)]
    for copy in ins:
        copy.start()
    io = [pltpu.make_async_copy(y, y_out, sem_io.at[0]), pltpu.make_async_copy(dx, dx_out, sem_io.at[1])]
    for copy in io:
        copy.start()
    for n in range(UNITS):
        ins[n].wait()
        wide[n] = f_v[n].astype(F32)
        if n < 4 or n == 8:
            parts = []
            for k in range(2):
                c = pl.ds(k * 256, 256)
                dst = down.at[pl.ds(n * 256, 256), c] if n < 4 else out.at[:, c]
                parts.append((wide.at[n, c], dst))
        elif n < 8:
            parts = [(wide.at[n], up.at[:, pl.ds((n - 4) * 256, 256)])]
        else:
            parts = [(wide.at[n], qkv.at[n - 9])]
        for k, (a, b) in enumerate(parts):
            copy = pltpu.make_async_copy(a, b, sem_out.at[2 * n + k])
            copy.start()
            io.append(copy)

    def row(first, count):
        return jnp.concatenate([s[first + i : first + i + 1, :] for i in range(count)], axis=1)

    qvb[0:1, :], qvb[1:2, :] = row(0, 2), row(2, 2)
    ub[...] = row(4, 8)
    ob[...], db[...] = row(12, 4), row(16, 4)
    gg[0:1, :], gg[1:2, :] = row(20, 4), row(24, 4)
    sh[0:1, :], sh[1:2, :] = row(28, 4), row(32, 4)
    for copy in io:
        copy.wait()


def shards(depth, tokens, lengths, qkv_weight, qv_bias, out_weight, out_bias, up_weight, up_bias, down_weight, down_bias, norm_gain, norm_shift, cotangent):
    total, width = tokens.shape
    count = lengths.shape[0]
    slots = total // count
    caps = count // 2
    pad = (slots + 15) // 16 * 16
    rws = caps * pad
    V = pl.BlockSpec(memory_space=pltpu.VMEM)
    A = pl.BlockSpec(memory_space=pl.ANY)
    S = pl.BlockSpec(memory_space=pltpu.SMEM)
    ins = [
        ("tok", tokens, A), ("cot", cotangent, A), ("lengths", lengths, S),
        ("wqkv_a", qkv_weight, A), ("wo_a", out_weight, A), ("wu_a", up_weight, A), ("wd_a", down_weight, A),
        ("qvb", qv_bias, V), ("ub", up_bias[None], V),
        ("ob", out_bias[None], V), ("db", down_bias[None], V), ("gains", norm_gain, V), ("shifts", norm_shift, V),
    ]
    outs = [
        ("y_out", (caps * slots, 512), BF16), ("dx_out", (caps * slots, 512), F32),
        ("f_out", (UNITS, 512, 256), BF16), ("s_out", (128, 128), F32),
    ]
    vm = pltpu.VMEM
    sems = UNITS + 1, 3 + 2 * depth
    scr = [
        ("tok_v", vm((total, 512), BF16)), ("cot_v", vm((total, 512), BF16)),
        ("stage", vm((total + 16, 512), F32)), ("xs", vm((rws, 512), BF16)), ("g", vm((rws, 512), BF16)),
        ("n1", vm((rws, 512), F32)), ("r1", vm((rws, 128), F32)), ("a1", vm((rws, 512), BF16)),
        ("w", vm((2 * UNITS, 512, 256), BF16)), ("qvb_b", vm((2, 256), BF16)), ("ub_b", vm((1, 1024), BF16)),
        ("bias_qkv", vm((6, 1, 256), F32)), ("bias_up", vm((8, 1, 256), F32)),
        ("pqkv", vm((6, rws, 256), BF16)), ("probs", vm((2 * caps, 4 * pad, pad), F32)), ("ctx", vm((2, rws, 256), BF16)),
        ("h1", vm((rws, 512), F32)), ("n2", vm((rws, 512), F32)), ("r2", vm((rws, 128), F32)), ("a2", vm((rws, 512), BF16)),
        ("hid", vm((8, rws, 256), BF16)), ("act", vm((8, rws, 256), F32)), ("du", vm((8, rws, 256), BF16)),
        ("e", vm((rws, 512), F32)), ("dh1", vm((rws, 512), F32)), ("dob", vm((rws, 512), BF16)), ("dctx", vm((2, rws, 256), BF16)),
        ("dqkv", vm((6, rws, 256), BF16)), ("yb", vm((caps * slots, 512), BF16)),
        ("small", vm((8, 512), F32)), ("small_up", vm((8, 1, 256), F32)), ("small_qkv", vm((6, 1, 256), F32)),
        ("grads", vm((UNITS, 2, 512, 256), BF16)), ("cr", vm((UNITS, 2, 256, 256), BF16)), ("yr", vm((UNITS, 256, 256), BF16)),
        ("xr", vm((UNITS, 128, 256), BF16)), ("zr", vm((UNITS, depth - 1, 128 // depth, 256), BF16)), ("f", vm((UNITS, 512, 256), BF16)),
        ("sg", vm((1, 2, 128, 128), F32)), ("scr", vm((1, 2, 64, 128), F32)), ("syr", vm((1, 64, 128), F32)),
        ("sxr", vm((1, 32, 128), F32)), ("szr", vm((1, depth - 1, 32 // depth, 128), F32)), ("sf", vm((1, 128, 128), F32)),
        ("lsem", pltpu.SemaphoreType.DMA((20,))), ("osem", pltpu.SemaphoreType.DMA((UNITS + 3,))), ("bsem", pltpu.SemaphoreType.DMA((4,))),
        ("wsend", pltpu.SemaphoreType.DMA((UNITS, 3))), ("wrecv", pltpu.SemaphoreType.DMA((UNITS, 3))),
        ("gsend", pltpu.SemaphoreType.DMA(sems)), ("grecv", pltpu.SemaphoreType.DMA(sems)),
    ]
    names = [n for n, _, _ in ins] + [n for n, _, _ in outs] + [n for n, _ in scr]
    y, dx, f, s = pl.pallas_call(
        functools.partial(kernel, caps, slots, pad, names),
        out_shape=[jax.ShapeDtypeStruct(s, d) for _, s, d in outs],
        in_specs=[s for _, _, s in ins],
        out_specs=[A] * len(outs),
        scratch_shapes=[s for _, s in scr],
        compiler_params=pltpu.CompilerParams(vmem_limit_bytes=61 << 20, collective_id=0, has_side_effects=True),
        name="layer",
    )(*[v for _, v, _ in ins])
    results = [
        (y.shape, BF16, A), (dx.shape, F32, A), (qkv_weight.shape, F32, A), (out_weight.shape, F32, A),
        (up_weight.shape, F32, A), (down_weight.shape, F32, A),
        (qv_bias.shape, F32, V), ((1, 512), F32, V), ((1, up_bias.shape[0]), F32, V), ((1, 512), F32, V), ((2, 512), F32, V), ((2, 512), F32, V),
    ]
    y, dx, qkv, out, up, down, qvb, ob, ub, db, gg, sh = pl.pallas_call(
        finish,
        out_shape=[jax.ShapeDtypeStruct(s, d) for s, d, _ in results],
        in_specs=[A, V, A, A],
        out_specs=[s for _, _, s in results],
        scratch_shapes=[
            vm((UNITS, 512, 256), BF16), vm((UNITS, 512, 256), F32),
            pltpu.SemaphoreType.DMA((UNITS,)), pltpu.SemaphoreType.DMA((2 * UNITS,)), pltpu.SemaphoreType.DMA((2,)),
        ],
        compiler_params=pltpu.CompilerParams(vmem_limit_bytes=24 << 20),
        name="finish",
    )(f, s, y, dx)
    return y, dx, qkv, qvb, out, ob[0], up, ub[0], down, db[0], gg, sh


def matmul_plain(left, right):
    return jnp.dot(left, right, preferred_element_type=jnp.float32)


def contract_rows(left, right):
    return lax.dot_general(
        left, right, (((0,), (0,)), ((), ())), preferred_element_type=jnp.float32
    )


def contract_cols(left, right):
    return lax.dot_general(
        left, right, (((1,), (1,)), ((), ())), preferred_element_type=jnp.float32
    )


def plain_norm_stats(values):
    center = values - jnp.mean(values, axis=-1, keepdims=True)
    inv_std = lax.rsqrt(jnp.mean(center * center, axis=-1, keepdims=True) + EPSILON)
    return (center * inv_std, inv_std)


def plain_norm_back(upstream, normed, inv_std, gain_vec):
    scaled = upstream * gain_vec
    inner_mean = jnp.mean(scaled * normed, axis=-1, keepdims=True)
    result = inv_std * (scaled - jnp.mean(scaled, axis=-1, keepdims=True) - normed * inner_mean)
    return (result, jnp.sum(upstream * normed, axis=0), jnp.sum(upstream, axis=0))


def row_slice(values, row_start, share_rows):
    return lax.dynamic_slice_in_dim(values, row_start, share_rows, 0)


def shards_by_heads(
    tokens,
    lengths,
    qkv_weight,
    qv_bias,
    out_weight,
    out_bias,
    up_weight,
    up_bias,
    down_weight,
    down_bias,
    norm_gain,
    norm_shift,
    cotangent,
):
    tensor_count = lax.axis_size("tensor")
    tensor_index = lax.axis_index("tensor")
    share_rows = tokens.shape[0] // tensor_count
    row_start = tensor_index * share_rows
    gains = norm_gain.astype(jnp.float32)
    shifts = norm_shift.astype(jnp.float32)
    total_rows = tokens.shape[0]
    count = lengths.shape[0]
    slots = total_rows // count
    local_width = qkv_weight.shape[2]
    local_heads = local_width // HD
    score_scale = HD ** (-0.5)
    qv_float = qv_bias.astype(jnp.float32)
    token_f = tokens.astype(jnp.float32)
    normed_one, inv_one = plain_norm_stats(token_f)
    first_in = (normed_one * gains[0] + shifts[0]).astype(jnp.bfloat16)
    queries = (matmul_plain(first_in, qkv_weight[0]) + qv_float[0]).astype(jnp.bfloat16)
    keys_all = matmul_plain(first_in, qkv_weight[1]).astype(jnp.bfloat16)
    values_all = (matmul_plain(first_in, qkv_weight[2]) + qv_float[1]).astype(jnp.bfloat16)
    shape4 = (count, slots, local_heads, HD)
    query_four = queries.reshape(shape4)
    key_four = keys_all.reshape(shape4)
    value_four = values_all.reshape(shape4)
    position = jnp.arange(slots)
    allowed = (position[None, :] <= position[:, None])[None, :, :] & (
        position[None, None, :] < lengths[:, None, None]
    )
    allowed = allowed[:, None, :, :]

    def masked_scores():
        raw = jnp.einsum(
            "cihd,cjhd->chij", query_four, key_four, preferred_element_type=jnp.float32
        )
        return jnp.where(allowed, raw * score_scale, -1e30)

    scores = masked_scores()
    row_max = jnp.max(scores, axis=-1, keepdims=True)
    log_total = row_max + jnp.log(jnp.sum(jnp.exp(scores - row_max), axis=-1, keepdims=True))
    probs_low = jnp.exp(scores - log_total).astype(jnp.bfloat16)
    context = jnp.einsum(
        "chij,cjhd->cihd", probs_low, value_four, preferred_element_type=jnp.float32
    )
    context = context.reshape(total_rows, local_width).astype(jnp.bfloat16)
    attn_part = matmul_plain(context, out_weight)
    attn_out = lax.psum(attn_part, "tensor") + out_bias.astype(jnp.float32)
    hidden_res = token_f + attn_out
    normed_two, inv_two = plain_norm_stats(hidden_res)
    second_in = (normed_two * gains[1] + shifts[1]).astype(jnp.bfloat16)
    upper = matmul_plain(second_in, up_weight) + up_bias.astype(jnp.float32)
    sigma = jax.nn.sigmoid(1.702 * upper)
    hidden = (upper * sigma).astype(jnp.bfloat16)
    mlp_part = matmul_plain(hidden, down_weight)
    result_rows = (
        hidden_res
        + lax.psum(mlp_part.astype(jnp.bfloat16), "tensor").astype(jnp.float32)
        + down_bias.astype(jnp.float32)
    )
    layer_out = row_slice(result_rows, row_start, share_rows).astype(jnp.bfloat16)
    grad_f = cotangent.astype(jnp.float32)
    down_grad = contract_rows(hidden, cotangent)
    down_bias_grad = jnp.sum(grad_f, axis=0)
    hidden_grad = contract_cols(cotangent, down_weight)
    upper_grad = (hidden_grad * (sigma + 1.702 * upper * sigma * (1.0 - sigma))).astype(
        jnp.bfloat16
    )
    up_grad = contract_rows(second_in, upper_grad)
    up_bias_grad = jnp.sum(upper_grad.astype(jnp.float32), axis=0)
    second_part = contract_cols(upper_grad, up_weight)
    second_grad = lax.psum(second_part, "tensor")
    residual_back, gain_two, shift_two = plain_norm_back(second_grad, normed_two, inv_two, gains[1])
    residual_full = grad_f + residual_back
    branch_grad = residual_full.astype(jnp.bfloat16)
    out_bias_grad = jnp.sum(branch_grad.astype(jnp.float32), axis=0)
    out_grad = contract_rows(context, branch_grad)
    context_grad = contract_cols(branch_grad, out_weight).astype(jnp.bfloat16).reshape(shape4)
    probs = jnp.exp(masked_scores() - log_total)
    probs_low = probs.astype(jnp.bfloat16)
    value_grad = jnp.einsum(
        "chij,cihd->cjhd", probs_low, context_grad, preferred_element_type=jnp.float32
    )
    prob_grad = jnp.einsum(
        "cihd,cjhd->chij", context_grad, value_four, preferred_element_type=jnp.float32
    )
    score_grad = probs * (prob_grad - jnp.sum(prob_grad * probs, axis=-1, keepdims=True))
    score_grad = score_grad.astype(jnp.bfloat16)
    query_grad = (
        jnp.einsum("chij,cjhd->cihd", score_grad, key_four, preferred_element_type=jnp.float32)
        * score_scale
    )
    key_grad = (
        jnp.einsum("chij,cihd->cjhd", score_grad, query_four, preferred_element_type=jnp.float32)
        * score_scale
    )
    query_grad = query_grad.reshape(total_rows, local_width).astype(jnp.bfloat16)
    key_grad = key_grad.reshape(total_rows, local_width).astype(jnp.bfloat16)
    value_grad = value_grad.reshape(total_rows, local_width).astype(jnp.bfloat16)
    qkv_grad = jnp.stack(
        [
            contract_rows(first_in, query_grad),
            contract_rows(first_in, key_grad),
            contract_rows(first_in, value_grad),
        ]
    )
    qv_bias_grad = jnp.stack(
        [
            jnp.sum(query_grad.astype(jnp.float32), axis=0),
            jnp.sum(value_grad.astype(jnp.float32), axis=0),
        ]
    )
    first_part = (
        contract_cols(query_grad, qkv_weight[0])
        + contract_cols(key_grad, qkv_weight[1])
        + contract_cols(value_grad, qkv_weight[2])
    )
    first_grad = lax.psum(first_part.astype(jnp.bfloat16), "tensor").astype(jnp.float32)
    input_back, gain_one, shift_one = plain_norm_back(first_grad, normed_one, inv_one, gains[0])
    input_grad = row_slice(residual_full + input_back, row_start, share_rows)
    gain_grads = jnp.stack([gain_one, gain_two])
    shift_grads = jnp.stack([shift_one, shift_two])
    summed = (
        lax.psum(qkv_grad.astype(jnp.bfloat16), "dp").astype(jnp.float32),
        lax.psum(qv_bias_grad.astype(jnp.bfloat16), "dp").astype(jnp.float32),
        lax.psum(out_grad.astype(jnp.bfloat16), "dp").astype(jnp.float32),
        lax.psum(out_bias_grad.astype(jnp.bfloat16), "dp").astype(jnp.float32),
        lax.psum(up_grad.astype(jnp.bfloat16), "dp").astype(jnp.float32),
        lax.psum(up_bias_grad.astype(jnp.bfloat16), "dp").astype(jnp.float32),
        lax.psum(down_grad.astype(jnp.bfloat16), "dp").astype(jnp.float32),
        lax.psum(down_bias_grad.astype(jnp.bfloat16), "dp").astype(jnp.float32),
        lax.psum(gain_grads.astype(jnp.bfloat16), "dp").astype(jnp.float32),
        lax.psum(shift_grads.astype(jnp.bfloat16), "dp").astype(jnp.float32),
    )
    return (
        layer_out,
        input_grad,
        summed[0],
        summed[1],
        summed[2],
        summed[3],
        summed[4],
        summed[5],
        summed[6],
        summed[7],
        summed[8],
        summed[9],
    )


def solution(mesh):
    dp, tensor = mesh.shape["dp"], mesh.shape["tensor"]
    if tensor == 2 and dp == 16:
        body = functools.partial(shards, dp // 4)
    else:
        body = shards_by_heads
    return jax.shard_map(
        body,
        mesh=mesh,
        in_specs=(P("dp", None), P("dp"), P(None, None, "tensor"), P(None, "tensor"), P("tensor", None), P(), P(None, "tensor"), P("tensor"), P("tensor", None), P(), P(), P(), P("dp", None)),
        out_specs=(P(("dp", "tensor"), None), P(("dp", "tensor"), None), P(None, None, "tensor"), P(None, "tensor"), P("tensor", None), P(), P(None, "tensor"), P("tensor"), P("tensor", None), P(), P(), P()),
        check_vma=False,
    )
```

```python
import functools

import jax
import jax.numpy as jnp
from jax import lax
from jax.experimental import pallas as pl
from jax.experimental.pallas import tpu as pltpu
from jax.sharding import PartitionSpec as P

HD = 64
EPSILON = 1e-05
F32 = jnp.float32
BF16 = jnp.bfloat16
LOG2E = 1.4426950408889634
UNITS = 12
EARLY = 9
LAG = 2
MESH = pl.DeviceIdType.MESH


def nn(left, right):
    return lax.dot_general(left, right, (((1,), (0,)), ((), ())), preferred_element_type=F32)


def nt(left, right):
    return lax.dot_general(left, right, (((1,), (1,)), ((), ())), preferred_element_type=F32)


def tn(left, right):
    return lax.dot_general(left, right, (((0,), (0,)), ((), ())), preferred_element_type=F32)


def loop(count, body):
    lax.fori_loop(0, count, lambda i, c: (body(i), c)[1], 0)


def norm(rows):
    center = rows - jnp.mean(rows, axis=-1, keepdims=True)
    inv = lax.rsqrt(jnp.mean(center * center, axis=-1, keepdims=True) + EPSILON)
    return center * inv, inv


def norm_back(grad, normed, inv, gain):
    t = grad * gain
    inner = jnp.mean(t * normed, axis=-1, keepdims=True)
    return inv * (t - jnp.mean(t, axis=-1, keepdims=True) - normed * inner)


def colsum(x):
    return jnp.sum(x, axis=0, keepdims=True)


class Layer:
    def __init__(self, caps, slots, pad, refs):
        self.caps, self.slots, self.pad = caps, slots, pad
        self.rows = caps * pad
        self.__dict__.update(refs)

    def head_mask(self, h, rows):
        lane = lax.broadcasted_iota(jnp.int32, (rows, 256), 1)
        return (lane >= h * HD) & (lane < (h + 1) * HD)

    def stack(self, block):
        parts = []
        for h in range(4):
            parts.append(jnp.where(self.head_mask(h, self.pad), block, jnp.zeros_like(block)))
        return jnp.concatenate(parts, axis=0)

    def unstack(self, block):
        out = None
        for h in range(4):
            part = block[h * self.pad : (h + 1) * self.pad]
            out = part if out is None else jnp.where(self.head_mask(h, self.pad), part, out)
        return out

    def widen(self, src, base, dst):
        total = src.shape[0]
        tile = self.slots * 2 if total % (self.slots * 2) == 0 else self.slots
        tile = 176 if total % 176 == 0 else total
        def conv(i):
            r = pl.ds(pl.multiple_of(i * tile, 16), tile)
            self.stage[r, :] = src[r, :].astype(F32)
        loop(total // tile, conv)
        self.stage[total : total + 16, :] = jnp.zeros((16, self.stage.shape[1]), F32)
        for c in range(self.caps):
            off = c * self.slots
            low = off // 8 * 8
            v = self.stage[pl.ds(pl.multiple_of(base + low, 8), self.pad + 8), :]
            v = v[off - low : off - low + self.pad]
            row = lax.broadcasted_iota(jnp.int32, v.shape, 0)
            v = jnp.where(row < self.slots, v, 0.0)
            dst[c * self.pad : (c + 1) * self.pad, :] = v.astype(BF16)

    def crows(self, c):
        return pl.ds(pl.multiple_of(c * self.pad, self.pad), self.pad)

    def norm_one(self):
        gain, shift = self.gains[0:1, :].astype(F32), self.shifts[0:1, :].astype(F32)
        def cap(c):
            r = self.crows(c)
            n, inv = norm(self.xs[r, :].astype(F32))
            self.n1[r, :] = n
            self.r1[r, :] = jnp.broadcast_to(inv, (self.pad, 128))
            self.a1[r, :] = (n * gain + shift).astype(BF16)
        loop(self.caps, cap)

    def biases(self, s, qvb, ub):
        for j in range(3):
            if j == 1:
                self.bias_qkv[s * 3 + j] = jnp.zeros((1, 256), F32)
            else:
                self.bias_qkv[s * 3 + j] = qvb[j // 2 : j // 2 + 1, :].astype(F32)
        up = ub[...].astype(F32).reshape(1, -1)
        for n in range(4):
            self.bias_up[s * 4 + n] = up[:, n * 256 : (n + 1) * 256]

    def qkv(self, i):
        s, j = i // 3, lax.rem(i, 3)
        out = nn(self.a1[...], self.w[s * UNITS + j]) + self.bias_qkv[i]
        self.pqkv[i] = out.astype(BF16)

    def attention(self, i):
        s, c = i // self.caps, lax.rem(i, self.caps)
        r = self.crows(c)
        q = self.pqkv[s * 3, r, :]
        km = self.stack(self.pqkv[s * 3 + 1, r, :])
        vm = self.stack(self.pqkv[s * 3 + 2, r, :])
        st = nt(km, q)
        length = self.lengths[self.cap_base + c]
        jj = lax.broadcasted_iota(jnp.int32, (self.pad, self.pad), 0)
        ii = lax.broadcasted_iota(jnp.int32, (self.pad, self.pad), 1)
        allowed = (jj <= ii) & (jj < length)
        blocks = []
        for h in range(4):
            blk = jnp.where(allowed, st[h * self.pad : (h + 1) * self.pad], -1e30)
            top = jnp.max(blk, axis=0, keepdims=True)
            e = jnp.exp2((blk - top) * (HD**-0.5 * LOG2E))
            blocks.append(e * (1.0 / jnp.sum(e, axis=0, keepdims=True)))
        p = jnp.concatenate(blocks, axis=0)
        self.probs[i] = p
        self.ctx[s, r, :] = tn(p.astype(BF16), vm).astype(BF16)

    def attention_back(self, i):
        s, c = i // self.caps, lax.rem(i, self.caps)
        r = self.crows(c)
        q = self.pqkv[s * 3, r, :]
        k = self.pqkv[s * 3 + 1, r, :]
        v = self.pqkv[s * 3 + 2, r, :]
        d = self.dctx[s, r, :]
        p = self.probs[i]
        self.dqkv[s * 3 + 2, r, :] = self.unstack(nn(p.astype(BF16), d)).astype(BF16)
        dp = nt(self.stack(v), d)
        blocks = []
        for h in range(4):
            rr = slice(h * self.pad, (h + 1) * self.pad)
            blocks.append(p[rr] * (dp[rr] - jnp.sum(dp[rr] * p[rr], axis=0, keepdims=True)))
        ds = jnp.concatenate(blocks, axis=0).astype(BF16)
        self.dqkv[s * 3 + 1, r, :] = (self.unstack(nn(ds, q)) * HD**-0.5).astype(BF16)
        self.dqkv[s * 3, r, :] = (tn(ds, self.stack(k)) * HD**-0.5).astype(BF16)

    def project(self, i):
        tile = self.rows // 4
        r = pl.ds(pl.multiple_of(i * tile, 16), tile)
        gain, shift = self.gains[1:2, :].astype(F32), self.shifts[1:2, :].astype(F32)
        c0, c1 = self.ctx[0, r, :], self.ctx[1, r, :]
        halves = []
        for n in range(2):
            w = slice(n * 256, (n + 1) * 256)
            halves.append(nn(c0, self.w[3, w, :]) + nn(c1, self.w[UNITS + 3, w, :]))
        o = jnp.concatenate(halves, axis=1)
        h1 = self.xs[r, :].astype(F32) + o + self.ob[...].astype(F32).reshape(1, -1)
        self.h1[r, :] = h1
        n, inv = norm(h1)
        self.n2[r, :] = n
        self.r2[r, :] = jnp.broadcast_to(inv, (tile, 128))
        self.a2[r, :] = (n * gain + shift).astype(BF16)

    def wup(self, m):
        return (m // 4) * UNITS + 4 + lax.rem(m, 4)

    def wdown(self, m):
        return (m // 4) * UNITS + 8 + lax.rem(m, 4)

    def up(self, m):
        u = nn(self.a2[...], self.w[self.wup(m)]) + self.bias_up[m]
        sg = 0.5 * jnp.tanh(0.851 * u) + 0.5
        h = u * sg
        self.hid[m] = h.astype(BF16)
        self.act[m] = sg + 1.702 * h * (1.0 - sg)

    def down_grad(self, m):
        w = tn(self.hid[m], self.g[...]).astype(BF16)
        s, n = m // 4, lax.rem(m, 4)
        self.grads[n, s, 0:256, :] = w[:, :256]
        self.grads[n, s, 256:512, :] = w[:, 256:]

    def hidden_back(self, m):
        w = self.wdown(m)
        back = nt(self.g[:, 0:256], self.w[w, 0:256, :]) + nt(self.g[:, 256:512], self.w[w, 256:512, :])
        du = (back * self.act[m]).astype(BF16)
        self.du[m] = du
        self.small_up[m] = colsum(du.astype(F32))

    def up_grad(self, m):
        s, n = m // 4, lax.rem(m, 4)
        self.grads[4 + n, s] = tn(self.a2[...], self.du[m]).astype(BF16)

    def half_tile(self, i):
        tile = self.rows // 2
        r = pl.ds(pl.multiple_of((i // 2) * tile, 16), tile)
        return r, lax.rem(i, 2)

    def second_grad(self, i):
        r, n = self.half_tile(i)
        w = pl.ds(pl.multiple_of(n * 256, 256), 256)
        acc = None
        for m in range(8):
            part = nt(self.du[m, r, :], self.w[(m // 4) * UNITS + 4 + m % 4, w, :])
            acc = part if acc is None else acc + part
        self.e[r, w] = acc

    def mlp_out(self, i):
        r, n = self.half_tile(i)
        w = pl.ds(pl.multiple_of(n * 256, 256), 256)
        acc = self.h1[r, w] + self.db[w].astype(F32).reshape(1, -1)
        for m in range(8):
            acc = acc + nn(self.hid[m, r, :], self.w[(m // 4) * UNITS + 8 + m % 4, w, :])
        self.h1[r, w] = acc

    def norm_two_back(self):
        gain = self.gains[1:2, :].astype(F32)
        zero = jnp.zeros((1, gain.shape[1]), F32)
        def cap(c, carry):
            gg, sg, ob, db = carry
            r = self.crows(c)
            e, n, g = self.e[r, :], self.n2[r, :], self.g[r, :].astype(F32)
            dh = g + norm_back(e, n, self.r2[r, 0:1], gain)
            self.dh1[r, :] = dh
            dob = dh.astype(BF16)
            self.dob[r, :] = dob
            return (gg + colsum(e * n), sg + colsum(e), ob + colsum(dob.astype(F32)), db + colsum(g))
        gg, sg, ob, db = lax.fori_loop(0, self.caps, cap, (zero, zero, zero, zero))
        self.small[1:2, :], self.small[3:4, :], self.small[4:5, :], self.small[5:6, :] = gg, sg, ob, db

    def out_back(self, s):
        w = tn(self.ctx[s], self.dob[...]).astype(BF16)
        self.grads[8, s, 0:256, :] = w[:, :256]
        self.grads[8, s, 256:512, :] = w[:, 256:]
        wo = s * UNITS + 3
        back = nt(self.dob[:, 0:256], self.w[wo, 0:256, :]) + nt(self.dob[:, 256:512], self.w[wo, 256:512, :])
        self.dctx[s] = back.astype(BF16)

    def qkv_grad(self, i):
        s, j = i // 3, lax.rem(i, 3)
        d = self.dqkv[i]
        self.grads[9 + j, s] = tn(self.a1[...], d).astype(BF16)
        self.small_qkv[i] = colsum(d.astype(F32))

    def first_grad(self, i):
        r, n = self.half_tile(i)
        w = pl.ds(pl.multiple_of(n * 256, 256), 256)
        acc = None
        for m in range(6):
            part = nt(self.dqkv[m, r, :], self.w[(m // 3) * UNITS + m % 3, w, :])
            acc = part if acc is None else acc + part
        self.e[r, w] = acc

    def norm_one_back(self, out, base):
        gain = self.gains[0:1, :].astype(F32)
        zero = jnp.zeros((1, gain.shape[1]), F32)
        gg, sg = zero, zero
        for c in range(self.caps):
            r = slice(c * self.pad, (c + 1) * self.pad)
            e, n = self.e[r, :], self.n1[r, :]
            dx = self.dh1[r, :] + norm_back(e, n, self.r1[r, 0:1], gain)
            out[base + c * self.slots : base + (c + 1) * self.slots, :] = dx[: self.slots]
            gg, sg = gg + colsum(e * n), sg + colsum(e)
        self.small[0:1, :], self.small[2:3, :] = gg, sg

    def layer_out(self, flat, out):
        for c in range(self.caps):
            flat[c * self.slots : (c + 1) * self.slots, :] = self.h1[c * self.pad : c * self.pad + self.slots, :]
        out[...] = flat[0 : self.caps * self.slots, :].astype(BF16)

    def pack_small(self, out):
        def put(slot, row, value):
            for i in range(value.shape[1] // 128):
                out[slot, row + i : row + i + 1, :] = value[:, i * 128 : (i + 1) * 128]
        for slot in range(2):
            out[slot] = jnp.zeros(out.shape[1:], F32)
            put(slot, 0, self.small_qkv[slot * 3])
            put(slot, 2, self.small_qkv[slot * 3 + 2])
            for n in range(4):
                put(slot, 4 + 2 * n, self.small_up[slot * 4 + n])
            for i, k in enumerate((4, 5, 0, 1, 2, 3)):
                put(slot, 12 + 4 * i, self.small[k : k + 1, :])


class Peers:
    def __init__(self):
        dp, t = lax.axis_index("dp"), lax.axis_index("tensor")
        depth = lax.axis_size("dp") // 4
        self.core = lax.rem(dp, 2)
        self.x = lax.rem(dp // 2, 2)
        self.z = dp // 4
        self.t = t
        self.to_y = (dp, 1 - t)
        self.to_x = (dp + 2 - 4 * self.x, t)
        self.to_core = (dp + 1 - 2 * self.core, t)
        self.depth = depth
        self.to_z = [(lax.rem(self.z + k, depth) * 4 + lax.rem(dp, 4), t) for k in range(1, depth)]
        self.z_of = [lax.rem(self.z + k, depth) for k in range(1, depth)]

    def all(self):
        return [self.to_y, self.to_x, self.to_core] + self.to_z

    def greet(self):
        barrier = pltpu.get_barrier_semaphore()
        for peer in self.all():
            pl.semaphore_signal(barrier, inc=1, device_id=peer, device_id_type=MESH)

    def meet(self):
        pl.semaphore_wait(pltpu.get_barrier_semaphore(), len(self.all()))


def rows(index, size):
    return pl.ds(pl.multiple_of(index * size, size), size)


def remote(src, dst, send, recv, peer):
    return pltpu.make_async_remote_copy(src_ref=src, dst_ref=dst, send_sem=send, recv_sem=recv, device_id=peer, device_id_type=MESH)


class Weights:
    def __init__(self, peers, w, send, recv):
        self.p, self.w, self.send, self.recv = peers, w, send, recv
        self.quarter = peers.core * 2 + peers.x
        self.size = w.shape[1] // 4

    def y(self, u):
        r = rows(self.quarter, self.size)
        return remote(self.w.at[u, r], self.w.at[UNITS + u, r], self.send.at[u, 0], self.recv.at[u, 0], self.p.to_y)

    def x(self, u):
        part = self.w.at[UNITS + u, rows(self.quarter, self.size)]
        return remote(part, part, self.send.at[u, 1], self.recv.at[u, 1], self.p.to_x)

    def c(self, u):
        part = self.w.at[UNITS + u, rows(self.p.core, self.size * 2)]
        return remote(part, part, self.send.at[u, 2], self.recv.at[u, 2], self.p.to_core)

    def relay_x(self, u):
        self.y(u).wait_recv()
        self.x(u).start()

    def relay_c(self, u):
        self.x(u).wait_recv()
        self.c(u).start()

    def tick(self, u):
        if u < UNITS:
            self.relay_x(u)
        if 2 <= u < UNITS + 2:
            self.relay_c(u - 2)

    def ready(self, u):
        self.c(u).wait_recv()

    def drain(self, u):
        self.y(u).wait_send()
        self.x(u).wait_send()
        self.c(u).wait_send()


class Reduce:
    def __init__(self, peers, refs, sem0, send, recv, across=None):
        self.p = peers
        self.g, self.cr, self.yr, self.xr, self.zr, self.f = refs
        self.x2r, self.y2r = across or (None, None)
        self.sem0, self.send, self.recv = sem0, send, recv
        self.count = self.g.shape[0]
        self.full = self.g.shape[2]
        self.half, self.quarter = self.full // 2, self.full // 4
        self.shard = self.quarter // peers.depth

    def sems(self, n, k):
        return self.send.at[self.sem0 + n, k], self.recv.at[self.sem0 + n, k]

    def c(self, n):
        return remote(self.g.at[n, :, rows(1 - self.p.core, self.half)], self.cr.at[n], *self.sems(n, 0), self.p.to_core)

    def y(self, n):
        return remote(self.cr.at[n, 1], self.yr.at[n], *self.sems(n, 1), self.p.to_y)

    def x(self, n):
        return remote(self.cr.at[n, 0, rows(1 - self.p.x, self.quarter)], self.xr.at[n], *self.sems(n, 2), self.p.to_x)

    def x2(self, n):
        return remote(
            self.cr.at[n, :, rows(1 - self.p.x, self.quarter)], self.x2r.at[n - EARLY], *self.sems(n, 2), self.p.to_x
        )

    def y2(self, n):
        return remote(self.cr.at[n, 1, rows(self.p.x, self.quarter)], self.y2r.at[n - EARLY], *self.sems(n, 1), self.p.to_y)

    def z(self, n):
        return [
            remote(
                self.cr.at[n, 0, pl.ds(pl.multiple_of(self.p.x * self.quarter + self.p.z_of[k] * self.shard, self.shard), self.shard)],
                self.zr.at[n, k],
                *self.sems(n, 5 + k),
                self.p.to_z[k],
            )
            for k in range(self.p.depth - 1)
        ]

    def own_shard(self):
        p = self.p
        return pl.ds(pl.multiple_of(p.core * self.half + p.x * self.quarter + p.z * self.shard, self.shard), self.shard)

    def za(self, n):
        part = self.f.at[n, self.own_shard()]
        return [
            remote(part, part, *self.sems(n, 4 + self.p.depth + k), self.p.to_z[k]) for k in range(self.p.depth - 1)
        ]

    def xa(self, n):
        part = self.f.at[n, pl.ds(pl.multiple_of(self.p.core * self.half + self.p.x * self.quarter, self.quarter), self.quarter)]
        return remote(part, part, *self.sems(n, 3), self.p.to_x)

    def ca(self, n):
        part = self.f.at[n, rows(self.p.core, self.half)]
        return remote(part, part, *self.sems(n, 4), self.p.to_core)

    def c_start(self, n):
        self.c(n).start()

    def c_add(self, n):
        self.c(n).wait_recv()
        self.cr[n] = self.cr[n] + self.g[n, :, rows(self.p.core, self.half), :]

    def c_done(self, n):
        self.c_add(n)
        self.y(n).start()

    def c_done_x(self, n):
        self.c_add(n)
        self.x2(n).start()

    def x2_done(self, n):
        self.x2(n).wait_recv()
        r = rows(self.p.x, self.quarter)
        self.cr[n, :, r, :] = self.cr[n, :, r, :] + self.x2r[n - EARLY]
        self.y2(n).start()

    def y2_done(self, n):
        self.y2(n).wait_recv()
        r = rows(self.p.x, self.quarter)
        self.cr[n, 0, r, :] = self.cr[n, 0, r, :] + self.y2r[n - EARLY]
        for copy in self.z(n):
            copy.start()

    def y_done(self, n):
        self.y(n).wait_recv()
        self.cr[n, 0] = self.cr[n, 0] + self.yr[n]
        self.x(n).start()

    def x_done(self, n):
        self.x(n).wait_recv()
        r = rows(self.p.x, self.quarter)
        self.cr[n, 0, r, :] = self.cr[n, 0, r, :] + self.xr[n]
        for copy in self.z(n):
            copy.start()

    def z_done(self, n):
        for copy in self.z(n):
            copy.wait_recv()
        mine = pl.ds(pl.multiple_of(self.p.x * self.quarter + self.p.z * self.shard, self.shard), self.shard)
        total = self.cr[n, 0, mine, :].astype(F32)
        for k in range(self.p.depth - 1):
            total = total + self.zr[n, k].astype(F32)
        self.f[n, self.own_shard(), :] = total.astype(self.f.dtype)
        for copy in self.za(n):
            copy.start()

    def za_done(self, n):
        for copy in self.za(n):
            copy.wait_recv()
        self.xa(n).start()

    def xa_done(self, n):
        self.xa(n).wait_recv()
        self.ca(n).start()

    def ca_done(self, n):
        self.ca(n).wait_recv()

    def drain(self, n, late=False):
        cross = [self.x2(n), self.y2(n)] if late else [self.x(n), self.y(n)]
        for copy in cross + [self.c(n), self.xa(n), self.ca(n)] + self.z(n) + self.za(n):
            copy.wait_send()


STAGES = ("y_done", "x_done", "z_done", "za_done", "xa_done", "ca_done")
STAGES_X = ("x2_done", "y2_done", "z_done", "za_done", "xa_done", "ca_done")


def when(condition, body):
    if isinstance(condition, bool):
        if condition:
            body()
    else:
        pl.when(condition)(body)


def both(a, b):
    return a and b if isinstance(a, bool) and isinstance(b, bool) else a & b


def step(big, outs, tick):
    for lag, name in enumerate(STAGES):
        unit = tick - LAG * lag

        def run(unit=unit, name=name):
            getattr(big, name)(unit)
            if name == "ca_done":
                outs(unit).start()

        when(both(unit >= 0, unit < EARLY), run)


def step_x(big, small, outs, tick):
    for lag, name in enumerate(STAGES_X):
        unit = tick - LAG * lag + EARLY

        def run(unit=unit, name=name):
            getattr(big, name)(unit)
            if name == "ca_done":
                outs(unit).start()

        when(both(unit >= EARLY, unit < UNITS), run)
        when(unit == UNITS, lambda lag=lag: getattr(small, STAGES[lag])(0))


def kernel(caps, slots, pad, names_in, *all_refs):
    L = Layer(caps, slots, pad, dict(zip(names_in, all_refs)))
    peers = Peers()
    peers.greet()
    L.cap_base = peers.t * caps
    weights = Weights(peers, L.w, L.wsend, L.wrecv)
    big = Reduce(peers, (L.grads, L.cr, L.yr, L.xr, L.zr, L.f), 0, L.gsend, L.grecv, (L.x2r, L.y2r))
    small = Reduce(peers, (L.sg, L.scr, L.syr, L.sxr, L.szr, L.sf), UNITS, L.gsend, L.grecv)

    local = []

    def load(a, b):
        copy = pltpu.make_async_copy(a, b, L.lsem.at[len(local)])
        copy.start()
        local.append(copy)

    load(L.tok, L.tok_v)
    for j in range(3):
        load(L.wqkv_a.at[j], L.w.at[j])
    for n in range(2):
        load(L.wo_a.at[:, pl.ds(n * 256, 256)], L.w.at[3, pl.ds(n * 256, 256)])
    for n in range(4):
        load(L.wu_a.at[:, pl.ds(n * 256, 256)], L.w.at[4 + n])
    for n in range(4):
        for k in range(2):
            load(L.wd_a.at[pl.ds(n * 256, 256), pl.ds(k * 256, 256)], L.w.at[8 + n, pl.ds(k * 256, 256)])
    load(L.cot, L.cot_v)
    local[0].wait()
    L.widen(L.tok_v, peers.t * caps * slots, L.xs)
    for copy in local[1:]:
        copy.wait()
    peers.meet()
    bias_send = [
        remote(L.qvb, L.qvb_b, L.bsem.at[0], L.bsem.at[1], peers.to_y),
        remote(L.ub, L.ub_b, L.bsem.at[2], L.bsem.at[3], peers.to_y),
    ]
    for copy in bias_send:
        copy.start()
    loop(UNITS, lambda u: weights.y(u).start())
    L.norm_one()
    L.biases(0, L.qvb, L.ub)
    loop(3, L.qkv)
    attend = lambda i: [L.attention(4 * i + k) for k in range(4)]
    loop(caps // 4, attend)
    L.widen(L.cot_v, peers.t * caps * slots, L.g)
    for copy in bias_send:
        copy.wait()
    L.biases(1, L.qvb_b, L.ub_b)
    for u in range(3):
        weights.tick(u)
    for j in range(3):
        weights.ready(j)
        L.qkv(3 + j)
        weights.tick(3 + j)
    attend(caps // 4)
    weights.tick(6)
    attend(caps // 4 + 1)
    weights.tick(7)
    weights.ready(3)
    loop(4, L.project)
    weights.tick(8)

    for n in range(4):
        L.up(n)
        weights.ready(4 + n)
        L.up(4 + n)
        L.down_grad(n)
        L.down_grad(4 + n)
        big.c_start(n)
        if n > 0:
            big.c_done(n - 1)
        weights.tick(9 + n)
    loop(4, L.hidden_back)
    big.c_done(3)
    weights.tick(13)
    loop(4, lambda i: (weights.ready(8 + i), L.hidden_back(4 + i)))

    outs = lambda n: pltpu.make_async_copy(L.f.at[n], L.f_out.at[n], L.osem.at[n])
    tick = functools.partial(step, big, outs)
    tick(0)

    def ups(i):
        L.up_grad(i)
        L.up_grad(4 + i)
        big.c_start(4 + i)

        @pl.when(i > 0)
        def _():
            big.c_done(3 + i)

    loop(4, ups)
    tick(1)
    loop(4, L.second_grad)
    big.c_done(7)
    L.norm_two_back()
    tick(2)
    loop(2, L.out_back)
    big.c_start(8)

    def attend_back(i):
        for k in range(4):
            L.attention_back(4 * i + k)
        when(i == 0, lambda: big.c_done(8))
        when(lax.rem(i, 2) == 1, lambda: tick(3 + i // 2))

    loop(caps // 2, attend_back)

    def qkvs(i):
        L.qkv_grad(i)
        L.qkv_grad(3 + i)
        big.c_start(9 + i)
        when(i > 0, lambda: big.c_done_x(8 + i))

    loop(3, qkvs)
    loop(4, L.first_grad)
    big.c_done_x(11)
    tick(5)
    size = caps * slots
    base = (size + 7) // 8 * 8
    L.norm_one_back(L.stage, base)
    dx_copy = pltpu.make_async_copy(L.stage.at[pl.ds(base, size)], L.dx_out, L.osem.at[UNITS])
    dx_copy.start()
    L.pack_small(L.sg.at[0])
    small.c_start(0)
    loop(4, L.mlp_out)
    tick(6)
    L.layer_out(L.stage, L.yb)
    y_copy = pltpu.make_async_copy(L.yb, L.y_out, L.osem.at[UNITS + 1])
    y_copy.start()
    small.c_done(0)
    late = UNITS - EARLY

    def last(i):
        step(big, outs, 7 + i)
        step_x(big, small, outs, i)

    loop(max(EARLY + LAG * (len(STAGES) - 1) - 7, late + 1 + LAG * (len(STAGES) - 1)), last)
    s_copy = pltpu.make_async_copy(L.sf.at[0], L.s_out, L.osem.at[UNITS + 2])
    s_copy.start()

    def drain(n):
        weights.drain(n)
        outs(n).wait()

    loop(UNITS, drain)
    loop(EARLY, big.drain)
    loop(late, lambda i: big.drain(EARLY + i, late=True))
    small.drain(0)
    dx_copy.wait()
    y_copy.wait()
    s_copy.wait()


def finish(f, s, y, dx, y_out, dx_out, qkv, out, up, down, qvb, ob, ub, db, gg, sh, f_v, y_v, dx_v, wide, sem_in, sem_out, sem_io):
    ins = [pltpu.make_async_copy(f.at[n], f_v.at[n], sem_in.at[n]) for n in range(UNITS)]
    for copy in ins:
        copy.start()
    rows_in = [pltpu.make_async_copy(y, y_v, sem_io.at[0]), pltpu.make_async_copy(dx, dx_v, sem_io.at[1])]
    for copy in rows_in:
        copy.start()
    io = []
    for n in range(UNITS):
        ins[n].wait()
        wide[n] = f_v[n].astype(F32)
        if n < 4 or n == 8:
            parts = []
            for k in range(2):
                c = pl.ds(k * 256, 256)
                dst = down.at[pl.ds(n * 256, 256), c] if n < 4 else out.at[:, c]
                parts.append((wide.at[n, c], dst))
        elif n < 8:
            parts = [(wide.at[n], up.at[:, pl.ds((n - 4) * 256, 256)])]
        else:
            parts = [(wide.at[n], qkv.at[n - 9])]
        for k, (a, b) in enumerate(parts):
            copy = pltpu.make_async_copy(a, b, sem_out.at[2 * n + k])
            copy.start()
            io.append(copy)
        if n == 3:
            for copy in rows_in:
                copy.wait()
            for k, (a, b) in enumerate(((y_v, y_out), (dx_v, dx_out))):
                copy = pltpu.make_async_copy(a, b, sem_io.at[2 + k])
                copy.start()
                io.append(copy)

    def row(first, count):
        return jnp.concatenate([s[first + i : first + i + 1, :] for i in range(count)], axis=1)

    qvb[0:1, :], qvb[1:2, :] = row(0, 2), row(2, 2)
    ub[...] = row(4, 8)
    ob[...], db[...] = row(12, 4), row(16, 4)
    gg[0:1, :], gg[1:2, :] = row(20, 4), row(24, 4)
    sh[0:1, :], sh[1:2, :] = row(28, 4), row(32, 4)
    for copy in io:
        copy.wait()


def shards(depth, tokens, lengths, qkv_weight, qv_bias, out_weight, out_bias, up_weight, up_bias, down_weight, down_bias, norm_gain, norm_shift, cotangent):
    total, width = tokens.shape
    count = lengths.shape[0]
    slots = total // count
    caps = count // 2
    pad = (slots + 15) // 16 * 16
    rws = caps * pad
    V = pl.BlockSpec(memory_space=pltpu.VMEM)
    A = pl.BlockSpec(memory_space=pl.ANY)
    S = pl.BlockSpec(memory_space=pltpu.SMEM)
    ins = [
        ("tok", tokens, A), ("cot", cotangent, A), ("lengths", lengths, S),
        ("wqkv_a", qkv_weight, A), ("wo_a", out_weight, A), ("wu_a", up_weight, A), ("wd_a", down_weight, A),
        ("qvb", qv_bias, V), ("ub", up_bias, V),
        ("ob", out_bias, V), ("db", down_bias, V), ("gains", norm_gain, V), ("shifts", norm_shift, V),
    ]
    outs = [
        ("y_out", (caps * slots, 512), BF16), ("dx_out", (caps * slots, 512), F32),
        ("f_out", (UNITS, 512, 256), BF16), ("s_out", (128, 128), F32),
    ]
    vm = pltpu.VMEM
    sems = UNITS + 1, 3 + 2 * depth
    scr = [
        ("tok_v", vm((total, 512), BF16)), ("cot_v", vm((total, 512), BF16)),
        ("stage", vm((total + 16, 512), F32)), ("xs", vm((rws, 512), BF16)), ("g", vm((rws, 512), BF16)),
        ("n1", vm((rws, 512), F32)), ("r1", vm((rws, 128), F32)), ("a1", vm((rws, 512), BF16)),
        ("w", vm((2 * UNITS, 512, 256), BF16)), ("qvb_b", vm((2, 256), BF16)), ("ub_b", vm(up_bias.shape, BF16)),
        ("bias_qkv", vm((6, 1, 256), F32)), ("bias_up", vm((8, 1, 256), F32)),
        ("pqkv", vm((6, rws, 256), BF16)), ("probs", vm((2 * caps, 4 * pad, pad), F32)), ("ctx", vm((2, rws, 256), BF16)),
        ("h1", vm((rws, 512), F32)), ("n2", vm((rws, 512), F32)), ("r2", vm((rws, 128), F32)), ("a2", vm((rws, 512), BF16)),
        ("hid", vm((8, rws, 256), BF16)), ("act", vm((8, rws, 256), F32)), ("du", vm((8, rws, 256), BF16)),
        ("e", vm((rws, 512), F32)), ("dh1", vm((rws, 512), F32)), ("dob", vm((rws, 512), BF16)), ("dctx", vm((2, rws, 256), BF16)),
        ("dqkv", vm((6, rws, 256), BF16)), ("yb", vm((caps * slots, 512), BF16)),
        ("small", vm((8, 512), F32)), ("small_up", vm((8, 1, 256), F32)), ("small_qkv", vm((6, 1, 256), F32)),
        ("grads", vm((UNITS, 2, 512, 256), BF16)), ("cr", vm((UNITS, 2, 256, 256), BF16)), ("yr", vm((UNITS, 256, 256), BF16)),
        ("xr", vm((UNITS, 128, 256), BF16)), ("zr", vm((UNITS, depth - 1, 128 // depth, 256), BF16)), ("f", vm((UNITS, 512, 256), BF16)),
        ("x2r", vm((UNITS - EARLY, 2, 128, 256), BF16)), ("y2r", vm((UNITS - EARLY, 128, 256), BF16)),
        ("sg", vm((1, 2, 128, 128), F32)), ("scr", vm((1, 2, 64, 128), F32)), ("syr", vm((1, 64, 128), F32)),
        ("sxr", vm((1, 32, 128), F32)), ("szr", vm((1, depth - 1, 32 // depth, 128), F32)), ("sf", vm((1, 128, 128), F32)),
        ("lsem", pltpu.SemaphoreType.DMA((20,))), ("osem", pltpu.SemaphoreType.DMA((UNITS + 3,))), ("bsem", pltpu.SemaphoreType.DMA((4,))),
        ("wsend", pltpu.SemaphoreType.DMA((UNITS, 3))), ("wrecv", pltpu.SemaphoreType.DMA((UNITS, 3))),
        ("gsend", pltpu.SemaphoreType.DMA(sems)), ("grecv", pltpu.SemaphoreType.DMA(sems)),
    ]
    names = [n for n, _, _ in ins] + [n for n, _, _ in outs] + [n for n, _ in scr]
    y, dx, f, s = pl.pallas_call(
        functools.partial(kernel, caps, slots, pad, names),
        out_shape=[jax.ShapeDtypeStruct(s, d) for _, s, d in outs],
        in_specs=[s for _, _, s in ins],
        out_specs=[A] * len(outs),
        scratch_shapes=[s for _, s in scr],
        compiler_params=pltpu.CompilerParams(vmem_limit_bytes=61 << 20, collective_id=0, has_side_effects=True),
        name="layer",
    )(*[v for _, v, _ in ins])
    results = [
        (y.shape, BF16, A), (dx.shape, F32, A), (qkv_weight.shape, F32, A), (out_weight.shape, F32, A),
        (up_weight.shape, F32, A), (down_weight.shape, F32, A),
        (qv_bias.shape, F32, V), ((1, 512), F32, V), ((1, up_bias.shape[0]), F32, V), ((1, 512), F32, V), ((2, 512), F32, V), ((2, 512), F32, V),
    ]
    y, dx, qkv, out, up, down, qvb, ob, ub, db, gg, sh = pl.pallas_call(
        finish,
        out_shape=[jax.ShapeDtypeStruct(s, d) for s, d, _ in results],
        in_specs=[A, V, A, A],
        out_specs=[s for _, _, s in results],
        scratch_shapes=[
            vm((UNITS, 512, 256), BF16), vm(y.shape, BF16), vm(dx.shape, F32), vm((UNITS, 512, 256), F32),
            pltpu.SemaphoreType.DMA((UNITS,)), pltpu.SemaphoreType.DMA((2 * UNITS,)), pltpu.SemaphoreType.DMA((4,)),
        ],
        compiler_params=pltpu.CompilerParams(vmem_limit_bytes=61 << 20),
        name="finish",
    )(f, s, y, dx)
    return y, dx, qkv, qvb, out, ob[0], up, ub[0], down, db[0], gg, sh


def matmul_plain(left, right):
    return jnp.dot(left, right, preferred_element_type=jnp.float32)


def contract_rows(left, right):
    return lax.dot_general(
        left, right, (((0,), (0,)), ((), ())), preferred_element_type=jnp.float32
    )


def contract_cols(left, right):
    return lax.dot_general(
        left, right, (((1,), (1,)), ((), ())), preferred_element_type=jnp.float32
    )


def plain_norm_stats(values):
    center = values - jnp.mean(values, axis=-1, keepdims=True)
    inv_std = lax.rsqrt(jnp.mean(center * center, axis=-1, keepdims=True) + EPSILON)
    return (center * inv_std, inv_std)


def plain_norm_back(upstream, normed, inv_std, gain_vec):
    scaled = upstream * gain_vec
    inner_mean = jnp.mean(scaled * normed, axis=-1, keepdims=True)
    result = inv_std * (scaled - jnp.mean(scaled, axis=-1, keepdims=True) - normed * inner_mean)
    return (result, jnp.sum(upstream * normed, axis=0), jnp.sum(upstream, axis=0))


def row_slice(values, row_start, share_rows):
    return lax.dynamic_slice_in_dim(values, row_start, share_rows, 0)


def shards_by_heads(
    tokens,
    lengths,
    qkv_weight,
    qv_bias,
    out_weight,
    out_bias,
    up_weight,
    up_bias,
    down_weight,
    down_bias,
    norm_gain,
    norm_shift,
    cotangent,
):
    tensor_count = lax.axis_size("tensor")
    tensor_index = lax.axis_index("tensor")
    share_rows = tokens.shape[0] // tensor_count
    row_start = tensor_index * share_rows
    gains = norm_gain.astype(jnp.float32)
    shifts = norm_shift.astype(jnp.float32)
    total_rows = tokens.shape[0]
    count = lengths.shape[0]
    slots = total_rows // count
    local_width = qkv_weight.shape[2]
    local_heads = local_width // HD
    score_scale = HD ** (-0.5)
    qv_float = qv_bias.astype(jnp.float32)
    token_f = tokens.astype(jnp.float32)
    normed_one, inv_one = plain_norm_stats(token_f)
    first_in = (normed_one * gains[0] + shifts[0]).astype(jnp.bfloat16)
    queries = (matmul_plain(first_in, qkv_weight[0]) + qv_float[0]).astype(jnp.bfloat16)
    keys_all = matmul_plain(first_in, qkv_weight[1]).astype(jnp.bfloat16)
    values_all = (matmul_plain(first_in, qkv_weight[2]) + qv_float[1]).astype(jnp.bfloat16)
    shape4 = (count, slots, local_heads, HD)
    query_four = queries.reshape(shape4)
    key_four = keys_all.reshape(shape4)
    value_four = values_all.reshape(shape4)
    position = jnp.arange(slots)
    allowed = (position[None, :] <= position[:, None])[None, :, :] & (
        position[None, None, :] < lengths[:, None, None]
    )
    allowed = allowed[:, None, :, :]

    def masked_scores():
        raw = jnp.einsum(
            "cihd,cjhd->chij", query_four, key_four, preferred_element_type=jnp.float32
        )
        return jnp.where(allowed, raw * score_scale, -1e30)

    scores = masked_scores()
    row_max = jnp.max(scores, axis=-1, keepdims=True)
    log_total = row_max + jnp.log(jnp.sum(jnp.exp(scores - row_max), axis=-1, keepdims=True))
    probs_low = jnp.exp(scores - log_total).astype(jnp.bfloat16)
    context = jnp.einsum(
        "chij,cjhd->cihd", probs_low, value_four, preferred_element_type=jnp.float32
    )
    context = context.reshape(total_rows, local_width).astype(jnp.bfloat16)
    attn_part = matmul_plain(context, out_weight)
    attn_out = lax.psum(attn_part, "tensor") + out_bias.astype(jnp.float32)
    hidden_res = token_f + attn_out
    normed_two, inv_two = plain_norm_stats(hidden_res)
    second_in = (normed_two * gains[1] + shifts[1]).astype(jnp.bfloat16)
    upper = matmul_plain(second_in, up_weight) + up_bias.astype(jnp.float32)
    sigma = jax.nn.sigmoid(1.702 * upper)
    hidden = (upper * sigma).astype(jnp.bfloat16)
    mlp_part = matmul_plain(hidden, down_weight)
    result_rows = (
        hidden_res
        + lax.psum(mlp_part.astype(jnp.bfloat16), "tensor").astype(jnp.float32)
        + down_bias.astype(jnp.float32)
    )
    layer_out = row_slice(result_rows, row_start, share_rows).astype(jnp.bfloat16)
    grad_f = cotangent.astype(jnp.float32)
    down_grad = contract_rows(hidden, cotangent)
    down_bias_grad = jnp.sum(grad_f, axis=0)
    hidden_grad = contract_cols(cotangent, down_weight)
    upper_grad = (hidden_grad * (sigma + 1.702 * upper * sigma * (1.0 - sigma))).astype(
        jnp.bfloat16
    )
    up_grad = contract_rows(second_in, upper_grad)
    up_bias_grad = jnp.sum(upper_grad.astype(jnp.float32), axis=0)
    second_part = contract_cols(upper_grad, up_weight)
    second_grad = lax.psum(second_part, "tensor")
    residual_back, gain_two, shift_two = plain_norm_back(second_grad, normed_two, inv_two, gains[1])
    residual_full = grad_f + residual_back
    branch_grad = residual_full.astype(jnp.bfloat16)
    out_bias_grad = jnp.sum(branch_grad.astype(jnp.float32), axis=0)
    out_grad = contract_rows(context, branch_grad)
    context_grad = contract_cols(branch_grad, out_weight).astype(jnp.bfloat16).reshape(shape4)
    probs = jnp.exp(masked_scores() - log_total)
    probs_low = probs.astype(jnp.bfloat16)
    value_grad = jnp.einsum(
        "chij,cihd->cjhd", probs_low, context_grad, preferred_element_type=jnp.float32
    )
    prob_grad = jnp.einsum(
        "cihd,cjhd->chij", context_grad, value_four, preferred_element_type=jnp.float32
    )
    score_grad = probs * (prob_grad - jnp.sum(prob_grad * probs, axis=-1, keepdims=True))
    score_grad = score_grad.astype(jnp.bfloat16)
    query_grad = (
        jnp.einsum("chij,cjhd->cihd", score_grad, key_four, preferred_element_type=jnp.float32)
        * score_scale
    )
    key_grad = (
        jnp.einsum("chij,cihd->cjhd", score_grad, query_four, preferred_element_type=jnp.float32)
        * score_scale
    )
    query_grad = query_grad.reshape(total_rows, local_width).astype(jnp.bfloat16)
    key_grad = key_grad.reshape(total_rows, local_width).astype(jnp.bfloat16)
    value_grad = value_grad.reshape(total_rows, local_width).astype(jnp.bfloat16)
    qkv_grad = jnp.stack(
        [
            contract_rows(first_in, query_grad),
            contract_rows(first_in, key_grad),
            contract_rows(first_in, value_grad),
        ]
    )
    qv_bias_grad = jnp.stack(
        [
            jnp.sum(query_grad.astype(jnp.float32), axis=0),
            jnp.sum(value_grad.astype(jnp.float32), axis=0),
        ]
    )
    first_part = (
        contract_cols(query_grad, qkv_weight[0])
        + contract_cols(key_grad, qkv_weight[1])
        + contract_cols(value_grad, qkv_weight[2])
    )
    first_grad = lax.psum(first_part.astype(jnp.bfloat16), "tensor").astype(jnp.float32)
    input_back, gain_one, shift_one = plain_norm_back(first_grad, normed_one, inv_one, gains[0])
    input_grad = row_slice(residual_full + input_back, row_start, share_rows)
    gain_grads = jnp.stack([gain_one, gain_two])
    shift_grads = jnp.stack([shift_one, shift_two])
    summed = (
        lax.psum(qkv_grad.astype(jnp.bfloat16), "dp").astype(jnp.float32),
        lax.psum(qv_bias_grad.astype(jnp.bfloat16), "dp").astype(jnp.float32),
        lax.psum(out_grad.astype(jnp.bfloat16), "dp").astype(jnp.float32),
        lax.psum(out_bias_grad.astype(jnp.bfloat16), "dp").astype(jnp.float32),
        lax.psum(up_grad.astype(jnp.bfloat16), "dp").astype(jnp.float32),
        lax.psum(up_bias_grad.astype(jnp.bfloat16), "dp").astype(jnp.float32),
        lax.psum(down_grad.astype(jnp.bfloat16), "dp").astype(jnp.float32),
        lax.psum(down_bias_grad.astype(jnp.bfloat16), "dp").astype(jnp.float32),
        lax.psum(gain_grads.astype(jnp.bfloat16), "dp").astype(jnp.float32),
        lax.psum(shift_grads.astype(jnp.bfloat16), "dp").astype(jnp.float32),
    )
    return (
        layer_out,
        input_grad,
        summed[0],
        summed[1],
        summed[2],
        summed[3],
        summed[4],
        summed[5],
        summed[6],
        summed[7],
        summed[8],
        summed[9],
    )


def solution(mesh):
    dp, tensor = mesh.shape["dp"], mesh.shape["tensor"]
    if tensor == 2 and dp == 16:
        body = functools.partial(shards, dp // 4)
    else:
        body = shards_by_heads
    return jax.shard_map(
        body,
        mesh=mesh,
        in_specs=(P("dp", None), P("dp"), P(None, None, "tensor"), P(None, "tensor"), P("tensor", None), P(), P(None, "tensor"), P("tensor"), P("tensor", None), P(), P(), P(), P("dp", None)),
        out_specs=(P(("dp", "tensor"), None), P(("dp", "tensor"), None), P(None, None, "tensor"), P(None, "tensor"), P("tensor", None), P(), P(None, "tensor"), P("tensor"), P("tensor", None), P(), P(), P()),
        check_vma=False,
    )
```

```python
import functools

import jax
import jax.numpy as jnp
from jax import lax
from jax.experimental import pallas as pl
from jax.experimental.pallas import tpu as pltpu
from jax.sharding import PartitionSpec as P

HD = 64
EPSILON = 1e-05
F32 = jnp.float32
BF16 = jnp.bfloat16
LOG2E = 1.4426950408889634
UNITS = 12
MESH = pl.DeviceIdType.MESH


def nn(left, right):
    return lax.dot_general(left, right, (((1,), (0,)), ((), ())), preferred_element_type=F32)


def nt(left, right):
    return lax.dot_general(left, right, (((1,), (1,)), ((), ())), preferred_element_type=F32)


def tn(left, right):
    return lax.dot_general(left, right, (((0,), (0,)), ((), ())), preferred_element_type=F32)


def loop(count, body):
    lax.fori_loop(0, count, lambda i, c: (body(i), c)[1], 0)


def norm(rows):
    center = rows - jnp.mean(rows, axis=-1, keepdims=True)
    inv = lax.rsqrt(jnp.mean(center * center, axis=-1, keepdims=True) + EPSILON)
    return center * inv, inv


def norm_back(grad, normed, inv, gain):
    t = grad * gain
    inner = jnp.mean(t * normed, axis=-1, keepdims=True)
    return inv * (t - jnp.mean(t, axis=-1, keepdims=True) - normed * inner)


def colsum(x):
    return jnp.sum(x, axis=0, keepdims=True)


class Layer:
    def __init__(self, caps, slots, pad, refs):
        self.caps, self.slots, self.pad = caps, slots, pad
        self.rows = caps * pad
        self.__dict__.update(refs)

    def head_mask(self, h, rows):
        lane = lax.broadcasted_iota(jnp.int32, (rows, 256), 1)
        return (lane >= h * HD) & (lane < (h + 1) * HD)

    def stack(self, block):
        parts = []
        for h in range(4):
            parts.append(jnp.where(self.head_mask(h, self.pad), block, jnp.zeros_like(block)))
        return jnp.concatenate(parts, axis=0)

    def unstack(self, block):
        out = None
        for h in range(4):
            part = block[h * self.pad : (h + 1) * self.pad]
            out = part if out is None else jnp.where(self.head_mask(h, self.pad), part, out)
        return out

    def widen(self, src, base, dst):
        total = src.shape[0]
        tile = self.slots * 2 if total % (self.slots * 2) == 0 else self.slots
        tile = 176 if total % 176 == 0 else total
        def conv(i):
            r = pl.ds(pl.multiple_of(i * tile, 16), tile)
            self.stage[r, :] = src[r, :].astype(F32)
        loop(total // tile, conv)
        self.stage[total : total + 16, :] = jnp.zeros((16, self.stage.shape[1]), F32)
        for c in range(self.caps):
            off = c * self.slots
            low = off // 8 * 8
            v = self.stage[pl.ds(pl.multiple_of(base + low, 8), self.pad + 8), :]
            v = v[off - low : off - low + self.pad]
            row = lax.broadcasted_iota(jnp.int32, v.shape, 0)
            v = jnp.where(row < self.slots, v, 0.0)
            dst[c * self.pad : (c + 1) * self.pad, :] = v.astype(BF16)

    def crows(self, c):
        return pl.ds(pl.multiple_of(c * self.pad, self.pad), self.pad)

    def norm_one(self):
        gain, shift = self.gains[0:1, :].astype(F32), self.shifts[0:1, :].astype(F32)
        def cap(c):
            r = self.crows(c)
            n, inv = norm(self.xs[r, :].astype(F32))
            self.n1[r, :] = n
            self.r1[r, :] = jnp.broadcast_to(inv, (self.pad, 128))
            self.a1[r, :] = (n * gain + shift).astype(BF16)
        loop(self.caps, cap)

    def biases(self, s, qvb, ub):
        for j in range(3):
            if j == 1:
                self.bias_qkv[s * 3 + j] = jnp.zeros((1, 256), F32)
            else:
                self.bias_qkv[s * 3 + j] = qvb[j // 2 : j // 2 + 1, :].astype(F32)
        up = ub[...].astype(F32).reshape(1, -1)
        for n in range(4):
            self.bias_up[s * 4 + n] = up[:, n * 256 : (n + 1) * 256]

    def qkv(self, i):
        s, j = i // 3, lax.rem(i, 3)
        out = nn(self.a1[...], self.w[s * UNITS + j]) + self.bias_qkv[i]
        self.pqkv[i] = out.astype(BF16)

    def attention(self, i):
        s, c = i // self.caps, lax.rem(i, self.caps)
        r = self.crows(c)
        q = self.pqkv[s * 3, r, :]
        km = self.stack(self.pqkv[s * 3 + 1, r, :])
        vm = self.stack(self.pqkv[s * 3 + 2, r, :])
        st = nt(km, q)
        length = self.lengths[self.cap_base + c]
        jj = lax.broadcasted_iota(jnp.int32, (self.pad, self.pad), 0)
        ii = lax.broadcasted_iota(jnp.int32, (self.pad, self.pad), 1)
        allowed = (jj <= ii) & (jj < length)
        blocks = []
        for h in range(4):
            blk = jnp.where(allowed, st[h * self.pad : (h + 1) * self.pad], -1e30)
            top = jnp.max(blk, axis=0, keepdims=True)
            e = jnp.exp2((blk - top) * (HD**-0.5 * LOG2E))
            blocks.append(e * (1.0 / jnp.sum(e, axis=0, keepdims=True)))
        p = jnp.concatenate(blocks, axis=0)
        self.probs[i] = p
        self.ctx[s, r, :] = tn(p.astype(BF16), vm).astype(BF16)

    def attention_back(self, i):
        s, c = i // self.caps, lax.rem(i, self.caps)
        r = self.crows(c)
        q = self.pqkv[s * 3, r, :]
        k = self.pqkv[s * 3 + 1, r, :]
        v = self.pqkv[s * 3 + 2, r, :]
        d = self.dctx[s, r, :]
        p = self.probs[i]
        self.dqkv[s * 3 + 2, r, :] = self.unstack(nn(p.astype(BF16), d)).astype(BF16)
        dp = nt(self.stack(v), d)
        blocks = []
        for h in range(4):
            rr = slice(h * self.pad, (h + 1) * self.pad)
            blocks.append(p[rr] * (dp[rr] - jnp.sum(dp[rr] * p[rr], axis=0, keepdims=True)))
        ds = jnp.concatenate(blocks, axis=0).astype(BF16)
        self.dqkv[s * 3 + 1, r, :] = (self.unstack(nn(ds, q)) * HD**-0.5).astype(BF16)
        self.dqkv[s * 3, r, :] = (tn(ds, self.stack(k)) * HD**-0.5).astype(BF16)

    def project(self, i):
        tile = self.rows // 4
        r = pl.ds(pl.multiple_of(i * tile, 16), tile)
        gain, shift = self.gains[1:2, :].astype(F32), self.shifts[1:2, :].astype(F32)
        c0, c1 = self.ctx[0, r, :], self.ctx[1, r, :]
        halves = []
        for n in range(2):
            w = slice(n * 256, (n + 1) * 256)
            halves.append(nn(c0, self.w[3, w, :]) + nn(c1, self.w[UNITS + 3, w, :]))
        o = jnp.concatenate(halves, axis=1)
        h1 = self.xs[r, :].astype(F32) + o + self.ob[...].astype(F32).reshape(1, -1)
        self.h1[r, :] = h1
        n, inv = norm(h1)
        self.n2[r, :] = n
        self.r2[r, :] = jnp.broadcast_to(inv, (tile, 128))
        self.a2[r, :] = (n * gain + shift).astype(BF16)

    def wup(self, m):
        return (m // 4) * UNITS + 4 + lax.rem(m, 4)

    def wdown(self, m):
        return (m // 4) * UNITS + 8 + lax.rem(m, 4)

    def up(self, m):
        u = nn(self.a2[...], self.w[self.wup(m)]) + self.bias_up[m]
        sg = 0.5 * jnp.tanh(0.851 * u) + 0.5
        h = u * sg
        self.hid[m] = h.astype(BF16)
        self.act[m] = sg + 1.702 * h * (1.0 - sg)

    def down_grad(self, m):
        w = tn(self.hid[m], self.g[...]).astype(BF16)
        s, n = m // 4, lax.rem(m, 4)
        self.grads[n, s, 0:256, :] = w[:, :256]
        self.grads[n, s, 256:512, :] = w[:, 256:]

    def hidden_back(self, m):
        w = self.wdown(m)
        back = nt(self.g[:, 0:256], self.w[w, 0:256, :]) + nt(self.g[:, 256:512], self.w[w, 256:512, :])
        du = (back * self.act[m]).astype(BF16)
        self.du[m] = du
        self.small_up[m] = colsum(du.astype(F32))

    def up_grad(self, m):
        s, n = m // 4, lax.rem(m, 4)
        self.grads[4 + n, s] = tn(self.a2[...], self.du[m]).astype(BF16)

    def half_tile(self, i):
        tile = self.rows // 2
        r = pl.ds(pl.multiple_of((i // 2) * tile, 16), tile)
        return r, lax.rem(i, 2)

    def second_grad(self, i):
        r, n = self.half_tile(i)
        w = pl.ds(pl.multiple_of(n * 256, 256), 256)
        acc = None
        for m in range(8):
            part = nt(self.du[m, r, :], self.w[(m // 4) * UNITS + 4 + m % 4, w, :])
            acc = part if acc is None else acc + part
        self.e[r, w] = acc

    def mlp_out(self, i):
        r, n = self.half_tile(i)
        w = pl.ds(pl.multiple_of(n * 256, 256), 256)
        acc = self.h1[r, w] + self.db[w].astype(F32).reshape(1, -1)
        for m in range(8):
            acc = acc + nn(self.hid[m, r, :], self.w[(m // 4) * UNITS + 8 + m % 4, w, :])
        self.h1[r, w] = acc

    def norm_two_back(self):
        gain = self.gains[1:2, :].astype(F32)
        zero = jnp.zeros((1, gain.shape[1]), F32)
        def cap(c, carry):
            gg, sg, ob, db = carry
            r = self.crows(c)
            e, n, g = self.e[r, :], self.n2[r, :], self.g[r, :].astype(F32)
            dh = g + norm_back(e, n, self.r2[r, 0:1], gain)
            self.dh1[r, :] = dh
            dob = dh.astype(BF16)
            self.dob[r, :] = dob
            return (gg + colsum(e * n), sg + colsum(e), ob + colsum(dob.astype(F32)), db + colsum(g))
        gg, sg, ob, db = lax.fori_loop(0, self.caps, cap, (zero, zero, zero, zero))
        self.small[1:2, :], self.small[3:4, :], self.small[4:5, :], self.small[5:6, :] = gg, sg, ob, db

    def out_back(self, s):
        w = tn(self.ctx[s], self.dob[...]).astype(BF16)
        self.grads[8, s, 0:256, :] = w[:, :256]
        self.grads[8, s, 256:512, :] = w[:, 256:]
        wo = s * UNITS + 3
        back = nt(self.dob[:, 0:256], self.w[wo, 0:256, :]) + nt(self.dob[:, 256:512], self.w[wo, 256:512, :])
        self.dctx[s] = back.astype(BF16)

    def qkv_grad(self, i):
        s, j = i // 3, lax.rem(i, 3)
        d = self.dqkv[i]
        self.grads[9 + j, s] = tn(self.a1[...], d).astype(BF16)
        self.small_qkv[i] = colsum(d.astype(F32))

    def first_grad(self, i):
        r, n = self.half_tile(i)
        w = pl.ds(pl.multiple_of(n * 256, 256), 256)
        acc = None
        for m in range(6):
            part = nt(self.dqkv[m, r, :], self.w[(m // 3) * UNITS + m % 3, w, :])
            acc = part if acc is None else acc + part
        self.e[r, w] = acc

    def norm_one_back(self, out, base):
        gain = self.gains[0:1, :].astype(F32)
        zero = jnp.zeros((1, gain.shape[1]), F32)
        gg, sg = zero, zero
        for c in range(self.caps):
            r = slice(c * self.pad, (c + 1) * self.pad)
            e, n = self.e[r, :], self.n1[r, :]
            dx = self.dh1[r, :] + norm_back(e, n, self.r1[r, 0:1], gain)
            out[base + c * self.slots : base + (c + 1) * self.slots, :] = dx[: self.slots]
            gg, sg = gg + colsum(e * n), sg + colsum(e)
        self.small[0:1, :], self.small[2:3, :] = gg, sg

    def layer_out(self, flat, out):
        for c in range(self.caps):
            flat[c * self.slots : (c + 1) * self.slots, :] = self.h1[c * self.pad : c * self.pad + self.slots, :]
        out[...] = flat[0 : self.caps * self.slots, :].astype(BF16)

    def pack_small(self, out):
        def put(slot, row, value):
            for i in range(value.shape[1] // 128):
                out[slot, row + i : row + i + 1, :] = value[:, i * 128 : (i + 1) * 128]
        for slot in range(2):
            out[slot] = jnp.zeros(out.shape[1:], F32)
            put(slot, 0, self.small_qkv[slot * 3])
            put(slot, 2, self.small_qkv[slot * 3 + 2])
            for n in range(4):
                put(slot, 4 + 2 * n, self.small_up[slot * 4 + n])
            for i, k in enumerate((4, 5, 0, 1, 2, 3)):
                put(slot, 12 + 4 * i, self.small[k : k + 1, :])


class Peers:
    def __init__(self):
        dp, t = lax.axis_index("dp"), lax.axis_index("tensor")
        depth = lax.axis_size("dp") // 4
        self.core = lax.rem(dp, 2)
        self.x = lax.rem(dp // 2, 2)
        self.z = dp // 4
        self.t = t
        self.to_y = (dp, 1 - t)
        self.to_x = (dp + 2 - 4 * self.x, t)
        self.to_core = (dp + 1 - 2 * self.core, t)
        self.depth = depth
        self.to_z = [(lax.rem(self.z + k, depth) * 4 + lax.rem(dp, 4), t) for k in range(1, depth)]
        self.z_of = [lax.rem(self.z + k, depth) for k in range(1, depth)]

    def all(self):
        return [self.to_y, self.to_x, self.to_core] + self.to_z

    def greet(self):
        barrier = pltpu.get_barrier_semaphore()
        for peer in self.all():
            pl.semaphore_signal(barrier, inc=1, device_id=peer, device_id_type=MESH)

    def meet(self):
        pl.semaphore_wait(pltpu.get_barrier_semaphore(), len(self.all()))


def rows(index, size):
    return pl.ds(pl.multiple_of(index * size, size), size)


def remote(src, dst, send, recv, peer):
    return pltpu.make_async_remote_copy(src_ref=src, dst_ref=dst, send_sem=send, recv_sem=recv, device_id=peer, device_id_type=MESH)


class Weights:
    def __init__(self, peers, w, send, recv):
        self.p, self.w, self.send, self.recv = peers, w, send, recv
        self.quarter = peers.core * 2 + peers.x
        self.size = w.shape[1] // 4

    def y(self, u):
        r = rows(self.quarter, self.size)
        return remote(self.w.at[u, r], self.w.at[UNITS + u, r], self.send.at[u, 0], self.recv.at[u, 0], self.p.to_y)

    def x(self, u):
        part = self.w.at[UNITS + u, rows(self.quarter, self.size)]
        return remote(part, part, self.send.at[u, 1], self.recv.at[u, 1], self.p.to_x)

    def c(self, u):
        part = self.w.at[UNITS + u, rows(self.p.core, self.size * 2)]
        return remote(part, part, self.send.at[u, 2], self.recv.at[u, 2], self.p.to_core)

    def relay_x(self, u):
        self.y(u).wait_recv()
        self.x(u).start()

    def relay_c(self, u):
        self.x(u).wait_recv()
        self.c(u).start()

    def ready(self, u):
        self.c(u).wait_recv()

    def drain(self, u):
        self.y(u).wait_send()
        self.x(u).wait_send()
        self.c(u).wait_send()


class Reduce:
    def __init__(self, peers, refs, sem0, send, recv):
        self.p = peers
        self.g, self.cr, self.yr, self.xr, self.zr, self.f = refs
        self.sem0, self.send, self.recv = sem0, send, recv
        self.count = self.g.shape[0]
        self.full = self.g.shape[2]
        self.half, self.quarter = self.full // 2, self.full // 4
        self.shard = self.quarter // peers.depth

    def sems(self, n, k):
        return self.send.at[self.sem0 + n, k], self.recv.at[self.sem0 + n, k]

    def c(self, n):
        return remote(self.g.at[n, :, rows(1 - self.p.core, self.half)], self.cr.at[n], *self.sems(n, 0), self.p.to_core)

    def y(self, n):
        return remote(self.cr.at[n, 1], self.yr.at[n], *self.sems(n, 1), self.p.to_y)

    def x(self, n):
        return remote(self.cr.at[n, 0, rows(1 - self.p.x, self.quarter)], self.xr.at[n], *self.sems(n, 2), self.p.to_x)

    def z(self, n):
        return [
            remote(
                self.cr.at[n, 0, pl.ds(pl.multiple_of(self.p.x * self.quarter + self.p.z_of[k] * self.shard, self.shard), self.shard)],
                self.zr.at[n, k],
                *self.sems(n, 5 + k),
                self.p.to_z[k],
            )
            for k in range(self.p.depth - 1)
        ]

    def own_shard(self):
        p = self.p
        return pl.ds(pl.multiple_of(p.core * self.half + p.x * self.quarter + p.z * self.shard, self.shard), self.shard)

    def za(self, n):
        part = self.f.at[n, self.own_shard()]
        return [
            remote(part, part, *self.sems(n, 4 + self.p.depth + k), self.p.to_z[k]) for k in range(self.p.depth - 1)
        ]

    def xa(self, n):
        part = self.f.at[n, pl.ds(pl.multiple_of(self.p.core * self.half + self.p.x * self.quarter, self.quarter), self.quarter)]
        return remote(part, part, *self.sems(n, 3), self.p.to_x)

    def ca(self, n):
        part = self.f.at[n, rows(self.p.core, self.half)]
        return remote(part, part, *self.sems(n, 4), self.p.to_core)

    def c_start(self, n):
        self.c(n).start()

    def c_done(self, n):
        self.c(n).wait_recv()
        self.cr[n] = self.cr[n] + self.g[n, :, rows(self.p.core, self.half), :]
        self.y(n).start()

    def y_done(self, n):
        self.y(n).wait_recv()
        self.cr[n, 0] = self.cr[n, 0] + self.yr[n]
        self.x(n).start()

    def x_done(self, n):
        self.x(n).wait_recv()
        r = rows(self.p.x, self.quarter)
        self.cr[n, 0, r, :] = self.cr[n, 0, r, :] + self.xr[n]
        for copy in self.z(n):
            copy.start()

    def z_done(self, n):
        for copy in self.z(n):
            copy.wait_recv()
        mine = pl.ds(pl.multiple_of(self.p.x * self.quarter + self.p.z * self.shard, self.shard), self.shard)
        total = self.cr[n, 0, mine, :].astype(F32)
        for k in range(self.p.depth - 1):
            total = total + self.zr[n, k].astype(F32)
        self.f[n, self.own_shard(), :] = total.astype(self.f.dtype)
        for copy in self.za(n):
            copy.start()

    def za_done(self, n):
        for copy in self.za(n):
            copy.wait_recv()
        self.xa(n).start()

    def xa_done(self, n):
        self.xa(n).wait_recv()
        self.ca(n).start()

    def ca_done(self, n):
        self.ca(n).wait_recv()

    def drain(self, n):
        for copy in [self.c(n), self.y(n), self.x(n), self.xa(n), self.ca(n)] + self.z(n) + self.za(n):
            copy.wait_send()


def when(condition, body):
    if isinstance(condition, bool):
        if condition:
            body()
    else:
        pl.when(condition)(body)


ON_WEIGHTS = ("relay_x", "relay_c", "ready")
ON_GRADS = ("c_start", "c_done", "y_done", "x_done", "z_done", "za_done", "xa_done", "ca_done")
PLAN = {
    "norm_one": (),
    "qkv_own": (),
    "att_own": ((1, 0, (0,)), ),
    "widen_g": ((0, 0, (1,)), ),
    "qkv_other": ((0, 0, (2, 100, 3, 200,)), (1, 0, (101, 4, 201,)), (2, 0, (102, 5, 202,)), ),
    "att_other": ((0, 0, (103,)), (1, 0, (104, 6,)), ),
    "proj": ((0, 0, (105, 7, 8, 203,)), ),
    "updown": ((0, 0, (9, 106,)), (0, 1, (204,)), (0, 3, (10,)), (1, 0, (1000, 107,)), (1, 1, (205,)), (1, 2, (11,)), (1, 3, (108, 1100,)), (2, 0, (1001,)), (2, 1, (206,)), (2, 2, (109,)), (2, 3, (1101,)), (3, 0, (1002,)), (3, 1, (110, 207,)), ),
    "hbug": ((0, 0, (1003, 111, 1102,)), (0, 1, (1200, 208,)), (1, 0, (1004,)), (1, 1, (209,)), (1, 2, (1103,)), (1, 3, (1201,)), (2, 0, (1005, 1300,)), (2, 1, (210,)), (3, 0, (1006, 1202, 1104,)), (3, 1, (211,)), (3, 2, (1301,)), ),
    "sg": ((0, 0, (1007, 1400,)), (1, 0, (1105, 1203,)), (2, 0, (1302,)), ),
    "ntb": (),
    "ob": ((0, 0, (1401, 1204, 1303, 1500, 1106,)), ),
    "ab": ((0, 0, (1008,)), (1, 0, (1402, 1205, 1107,)), (2, 0, (1501, 1304,)), (3, 0, (1600, 1403, 1206, 1108,)), ),
    "qg": ((0, 0, (1700, 1502, 1305,)), (1, 0, (1009, 1601, 1404, 1207,)), (2, 0, (1010, 1306, 1109, 1503,)), (2, 1, (1701,)), ),
    "fg": ((0, 0, (1011,)), (1, 0, (1602, 1208, 1405, 1110,)), (3, 0, (1702, 1307,)), ),
    "nob": ((0, 0, (1504,)), ),
    "mo": ((0, 0, (1012, 1603,)), (1, 0, (1406, 1209, 1111,)), (2, 0, (1703, 1308,)), (3, 0, (1505,)), ),
    "lo": (),
    "tail": ((0, 0, (1604, 1112, 1407, 1210, 1704, 1309, 1506, 1605, 1408, 1211, 1705, 1212, 1310, 1507, 1606, 1409, 1706, 1311, 1508, 1312, 1607, 1410, 1707, 1509, 1608, 1411, 1708, 1412, 1510, 1609, 1709, 1511, 1512, 1610, 1710, 1611, 1612, 1711, 1712,)), ),
}


def kernel(caps, slots, pad, names_in, *all_refs):
    L = Layer(caps, slots, pad, dict(zip(names_in, all_refs)))
    peers = Peers()
    peers.greet()
    L.cap_base = peers.t * caps
    weights = Weights(peers, L.w, L.wsend, L.wrecv)
    big = Reduce(peers, (L.grads, L.cr, L.yr, L.xr, L.zr, L.f), 0, L.gsend, L.grecv)
    small = Reduce(peers, (L.sg, L.scr, L.syr, L.sxr, L.szr, L.sf), UNITS, L.gsend, L.grecv)
    outs = lambda n: pltpu.make_async_copy(L.f.at[n], L.f_out.at[n], L.osem.at[n])

    def arrive(codes):
        for code in codes:
            stage, unit = code // 100, code % 100
            if stage < 10:
                getattr(weights, ON_WEIGHTS[stage])(unit)
            elif unit == UNITS:
                getattr(small, ON_GRADS[stage - 10])(0)
            else:
                getattr(big, ON_GRADS[stage - 10])(unit)
                if stage == 17:
                    outs(unit).start()

    def run(name, count, *parts):
        def body(i):
            for k, part in enumerate(parts):
                for when_i, when_k, codes in PLAN[name]:
                    if when_k == k:
                        when(i == when_i, functools.partial(arrive, codes))
                part(i)

        if count == 1:
            body(0)
        else:
            loop(count, body)

    local = []

    def load(a, b):
        copy = pltpu.make_async_copy(a, b, L.lsem.at[len(local)])
        copy.start()
        local.append(copy)

    load(L.tok, L.tok_v)
    for j in range(3):
        load(L.wqkv_a.at[j], L.w.at[j])
    for n in range(2):
        load(L.wo_a.at[:, pl.ds(n * 256, 256)], L.w.at[3, pl.ds(n * 256, 256)])
    for n in range(4):
        load(L.wu_a.at[:, pl.ds(n * 256, 256)], L.w.at[4 + n])
    for n in range(4):
        for k in range(2):
            load(L.wd_a.at[pl.ds(n * 256, 256), pl.ds(k * 256, 256)], L.w.at[8 + n, pl.ds(k * 256, 256)])
    load(L.cot, L.cot_v)
    local[0].wait()
    L.widen(L.tok_v, peers.t * caps * slots, L.xs)
    for copy in local[1:]:
        copy.wait()
    peers.meet()
    bias_send = [
        remote(L.qvb, L.qvb_b, L.bsem.at[0], L.bsem.at[1], peers.to_y),
        remote(L.ub, L.ub_b, L.bsem.at[2], L.bsem.at[3], peers.to_y),
    ]
    for copy in bias_send:
        copy.start()
    loop(UNITS, lambda u: weights.y(u).start())
    attend = lambda i: [L.attention(4 * i + k) for k in range(4)]

    def rows_and_biases():
        L.widen(L.cot_v, peers.t * caps * slots, L.g)
        for copy in bias_send:
            copy.wait()
        L.biases(1, L.qvb_b, L.ub_b)

    size = caps * slots
    base = (size + 7) // 8 * 8
    dx_copy = pltpu.make_async_copy(L.stage.at[pl.ds(base, size)], L.dx_out, L.osem.at[UNITS])
    y_copy = pltpu.make_async_copy(L.yb, L.y_out, L.osem.at[UNITS + 1])
    s_copy = pltpu.make_async_copy(L.sf.at[0], L.s_out, L.osem.at[UNITS + 2])

    def input_rows():
        L.norm_one_back(L.stage, base)
        dx_copy.start()
        L.pack_small(L.sg.at[0])

    def output_rows():
        L.layer_out(L.stage, L.yb)
        y_copy.start()

    run("norm_one", 1, lambda i: (L.norm_one(), L.biases(0, L.qvb, L.ub)))
    run("qkv_own", 3, L.qkv)
    run("att_own", caps // 4, attend)
    run("widen_g", 1, lambda i: rows_and_biases())
    run("qkv_other", 3, lambda j: L.qkv(3 + j))
    run("att_other", caps // 4, lambda i: attend(caps // 4 + i))
    run("proj", 4, L.project)
    run("updown", 4, L.up, lambda n: L.up(4 + n), L.down_grad, lambda n: L.down_grad(4 + n))
    run("hbug", 4, L.hidden_back, lambda n: L.hidden_back(4 + n), L.up_grad, lambda n: L.up_grad(4 + n))
    run("sg", 4, L.second_grad)
    run("ntb", 1, lambda i: L.norm_two_back())
    run("ob", 2, L.out_back)
    run("ab", caps // 2, lambda i: [L.attention_back(4 * i + k) for k in range(4)])
    run("qg", 3, L.qkv_grad, lambda j: L.qkv_grad(3 + j))
    run("fg", 4, L.first_grad)
    run("nob", 1, lambda i: input_rows())
    run("mo", 4, L.mlp_out)
    run("lo", 1, lambda i: output_rows())
    run("tail", 1, lambda i: s_copy.start())

    def drain(n):
        weights.drain(n)
        big.drain(n)
        outs(n).wait()

    loop(UNITS, drain)
    small.drain(0)
    dx_copy.wait()
    y_copy.wait()
    s_copy.wait()


def finish(f, s, y, dx, y_out, dx_out, qkv, out, up, down, qvb, ob, ub, db, gg, sh, f_v, y_v, dx_v, wide, sem_in, sem_out, sem_io):
    ins = [pltpu.make_async_copy(f.at[n], f_v.at[n], sem_in.at[n]) for n in range(UNITS)]
    for copy in ins:
        copy.start()
    rows_in = [pltpu.make_async_copy(y, y_v, sem_io.at[0]), pltpu.make_async_copy(dx, dx_v, sem_io.at[1])]
    for copy in rows_in:
        copy.start()
    io = []
    for n in range(UNITS):
        ins[n].wait()
        wide[n] = f_v[n].astype(F32)
        if n < 4 or n == 8:
            parts = []
            for k in range(2):
                c = pl.ds(k * 256, 256)
                dst = down.at[pl.ds(n * 256, 256), c] if n < 4 else out.at[:, c]
                parts.append((wide.at[n, c], dst))
        elif n < 8:
            parts = [(wide.at[n], up.at[:, pl.ds((n - 4) * 256, 256)])]
        else:
            parts = [(wide.at[n], qkv.at[n - 9])]
        for k, (a, b) in enumerate(parts):
            copy = pltpu.make_async_copy(a, b, sem_out.at[2 * n + k])
            copy.start()
            io.append(copy)
        if n == 3:
            for copy in rows_in:
                copy.wait()
            for k, (a, b) in enumerate(((y_v, y_out), (dx_v, dx_out))):
                copy = pltpu.make_async_copy(a, b, sem_io.at[2 + k])
                copy.start()
                io.append(copy)

    def row(first, count):
        return jnp.concatenate([s[first + i : first + i + 1, :] for i in range(count)], axis=1)

    qvb[0:1, :], qvb[1:2, :] = row(0, 2), row(2, 2)
    ub[...] = row(4, 8)
    ob[...], db[...] = row(12, 4), row(16, 4)
    gg[0:1, :], gg[1:2, :] = row(20, 4), row(24, 4)
    sh[0:1, :], sh[1:2, :] = row(28, 4), row(32, 4)
    for copy in io:
        copy.wait()


def shards(depth, tokens, lengths, qkv_weight, qv_bias, out_weight, out_bias, up_weight, up_bias, down_weight, down_bias, norm_gain, norm_shift, cotangent):
    total, width = tokens.shape
    count = lengths.shape[0]
    slots = total // count
    caps = count // 2
    pad = (slots + 15) // 16 * 16
    rws = caps * pad
    V = pl.BlockSpec(memory_space=pltpu.VMEM)
    A = pl.BlockSpec(memory_space=pl.ANY)
    S = pl.BlockSpec(memory_space=pltpu.SMEM)
    ins = [
        ("tok", tokens, A), ("cot", cotangent, A), ("lengths", lengths, S),
        ("wqkv_a", qkv_weight, A), ("wo_a", out_weight, A), ("wu_a", up_weight, A), ("wd_a", down_weight, A),
        ("qvb", qv_bias, V), ("ub", up_bias, V),
        ("ob", out_bias, V), ("db", down_bias, V), ("gains", norm_gain, V), ("shifts", norm_shift, V),
    ]
    outs = [
        ("y_out", (caps * slots, 512), BF16), ("dx_out", (caps * slots, 512), F32),
        ("f_out", (UNITS, 512, 256), BF16), ("s_out", (128, 128), F32),
    ]
    vm = pltpu.VMEM
    sems = UNITS + 1, 3 + 2 * depth
    scr = [
        ("tok_v", vm((total, 512), BF16)), ("cot_v", vm((total, 512), BF16)),
        ("stage", vm((total + 16, 512), F32)), ("xs", vm((rws, 512), BF16)), ("g", vm((rws, 512), BF16)),
        ("n1", vm((rws, 512), F32)), ("r1", vm((rws, 128), F32)), ("a1", vm((rws, 512), BF16)),
        ("w", vm((2 * UNITS, 512, 256), BF16)), ("qvb_b", vm((2, 256), BF16)), ("ub_b", vm(up_bias.shape, BF16)),
        ("bias_qkv", vm((6, 1, 256), F32)), ("bias_up", vm((8, 1, 256), F32)),
        ("pqkv", vm((6, rws, 256), BF16)), ("probs", vm((2 * caps, 4 * pad, pad), F32)), ("ctx", vm((2, rws, 256), BF16)),
        ("h1", vm((rws, 512), F32)), ("n2", vm((rws, 512), F32)), ("r2", vm((rws, 128), F32)), ("a2", vm((rws, 512), BF16)),
        ("hid", vm((8, rws, 256), BF16)), ("act", vm((8, rws, 256), F32)), ("du", vm((8, rws, 256), BF16)),
        ("e", vm((rws, 512), F32)), ("dh1", vm((rws, 512), F32)), ("dob", vm((rws, 512), BF16)), ("dctx", vm((2, rws, 256), BF16)),
        ("dqkv", vm((6, rws, 256), BF16)), ("yb", vm((caps * slots, 512), BF16)),
        ("small", vm((8, 512), F32)), ("small_up", vm((8, 1, 256), F32)), ("small_qkv", vm((6, 1, 256), F32)),
        ("grads", vm((UNITS, 2, 512, 256), BF16)), ("cr", vm((UNITS, 2, 256, 256), BF16)), ("yr", vm((UNITS, 256, 256), BF16)),
        ("xr", vm((UNITS, 128, 256), BF16)), ("zr", vm((UNITS, depth - 1, 128 // depth, 256), BF16)), ("f", vm((UNITS, 512, 256), BF16)),
        ("sg", vm((1, 2, 128, 128), F32)), ("scr", vm((1, 2, 64, 128), F32)), ("syr", vm((1, 64, 128), F32)),
        ("sxr", vm((1, 32, 128), F32)), ("szr", vm((1, depth - 1, 32 // depth, 128), F32)), ("sf", vm((1, 128, 128), F32)),
        ("lsem", pltpu.SemaphoreType.DMA((20,))), ("osem", pltpu.SemaphoreType.DMA((UNITS + 3,))), ("bsem", pltpu.SemaphoreType.DMA((4,))),
        ("wsend", pltpu.SemaphoreType.DMA((UNITS, 3))), ("wrecv", pltpu.SemaphoreType.DMA((UNITS, 3))),
        ("gsend", pltpu.SemaphoreType.DMA(sems)), ("grecv", pltpu.SemaphoreType.DMA(sems)),
    ]
    names = [n for n, _, _ in ins] + [n for n, _, _ in outs] + [n for n, _ in scr]
    y, dx, f, s = pl.pallas_call(
        functools.partial(kernel, caps, slots, pad, names),
        out_shape=[jax.ShapeDtypeStruct(s, d) for _, s, d in outs],
        in_specs=[s for _, _, s in ins],
        out_specs=[A] * len(outs),
        scratch_shapes=[s for _, s in scr],
        compiler_params=pltpu.CompilerParams(vmem_limit_bytes=61 << 20, collective_id=0, has_side_effects=True),
        name="layer",
    )(*[v for _, v, _ in ins])
    results = [
        (y.shape, BF16, A), (dx.shape, F32, A), (qkv_weight.shape, F32, A), (out_weight.shape, F32, A),
        (up_weight.shape, F32, A), (down_weight.shape, F32, A),
        (qv_bias.shape, F32, V), ((1, 512), F32, V), ((1, up_bias.shape[0]), F32, V), ((1, 512), F32, V), ((2, 512), F32, V), ((2, 512), F32, V),
    ]
    y, dx, qkv, out, up, down, qvb, ob, ub, db, gg, sh = pl.pallas_call(
        finish,
        out_shape=[jax.ShapeDtypeStruct(s, d) for s, d, _ in results],
        in_specs=[A, V, A, A],
        out_specs=[s for _, _, s in results],
        scratch_shapes=[
            vm((UNITS, 512, 256), BF16), vm(y.shape, BF16), vm(dx.shape, F32), vm((UNITS, 512, 256), F32),
            pltpu.SemaphoreType.DMA((UNITS,)), pltpu.SemaphoreType.DMA((2 * UNITS,)), pltpu.SemaphoreType.DMA((4,)),
        ],
        compiler_params=pltpu.CompilerParams(vmem_limit_bytes=61 << 20),
        name="finish",
    )(f, s, y, dx)
    return y, dx, qkv, qvb, out, ob[0], up, ub[0], down, db[0], gg, sh


def matmul_plain(left, right):
    return jnp.dot(left, right, preferred_element_type=jnp.float32)


def contract_rows(left, right):
    return lax.dot_general(
        left, right, (((0,), (0,)), ((), ())), preferred_element_type=jnp.float32
    )


def contract_cols(left, right):
    return lax.dot_general(
        left, right, (((1,), (1,)), ((), ())), preferred_element_type=jnp.float32
    )


def plain_norm_stats(values):
    center = values - jnp.mean(values, axis=-1, keepdims=True)
    inv_std = lax.rsqrt(jnp.mean(center * center, axis=-1, keepdims=True) + EPSILON)
    return (center * inv_std, inv_std)


def plain_norm_back(upstream, normed, inv_std, gain_vec):
    scaled = upstream * gain_vec
    inner_mean = jnp.mean(scaled * normed, axis=-1, keepdims=True)
    result = inv_std * (scaled - jnp.mean(scaled, axis=-1, keepdims=True) - normed * inner_mean)
    return (result, jnp.sum(upstream * normed, axis=0), jnp.sum(upstream, axis=0))


def row_slice(values, row_start, share_rows):
    return lax.dynamic_slice_in_dim(values, row_start, share_rows, 0)


def shards_by_heads(
    tokens,
    lengths,
    qkv_weight,
    qv_bias,
    out_weight,
    out_bias,
    up_weight,
    up_bias,
    down_weight,
    down_bias,
    norm_gain,
    norm_shift,
    cotangent,
):
    tensor_count = lax.axis_size("tensor")
    tensor_index = lax.axis_index("tensor")
    share_rows = tokens.shape[0] // tensor_count
    row_start = tensor_index * share_rows
    gains = norm_gain.astype(jnp.float32)
    shifts = norm_shift.astype(jnp.float32)
    total_rows = tokens.shape[0]
    count = lengths.shape[0]
    slots = total_rows // count
    local_width = qkv_weight.shape[2]
    local_heads = local_width // HD
    score_scale = HD ** (-0.5)
    qv_float = qv_bias.astype(jnp.float32)
    token_f = tokens.astype(jnp.float32)
    normed_one, inv_one = plain_norm_stats(token_f)
    first_in = (normed_one * gains[0] + shifts[0]).astype(jnp.bfloat16)
    queries = (matmul_plain(first_in, qkv_weight[0]) + qv_float[0]).astype(jnp.bfloat16)
    keys_all = matmul_plain(first_in, qkv_weight[1]).astype(jnp.bfloat16)
    values_all = (matmul_plain(first_in, qkv_weight[2]) + qv_float[1]).astype(jnp.bfloat16)
    shape4 = (count, slots, local_heads, HD)
    query_four = queries.reshape(shape4)
    key_four = keys_all.reshape(shape4)
    value_four = values_all.reshape(shape4)
    position = jnp.arange(slots)
    allowed = (position[None, :] <= position[:, None])[None, :, :] & (
        position[None, None, :] < lengths[:, None, None]
    )
    allowed = allowed[:, None, :, :]

    def masked_scores():
        raw = jnp.einsum(
            "cihd,cjhd->chij", query_four, key_four, preferred_element_type=jnp.float32
        )
        return jnp.where(allowed, raw * score_scale, -1e30)

    scores = masked_scores()
    row_max = jnp.max(scores, axis=-1, keepdims=True)
    log_total = row_max + jnp.log(jnp.sum(jnp.exp(scores - row_max), axis=-1, keepdims=True))
    probs_low = jnp.exp(scores - log_total).astype(jnp.bfloat16)
    context = jnp.einsum(
        "chij,cjhd->cihd", probs_low, value_four, preferred_element_type=jnp.float32
    )
    context = context.reshape(total_rows, local_width).astype(jnp.bfloat16)
    attn_part = matmul_plain(context, out_weight)
    attn_out = lax.psum(attn_part, "tensor") + out_bias.astype(jnp.float32)
    hidden_res = token_f + attn_out
    normed_two, inv_two = plain_norm_stats(hidden_res)
    second_in = (normed_two * gains[1] + shifts[1]).astype(jnp.bfloat16)
    upper = matmul_plain(second_in, up_weight) + up_bias.astype(jnp.float32)
    sigma = jax.nn.sigmoid(1.702 * upper)
    hidden = (upper * sigma).astype(jnp.bfloat16)
    mlp_part = matmul_plain(hidden, down_weight)
    result_rows = (
        hidden_res
        + lax.psum(mlp_part.astype(jnp.bfloat16), "tensor").astype(jnp.float32)
        + down_bias.astype(jnp.float32)
    )
    layer_out = row_slice(result_rows, row_start, share_rows).astype(jnp.bfloat16)
    grad_f = cotangent.astype(jnp.float32)
    down_grad = contract_rows(hidden, cotangent)
    down_bias_grad = jnp.sum(grad_f, axis=0)
    hidden_grad = contract_cols(cotangent, down_weight)
    upper_grad = (hidden_grad * (sigma + 1.702 * upper * sigma * (1.0 - sigma))).astype(
        jnp.bfloat16
    )
    up_grad = contract_rows(second_in, upper_grad)
    up_bias_grad = jnp.sum(upper_grad.astype(jnp.float32), axis=0)
    second_part = contract_cols(upper_grad, up_weight)
    second_grad = lax.psum(second_part, "tensor")
    residual_back, gain_two, shift_two = plain_norm_back(second_grad, normed_two, inv_two, gains[1])
    residual_full = grad_f + residual_back
    branch_grad = residual_full.astype(jnp.bfloat16)
    out_bias_grad = jnp.sum(branch_grad.astype(jnp.float32), axis=0)
    out_grad = contract_rows(context, branch_grad)
    context_grad = contract_cols(branch_grad, out_weight).astype(jnp.bfloat16).reshape(shape4)
    probs = jnp.exp(masked_scores() - log_total)
    probs_low = probs.astype(jnp.bfloat16)
    value_grad = jnp.einsum(
        "chij,cihd->cjhd", probs_low, context_grad, preferred_element_type=jnp.float32
    )
    prob_grad = jnp.einsum(
        "cihd,cjhd->chij", context_grad, value_four, preferred_element_type=jnp.float32
    )
    score_grad = probs * (prob_grad - jnp.sum(prob_grad * probs, axis=-1, keepdims=True))
    score_grad = score_grad.astype(jnp.bfloat16)
    query_grad = (
        jnp.einsum("chij,cjhd->cihd", score_grad, key_four, preferred_element_type=jnp.float32)
        * score_scale
    )
    key_grad = (
        jnp.einsum("chij,cihd->cjhd", score_grad, query_four, preferred_element_type=jnp.float32)
        * score_scale
    )
    query_grad = query_grad.reshape(total_rows, local_width).astype(jnp.bfloat16)
    key_grad = key_grad.reshape(total_rows, local_width).astype(jnp.bfloat16)
    value_grad = value_grad.reshape(total_rows, local_width).astype(jnp.bfloat16)
    qkv_grad = jnp.stack(
        [
            contract_rows(first_in, query_grad),
            contract_rows(first_in, key_grad),
            contract_rows(first_in, value_grad),
        ]
    )
    qv_bias_grad = jnp.stack(
        [
            jnp.sum(query_grad.astype(jnp.float32), axis=0),
            jnp.sum(value_grad.astype(jnp.float32), axis=0),
        ]
    )
    first_part = (
        contract_cols(query_grad, qkv_weight[0])
        + contract_cols(key_grad, qkv_weight[1])
        + contract_cols(value_grad, qkv_weight[2])
    )
    first_grad = lax.psum(first_part.astype(jnp.bfloat16), "tensor").astype(jnp.float32)
    input_back, gain_one, shift_one = plain_norm_back(first_grad, normed_one, inv_one, gains[0])
    input_grad = row_slice(residual_full + input_back, row_start, share_rows)
    gain_grads = jnp.stack([gain_one, gain_two])
    shift_grads = jnp.stack([shift_one, shift_two])
    summed = (
        lax.psum(qkv_grad.astype(jnp.bfloat16), "dp").astype(jnp.float32),
        lax.psum(qv_bias_grad.astype(jnp.bfloat16), "dp").astype(jnp.float32),
        lax.psum(out_grad.astype(jnp.bfloat16), "dp").astype(jnp.float32),
        lax.psum(out_bias_grad.astype(jnp.bfloat16), "dp").astype(jnp.float32),
        lax.psum(up_grad.astype(jnp.bfloat16), "dp").astype(jnp.float32),
        lax.psum(up_bias_grad.astype(jnp.bfloat16), "dp").astype(jnp.float32),
        lax.psum(down_grad.astype(jnp.bfloat16), "dp").astype(jnp.float32),
        lax.psum(down_bias_grad.astype(jnp.bfloat16), "dp").astype(jnp.float32),
        lax.psum(gain_grads.astype(jnp.bfloat16), "dp").astype(jnp.float32),
        lax.psum(shift_grads.astype(jnp.bfloat16), "dp").astype(jnp.float32),
    )
    return (
        layer_out,
        input_grad,
        summed[0],
        summed[1],
        summed[2],
        summed[3],
        summed[4],
        summed[5],
        summed[6],
        summed[7],
        summed[8],
        summed[9],
    )


def solution(mesh):
    dp, tensor = mesh.shape["dp"], mesh.shape["tensor"]
    if tensor == 2 and dp == 16:
        body = functools.partial(shards, dp // 4)
    else:
        body = shards_by_heads
    return jax.shard_map(
        body,
        mesh=mesh,
        in_specs=(P("dp", None), P("dp"), P(None, None, "tensor"), P(None, "tensor"), P("tensor", None), P(), P(None, "tensor"), P("tensor"), P("tensor", None), P(), P(), P(), P("dp", None)),
        out_specs=(P(("dp", "tensor"), None), P(("dp", "tensor"), None), P(None, None, "tensor"), P(None, "tensor"), P("tensor", None), P(), P(None, "tensor"), P("tensor"), P("tensor", None), P(), P(), P()),
        check_vma=False,
    )
```

```python
import functools

import jax
import jax.numpy as jnp
from jax import lax
from jax.experimental import pallas as pl
from jax.experimental.pallas import tpu as pltpu
from jax.sharding import PartitionSpec as P

HD = 64
EPSILON = 1e-05
F32 = jnp.float32
BF16 = jnp.bfloat16
LOG2E = 1.4426950408889634
UNITS = 12
VLIM = 54 << 20
MESH = pl.DeviceIdType.MESH


def nn(left, right):
    return lax.dot_general(left, right, (((1,), (0,)), ((), ())), preferred_element_type=F32)


def nt(left, right):
    return lax.dot_general(left, right, (((1,), (1,)), ((), ())), preferred_element_type=F32)


def tn(left, right):
    return lax.dot_general(left, right, (((0,), (0,)), ((), ())), preferred_element_type=F32)


def loop(count, body):
    lax.fori_loop(0, count, lambda i, c: (body(i), c)[1], 0)


def norm(rows):
    center = rows - jnp.mean(rows, axis=-1, keepdims=True)
    inv = lax.rsqrt(jnp.mean(center * center, axis=-1, keepdims=True) + EPSILON)
    return center * inv, inv


def norm_back(grad, normed, inv, gain):
    t = grad * gain
    inner = jnp.mean(t * normed, axis=-1, keepdims=True)
    return inv * (t - jnp.mean(t, axis=-1, keepdims=True) - normed * inner)


def colsum(x):
    return jnp.sum(x, axis=0, keepdims=True)


class Layer:
    def __init__(self, caps, slots, pad, refs):
        self.caps, self.slots, self.pad = caps, slots, pad
        self.rows = caps * pad
        self.__dict__.update(refs)

    def head_mask(self, h, rows):
        lane = lax.broadcasted_iota(jnp.int32, (rows, 256), 1)
        return (lane >= h * HD) & (lane < (h + 1) * HD)

    def stack(self, block):
        parts = []
        for h in range(4):
            parts.append(jnp.where(self.head_mask(h, self.pad), block, jnp.zeros_like(block)))
        return jnp.concatenate(parts, axis=0)

    def unstack(self, block):
        out = None
        for h in range(4):
            part = block[h * self.pad : (h + 1) * self.pad]
            out = part if out is None else jnp.where(self.head_mask(h, self.pad), part, out)
        return out

    def widen(self, src, base, dst):
        total = src.shape[0]
        tile = self.slots * 2 if total % (self.slots * 2) == 0 else self.slots
        tile = 176 if total % 176 == 0 else total
        def conv(i):
            r = pl.ds(pl.multiple_of(i * tile, 16), tile)
            self.stage[r, :] = src[r, :].astype(F32)
        loop(total // tile, conv)
        self.stage[total : total + 16, :] = jnp.zeros((16, self.stage.shape[1]), F32)
        for c in range(self.caps):
            off = c * self.slots
            low = off // 8 * 8
            v = self.stage[pl.ds(pl.multiple_of(base + low, 8), self.pad + 8), :]
            v = v[off - low : off - low + self.pad]
            row = lax.broadcasted_iota(jnp.int32, v.shape, 0)
            v = jnp.where(row < self.slots, v, 0.0)
            dst[c * self.pad : (c + 1) * self.pad, :] = v.astype(BF16)

    def crows(self, c):
        return pl.ds(pl.multiple_of(c * self.pad, self.pad), self.pad)

    def norm_one(self):
        gain, shift = self.gains[0:1, :].astype(F32), self.shifts[0:1, :].astype(F32)
        def cap(c):
            r = self.crows(c)
            n, inv = norm(self.xs[r, :].astype(F32))
            self.n1[r, :] = n
            self.r1[r, :] = jnp.broadcast_to(inv, (self.pad, 128))
            self.a1[r, :] = (n * gain + shift).astype(BF16)
        loop(self.caps, cap)

    def biases(self, s, qvb, ub):
        for j in range(3):
            if j == 1:
                self.bias_qkv[s * 3 + j] = jnp.zeros((1, 256), F32)
            else:
                self.bias_qkv[s * 3 + j] = qvb[j // 2 : j // 2 + 1, :].astype(F32)
        up = ub[...].astype(F32).reshape(1, -1)
        for n in range(4):
            self.bias_up[s * 4 + n] = up[:, n * 256 : (n + 1) * 256]

    def qkv(self, i):
        s, j = i // 3, lax.rem(i, 3)
        out = nn(self.a1[...], self.w[s * UNITS + j]) + self.bias_qkv[i]
        self.pqkv[i] = out.astype(BF16)

    def attention(self, i):
        s, c = i // self.caps, lax.rem(i, self.caps)
        r = self.crows(c)
        q = self.pqkv[s * 3, r, :]
        km = self.stack(self.pqkv[s * 3 + 1, r, :])
        vm = self.stack(self.pqkv[s * 3 + 2, r, :])
        st = nt(km, q)
        length = self.lengths[self.cap_base + c]
        jj = lax.broadcasted_iota(jnp.int32, (self.pad, self.pad), 0)
        ii = lax.broadcasted_iota(jnp.int32, (self.pad, self.pad), 1)
        allowed = (jj <= ii) & (jj < length)
        blocks = []
        for h in range(4):
            blk = jnp.where(allowed, st[h * self.pad : (h + 1) * self.pad], -1e30)
            top = jnp.max(blk, axis=0, keepdims=True)
            e = jnp.exp2((blk - top) * (HD**-0.5 * LOG2E))
            blocks.append(e * (1.0 / jnp.sum(e, axis=0, keepdims=True)))
        p = jnp.concatenate(blocks, axis=0)
        self.probs[i] = p
        self.ctx[s, r, :] = tn(p.astype(BF16), vm).astype(BF16)

    def attention_back(self, i):
        s, c = i // self.caps, lax.rem(i, self.caps)
        r = self.crows(c)
        q = self.pqkv[s * 3, r, :]
        k = self.pqkv[s * 3 + 1, r, :]
        v = self.pqkv[s * 3 + 2, r, :]
        d = self.ctx[s, r, :]
        p = self.probs[i]
        self.dqkv[s * 3 + 2, r, :] = self.unstack(nn(p.astype(BF16), d)).astype(BF16)
        dp = nt(self.stack(v), d)
        blocks = []
        for h in range(4):
            rr = slice(h * self.pad, (h + 1) * self.pad)
            blocks.append(p[rr] * (dp[rr] - jnp.sum(dp[rr] * p[rr], axis=0, keepdims=True)))
        ds = jnp.concatenate(blocks, axis=0).astype(BF16)
        self.dqkv[s * 3 + 1, r, :] = (self.unstack(nn(ds, q)) * HD**-0.5).astype(BF16)
        self.dqkv[s * 3, r, :] = (tn(ds, self.stack(k)) * HD**-0.5).astype(BF16)

    def project(self, i):
        tile = self.rows // 4
        r = pl.ds(pl.multiple_of(i * tile, 16), tile)
        gain, shift = self.gains[1:2, :].astype(F32), self.shifts[1:2, :].astype(F32)
        c0, c1 = self.ctx[0, r, :], self.ctx[1, r, :]
        halves = []
        for n in range(2):
            w = slice(n * 256, (n + 1) * 256)
            halves.append(nn(c0, self.w[3, w, :]) + nn(c1, self.w[UNITS + 3, w, :]))
        o = jnp.concatenate(halves, axis=1)
        h1 = self.xs[r, :].astype(F32) + o + self.ob[...].astype(F32).reshape(1, -1)
        self.h1[r, :] = h1
        n, inv = norm(h1)
        self.n2[r, :] = n
        self.r2[r, :] = jnp.broadcast_to(inv, (tile, 128))
        self.a2[r, :] = (n * gain + shift).astype(BF16)

    def wup(self, m):
        return (m // 4) * UNITS + 4 + lax.rem(m, 4)

    def wdown(self, m):
        return (m // 4) * UNITS + 8 + lax.rem(m, 4)

    def up(self, m):
        u = nn(self.a2[...], self.w[self.wup(m)]) + self.bias_up[m]
        sg = 0.5 * jnp.tanh(0.851 * u) + 0.5
        h = u * sg
        self.hid[m] = h.astype(BF16)
        self.act[m] = sg + 1.702 * h * (1.0 - sg)

    def down_grad(self, m):
        w = tn(self.hid[m], self.g[...]).astype(BF16)
        s, n = m // 4, lax.rem(m, 4)
        self.grads[n, s, 0:256, :] = w[:, :256]
        self.grads[n, s, 256:512, :] = w[:, 256:]

    def hidden_back(self, m):
        w = self.wdown(m)
        back = nt(self.g[:, 0:256], self.w[w, 0:256, :]) + nt(self.g[:, 256:512], self.w[w, 256:512, :])
        du = (back * self.act[m]).astype(BF16)
        self.du[m] = du
        self.small_up[m] = colsum(du.astype(F32))

    def up_grad(self, m):
        s, n = m // 4, lax.rem(m, 4)
        self.grads[4 + n, s] = tn(self.a2[...], self.du[m]).astype(BF16)

    def half_tile(self, i):
        tile = self.rows // 2
        r = pl.ds(pl.multiple_of((i // 2) * tile, 16), tile)
        return r, lax.rem(i, 2)

    def second_grad(self, i):
        r, n = self.half_tile(i)
        w = pl.ds(pl.multiple_of(n * 256, 256), 256)
        acc = None
        for m in range(8):
            part = nt(self.du[m, r, :], self.w[(m // 4) * UNITS + 4 + m % 4, w, :])
            acc = part if acc is None else acc + part
        self.e[r, w] = acc

    def mlp_out(self, i):
        r, n = self.half_tile(i)
        w = pl.ds(pl.multiple_of(n * 256, 256), 256)
        acc = self.h1[r, w] + self.db[w].astype(F32).reshape(1, -1)
        for m in range(8):
            acc = acc + nn(self.hid[m, r, :], self.w[(m // 4) * UNITS + 8 + m % 4, w, :])
        self.h1[r, w] = acc

    def norm_two_back(self):
        gain = self.gains[1:2, :].astype(F32)
        zero = jnp.zeros((1, gain.shape[1]), F32)
        def cap(c, carry):
            gg, sg, ob, db = carry
            r = self.crows(c)
            e, n, g = self.e[r, :], self.n2[r, :], self.g[r, :].astype(F32)
            dh = g + norm_back(e, n, self.r2[r, 0:1], gain)
            self.n2[r, :] = dh
            dob = dh.astype(BF16)
            self.dob[r, :] = dob
            return (gg + colsum(e * n), sg + colsum(e), ob + colsum(dob.astype(F32)), db + colsum(g))
        gg, sg, ob, db = lax.fori_loop(0, self.caps, cap, (zero, zero, zero, zero))
        self.small[1:2, :], self.small[3:4, :], self.small[4:5, :], self.small[5:6, :] = gg, sg, ob, db

    def out_back(self, s):
        w = tn(self.ctx[s], self.dob[...]).astype(BF16)
        self.grads[8, s, 0:256, :] = w[:, :256]
        self.grads[8, s, 256:512, :] = w[:, 256:]
        wo = s * UNITS + 3
        back = nt(self.dob[:, 0:256], self.w[wo, 0:256, :]) + nt(self.dob[:, 256:512], self.w[wo, 256:512, :])
        self.ctx[s] = back.astype(BF16)

    def qkv_grad(self, i):
        s, j = i // 3, lax.rem(i, 3)
        d = self.dqkv[i]
        self.grads[9 + j, s] = tn(self.a1[...], d).astype(BF16)
        self.small_qkv[i] = colsum(d.astype(F32))

    def first_grad(self, i):
        r, n = self.half_tile(i)
        w = pl.ds(pl.multiple_of(n * 256, 256), 256)
        acc = None
        for m in range(6):
            part = nt(self.dqkv[m, r, :], self.w[(m // 3) * UNITS + m % 3, w, :])
            acc = part if acc is None else acc + part
        self.e[r, w] = acc

    def norm_one_back(self, out):
        gain = self.gains[0:1, :].astype(F32)
        zero = jnp.zeros((1, gain.shape[1]), F32)
        gg, sg = zero, zero
        for c in range(self.caps):
            r = slice(c * self.pad, (c + 1) * self.pad)
            e, n = self.e[r, :], self.n1[r, :]
            dx = self.n2[r, :] + norm_back(e, n, self.r1[r, 0:1], gain)
            out[c * self.slots : (c + 1) * self.slots, :] = dx[: self.slots]
            gg, sg = gg + colsum(e * n), sg + colsum(e)
        self.small[0:1, :], self.small[2:3, :] = gg, sg

    def layer_out(self, flat, out):
        for c in range(self.caps):
            flat[c * self.slots : (c + 1) * self.slots, :] = self.h1[c * self.pad : c * self.pad + self.slots, :]
        out[...] = flat[0 : self.caps * self.slots, :].astype(BF16)

    def pack_small(self, out):
        def put(slot, row, value):
            for i in range(value.shape[1] // 128):
                out[slot, row + i : row + i + 1, :] = value[:, i * 128 : (i + 1) * 128]
        for slot in range(2):
            out[slot] = jnp.zeros(out.shape[1:], F32)
            put(slot, 0, self.small_qkv[slot * 3])
            put(slot, 2, self.small_qkv[slot * 3 + 2])
            for n in range(4):
                put(slot, 4 + 2 * n, self.small_up[slot * 4 + n])
            for i, k in enumerate((4, 5, 0, 1, 2, 3)):
                put(slot, 12 + 4 * i, self.small[k : k + 1, :])


class Peers:
    def __init__(self):
        dp, t = lax.axis_index("dp"), lax.axis_index("tensor")
        depth = lax.axis_size("dp") // 4
        self.core = lax.rem(dp, 2)
        self.x = lax.rem(dp // 2, 2)
        self.z = dp // 4
        self.t = t
        self.to_y = (dp, 1 - t)
        self.to_x = (dp + 2 - 4 * self.x, t)
        self.to_core = (dp + 1 - 2 * self.core, t)
        self.depth = depth
        self.to_z = [(lax.rem(self.z + k, depth) * 4 + lax.rem(dp, 4), t) for k in range(1, depth)]
        self.z_of = [lax.rem(self.z + k, depth) for k in range(1, depth)]

    def all(self):
        return [self.to_y, self.to_x, self.to_core] + self.to_z

    def greet(self):
        barrier = pltpu.get_barrier_semaphore()
        for peer in self.all():
            pl.semaphore_signal(barrier, inc=1, device_id=peer, device_id_type=MESH)

    def meet(self):
        pl.semaphore_wait(pltpu.get_barrier_semaphore(), len(self.all()))


def rows(index, size):
    return pl.ds(pl.multiple_of(index * size, size), size)


def remote(src, dst, send, recv, peer):
    return pltpu.make_async_remote_copy(src_ref=src, dst_ref=dst, send_sem=send, recv_sem=recv, device_id=peer, device_id_type=MESH)


class Weights:
    def __init__(self, peers, w, send, recv):
        self.p, self.w, self.send, self.recv = peers, w, send, recv
        self.quarter = peers.core * 2 + peers.x
        self.size = w.shape[1] // 4

    def y(self, u):
        r = rows(self.quarter, self.size)
        return remote(self.w.at[u, r], self.w.at[UNITS + u, r], self.send.at[u, 0], self.recv.at[u, 0], self.p.to_y)

    def x(self, u):
        part = self.w.at[UNITS + u, rows(self.quarter, self.size)]
        return remote(part, part, self.send.at[u, 1], self.recv.at[u, 1], self.p.to_x)

    def c(self, u):
        part = self.w.at[UNITS + u, rows(self.p.core, self.size * 2)]
        return remote(part, part, self.send.at[u, 2], self.recv.at[u, 2], self.p.to_core)

    def relay_x(self, u):
        self.y(u).wait_recv()
        self.x(u).start()

    def relay_c(self, u):
        self.x(u).wait_recv()
        self.c(u).start()

    def ready(self, u):
        self.c(u).wait_recv()

    def drain(self, u):
        self.y(u).wait_send()
        self.x(u).wait_send()
        self.c(u).wait_send()


class Reduce:
    def __init__(self, peers, refs, sem0, send, recv):
        self.p = peers
        self.g, self.cr, self.yr, self.xr, self.zr, self.f = refs
        self.sem0, self.send, self.recv = sem0, send, recv
        self.count = self.g.shape[0]
        self.full = self.g.shape[2]
        self.half, self.quarter = self.full // 2, self.full // 4
        self.shard = self.quarter // peers.depth

    def sems(self, n, k):
        return self.send.at[self.sem0 + n, k], self.recv.at[self.sem0 + n, k]

    def c(self, n):
        return remote(self.g.at[n, :, rows(1 - self.p.core, self.half)], self.cr.at[n], *self.sems(n, 0), self.p.to_core)

    def y(self, n):
        return remote(self.cr.at[n, 1], self.yr.at[n], *self.sems(n, 1), self.p.to_y)

    def x(self, n):
        return remote(self.cr.at[n, 0, rows(1 - self.p.x, self.quarter)], self.xr.at[n], *self.sems(n, 2), self.p.to_x)

    def z(self, n):
        return [
            remote(
                self.cr.at[n, 0, pl.ds(pl.multiple_of(self.p.x * self.quarter + self.p.z_of[k] * self.shard, self.shard), self.shard)],
                self.zr.at[n, k],
                *self.sems(n, 5 + k),
                self.p.to_z[k],
            )
            for k in range(self.p.depth - 1)
        ]

    def own_shard(self):
        p = self.p
        return pl.ds(pl.multiple_of(p.core * self.half + p.x * self.quarter + p.z * self.shard, self.shard), self.shard)

    def za(self, n):
        part = self.f.at[n, self.own_shard()]
        return [
            remote(part, part, *self.sems(n, 4 + self.p.depth + k), self.p.to_z[k]) for k in range(self.p.depth - 1)
        ]

    def xa(self, n):
        part = self.f.at[n, pl.ds(pl.multiple_of(self.p.core * self.half + self.p.x * self.quarter, self.quarter), self.quarter)]
        return remote(part, part, *self.sems(n, 3), self.p.to_x)

    def ca(self, n):
        part = self.f.at[n, rows(self.p.core, self.half)]
        return remote(part, part, *self.sems(n, 4), self.p.to_core)

    def c_start(self, n):
        self.c(n).start()

    def c_done(self, n):
        self.c(n).wait_recv()
        self.cr[n] = self.cr[n] + self.g[n, :, rows(self.p.core, self.half), :]
        self.y(n).start()

    def y_done(self, n):
        self.y(n).wait_recv()
        self.cr[n, 0] = self.cr[n, 0] + self.yr[n]
        self.x(n).start()

    def x_done(self, n):
        self.x(n).wait_recv()
        r = rows(self.p.x, self.quarter)
        self.cr[n, 0, r, :] = self.cr[n, 0, r, :] + self.xr[n]
        for copy in self.z(n):
            copy.start()

    def z_done(self, n):
        for copy in self.z(n):
            copy.wait_recv()
        mine = pl.ds(pl.multiple_of(self.p.x * self.quarter + self.p.z * self.shard, self.shard), self.shard)
        total = self.cr[n, 0, mine, :].astype(F32)
        for k in range(self.p.depth - 1):
            total = total + self.zr[n, k].astype(F32)
        self.f[n, self.own_shard(), :] = total.astype(self.f.dtype)
        for copy in self.za(n):
            copy.start()

    def za_done(self, n):
        for copy in self.za(n):
            copy.wait_recv()
        self.xa(n).start()

    def xa_done(self, n):
        self.xa(n).wait_recv()
        self.ca(n).start()

    def ca_done(self, n):
        self.ca(n).wait_recv()

    def drain(self, n):
        for copy in [self.c(n), self.y(n), self.x(n), self.xa(n), self.ca(n)] + self.z(n) + self.za(n):
            copy.wait_send()


def when(condition, body):
    if isinstance(condition, bool):
        if condition:
            body()
    else:
        pl.when(condition)(body)


ON_WEIGHTS = ("relay_x", "relay_c", "ready")
ON_GRADS = ("c_start", "c_done", "y_done", "x_done", "z_done", "za_done", "xa_done", "ca_done")
PLAN = {
    "norm_one": (),
    "qkv_own": (),
    "att_own": ((1, 0, (0,)), ),
    "widen_g": ((0, 0, (1,)), ),
    "qkv_other": ((0, 0, (2, 100, 3, 200,)), (1, 0, (101, 4, 201,)), (2, 0, (102, 5, 202,)), ),
    "att_other": ((0, 0, (103,)), (1, 0, (104, 6,)), ),
    "proj": ((0, 0, (105, 7, 8, 203,)), ),
    "updown": ((0, 0, (9, 106,)), (0, 1, (204,)), (0, 3, (10,)), (1, 0, (1000, 107,)), (1, 1, (205,)), (1, 2, (11,)), (1, 3, (108, 1100,)), (2, 0, (1001,)), (2, 1, (206,)), (2, 2, (109,)), (2, 3, (1101,)), (3, 0, (1002,)), (3, 1, (110, 207,)), ),
    "hbug": ((0, 0, (1003, 111, 1102,)), (0, 1, (1200, 208,)), (1, 0, (1004,)), (1, 1, (209,)), (1, 2, (1103,)), (1, 3, (1201,)), (2, 0, (1005, 1300,)), (2, 1, (210,)), (3, 0, (1006, 1202, 1104,)), (3, 1, (211,)), (3, 2, (1301,)), ),
    "sg": ((0, 0, (1007, 1400,)), (1, 0, (1105, 1203,)), (2, 0, (1302,)), ),
    "ntb": (),
    "ob": ((0, 0, (1401, 1204, 1303, 1500, 1106,)), ),
    "ab": ((0, 0, (1008,)), (1, 0, (1402, 1205, 1107,)), (2, 0, (1501, 1304,)), (3, 0, (1600, 1403, 1206, 1108,)), ),
    "qg": ((0, 0, (1700, 1502, 1305,)), (1, 0, (1009, 1601, 1404, 1207,)), (2, 0, (1010, 1306, 1109, 1503,)), (2, 1, (1701,)), ),
    "fg": ((0, 0, (1011,)), (1, 0, (1602, 1208, 1405, 1110,)), (3, 0, (1702, 1307,)), ),
    "nob": ((0, 0, (1504,)), ),
    "mo": ((0, 0, (1012, 1603,)), (1, 0, (1406, 1209, 1111,)), (2, 0, (1703, 1308,)), (3, 0, (1505,)), ),
    "lo": (),
    "tail": ((0, 0, (1604, 1112, 1407, 1210, 1704, 1309, 1506, 1605, 1408, 1211, 1705, 1212, 1310, 1507, 1606, 1409, 1706, 1311, 1508, 1312, 1607, 1410, 1707, 1509, 1608, 1411, 1708, 1412, 1510, 1609, 1709, 1511, 1512, 1610, 1710, 1611, 1612, 1711, 1712,)), ),
}


def kernel(caps, slots, pad, names_in, *all_refs):
    L = Layer(caps, slots, pad, dict(zip(names_in, all_refs)))
    peers = Peers()
    peers.greet()
    L.cap_base = peers.t * caps
    weights = Weights(peers, L.w, L.wsend, L.wrecv)
    big = Reduce(peers, (L.grads, L.cr, L.yr, L.xr, L.zr, L.f), 0, L.gsend, L.grecv)
    small = Reduce(peers, (L.sg, L.scr, L.syr, L.sxr, L.szr, L.sf), UNITS, L.gsend, L.grecv)

    def arrive(codes):
        for code in codes:
            stage, unit = code // 100, code % 100
            if stage < 10:
                getattr(weights, ON_WEIGHTS[stage])(unit)
            elif unit == UNITS:
                getattr(small, ON_GRADS[stage - 10])(0)
            else:
                getattr(big, ON_GRADS[stage - 10])(unit)

    def run(name, count, *parts):
        def body(i):
            for k, part in enumerate(parts):
                for when_i, when_k, codes in PLAN[name]:
                    if when_k == k:
                        when(i == when_i, functools.partial(arrive, codes))
                part(i)

        if count == 1:
            body(0)
        else:
            loop(count, body)

    local = []

    def load(a, b):
        copy = pltpu.make_async_copy(a, b, L.lsem.at[len(local)])
        copy.start()
        local.append(copy)

    load(L.tok, L.tok_v)
    for j in range(3):
        load(L.wqkv_a.at[j], L.w.at[j])
    for n in range(2):
        load(L.wo_a.at[:, pl.ds(n * 256, 256)], L.w.at[3, pl.ds(n * 256, 256)])
    for n in range(4):
        load(L.wu_a.at[:, pl.ds(n * 256, 256)], L.w.at[4 + n])
    for n in range(4):
        for k in range(2):
            load(L.wd_a.at[pl.ds(n * 256, 256), pl.ds(k * 256, 256)], L.w.at[8 + n, pl.ds(k * 256, 256)])
    load(L.cot, L.cot_v)
    local[0].wait()
    L.widen(L.tok_v, peers.t * caps * slots, L.xs)
    for copy in local[1:]:
        copy.wait()
    peers.meet()
    bias_send = [
        remote(L.qvb, L.qvb_b, L.bsem.at[0], L.bsem.at[1], peers.to_y),
        remote(L.ub, L.ub_b, L.bsem.at[2], L.bsem.at[3], peers.to_y),
    ]
    for copy in bias_send:
        copy.start()
    loop(UNITS, lambda u: weights.y(u).start())
    attend = lambda i: [L.attention(4 * i + k) for k in range(4)]

    def rows_and_biases():
        L.widen(L.cot_v, peers.t * caps * slots, L.g)
        for copy in bias_send:
            copy.wait()
        L.biases(1, L.qvb_b, L.ub_b)

    def input_rows():
        L.norm_one_back(L.dx_out)
        L.pack_small(L.sg.at[0])

    def output_rows():
        L.layer_out(L.stage, L.y_out)

    run("norm_one", 1, lambda i: (L.norm_one(), L.biases(0, L.qvb, L.ub)))
    run("qkv_own", 3, L.qkv)
    run("att_own", caps // 4, attend)
    run("widen_g", 1, lambda i: rows_and_biases())
    run("qkv_other", 3, lambda j: L.qkv(3 + j))
    run("att_other", caps // 4, lambda i: attend(caps // 4 + i))
    run("proj", 4, L.project)
    run("updown", 4, L.up, lambda n: L.up(4 + n), L.down_grad, lambda n: L.down_grad(4 + n))
    run("hbug", 4, L.hidden_back, lambda n: L.hidden_back(4 + n), L.up_grad, lambda n: L.up_grad(4 + n))
    run("sg", 4, L.second_grad)
    run("ntb", 1, lambda i: L.norm_two_back())
    run("ob", 2, L.out_back)
    run("ab", caps // 2, lambda i: [L.attention_back(4 * i + k) for k in range(4)])
    run("qg", 3, L.qkv_grad, lambda j: L.qkv_grad(3 + j))
    run("fg", 4, L.first_grad)
    run("nob", 1, lambda i: input_rows())
    run("mo", 4, L.mlp_out)
    run("lo", 1, lambda i: output_rows())
    run("tail", 1, lambda i: None)

    def drain(n):
        weights.drain(n)
        big.drain(n)

    loop(UNITS, drain)
    small.drain(0)


def finish(f, s, y, dx, y_out, dx_out, qkv, out, up, down, qvb, ob, ub, db, gg, sh, wide, sem_out, sem_io):
    io = [pltpu.make_async_copy(y, y_out, sem_io.at[0]), pltpu.make_async_copy(dx, dx_out, sem_io.at[1])]
    for copy in io:
        copy.start()
    for n in range(UNITS):
        wide[n] = f[n].astype(F32)
        if n < 4 or n == 8:
            parts = []
            for k in range(2):
                c = pl.ds(k * 256, 256)
                dst = down.at[pl.ds(n * 256, 256), c] if n < 4 else out.at[:, c]
                parts.append((wide.at[n, c], dst))
        elif n < 8:
            parts = [(wide.at[n], up.at[:, pl.ds((n - 4) * 256, 256)])]
        else:
            parts = [(wide.at[n], qkv.at[n - 9])]
        for k, (a, b) in enumerate(parts):
            copy = pltpu.make_async_copy(a, b, sem_out.at[2 * n + k])
            copy.start()
            io.append(copy)

    def row(first, count):
        return jnp.concatenate([s[0, first + i : first + i + 1, :] for i in range(count)], axis=1)

    qvb[0:1, :], qvb[1:2, :] = row(0, 2), row(2, 2)
    ub[...] = row(4, 8)
    ob[...], db[...] = row(12, 4), row(16, 4)
    gg[0:1, :], gg[1:2, :] = row(20, 4), row(24, 4)
    sh[0:1, :], sh[1:2, :] = row(28, 4), row(32, 4)
    for copy in io:
        copy.wait()


def shards(depth, tokens, lengths, qkv_weight, qv_bias, out_weight, out_bias, up_weight, up_bias, down_weight, down_bias, norm_gain, norm_shift, cotangent):
    total, width = tokens.shape
    count = lengths.shape[0]
    slots = total // count
    caps = count // 2
    pad = (slots + 15) // 16 * 16
    rws = caps * pad
    V = pl.BlockSpec(memory_space=pltpu.VMEM)
    A = pl.BlockSpec(memory_space=pl.ANY)
    S = pl.BlockSpec(memory_space=pltpu.SMEM)
    ins = [
        ("tok", tokens, A), ("cot", cotangent, A), ("lengths", lengths, S),
        ("wqkv_a", qkv_weight, A), ("wo_a", out_weight, A), ("wu_a", up_weight, A), ("wd_a", down_weight, A),
        ("qvb", qv_bias, V), ("ub", up_bias, V),
        ("ob", out_bias, V), ("db", down_bias, V), ("gains", norm_gain, V), ("shifts", norm_shift, V),
    ]
    outs = [
        ("y_out", (caps * slots, 512), BF16), ("dx_out", (caps * slots, 512), F32),
        ("f", (UNITS, 512, 256), BF16), ("sf", (1, 128, 128), F32),
    ]
    vm = pltpu.VMEM
    sems = UNITS + 1, 3 + 2 * depth
    scr = [
        ("tok_v", vm((total, 512), BF16)), ("cot_v", vm((total, 512), BF16)),
        ("stage", vm((total + 16, 512), F32)), ("xs", vm((rws, 512), BF16)), ("g", vm((rws, 512), BF16)),
        ("n1", vm((rws, 512), F32)), ("r1", vm((rws, 128), F32)), ("a1", vm((rws, 512), BF16)),
        ("w", vm((2 * UNITS, 512, 256), BF16)), ("qvb_b", vm((2, 256), BF16)), ("ub_b", vm(up_bias.shape, BF16)),
        ("bias_qkv", vm((6, 1, 256), F32)), ("bias_up", vm((8, 1, 256), F32)),
        ("pqkv", vm((6, rws, 256), BF16)), ("probs", vm((2 * caps, 4 * pad, pad), F32)), ("ctx", vm((2, rws, 256), BF16)),
        ("h1", vm((rws, 512), F32)), ("n2", vm((rws, 512), F32)), ("r2", vm((rws, 128), F32)), ("a2", vm((rws, 512), BF16)),
        ("hid", vm((8, rws, 256), BF16)), ("act", vm((8, rws, 256), F32)), ("du", vm((8, rws, 256), BF16)),
        ("e", vm((rws, 512), F32)), ("dob", vm((rws, 512), BF16)),
        ("dqkv", vm((6, rws, 256), BF16)),
        ("small", vm((8, 512), F32)), ("small_up", vm((8, 1, 256), F32)), ("small_qkv", vm((6, 1, 256), F32)),
        ("grads", vm((UNITS, 2, 512, 256), BF16)), ("cr", vm((UNITS, 2, 256, 256), BF16)), ("yr", vm((UNITS, 256, 256), BF16)),
        ("xr", vm((UNITS, 128, 256), BF16)), ("zr", vm((UNITS, depth - 1, 128 // depth, 256), BF16)),
        ("sg", vm((1, 2, 128, 128), F32)), ("scr", vm((1, 2, 64, 128), F32)), ("syr", vm((1, 64, 128), F32)),
        ("sxr", vm((1, 32, 128), F32)), ("szr", vm((1, depth - 1, 32 // depth, 128), F32)),
        ("lsem", pltpu.SemaphoreType.DMA((20,))), ("bsem", pltpu.SemaphoreType.DMA((4,))),
        ("wsend", pltpu.SemaphoreType.DMA((UNITS, 3))), ("wrecv", pltpu.SemaphoreType.DMA((UNITS, 3))),
        ("gsend", pltpu.SemaphoreType.DMA(sems)), ("grecv", pltpu.SemaphoreType.DMA(sems)),
    ]
    names = [n for n, _, _ in ins] + [n for n, _, _ in outs] + [n for n, _ in scr]
    y, dx, f, s = pl.pallas_call(
        functools.partial(kernel, caps, slots, pad, names),
        out_shape=[vm(s, d) for _, s, d in outs],
        in_specs=[s for _, _, s in ins],
        out_specs=[V] * len(outs),
        scratch_shapes=[s for _, s in scr],
        compiler_params=pltpu.CompilerParams(vmem_limit_bytes=VLIM, collective_id=0, has_side_effects=True),
        name="layer",
    )(*[v for _, v, _ in ins])
    results = [
        (y.shape, BF16, A), (dx.shape, F32, A), (qkv_weight.shape, F32, A), (out_weight.shape, F32, A),
        (up_weight.shape, F32, A), (down_weight.shape, F32, A),
        (qv_bias.shape, F32, V), ((1, 512), F32, V), ((1, up_bias.shape[0]), F32, V), ((1, 512), F32, V), ((2, 512), F32, V), ((2, 512), F32, V),
    ]
    y, dx, qkv, out, up, down, qvb, ob, ub, db, gg, sh = pl.pallas_call(
        finish,
        out_shape=[jax.ShapeDtypeStruct(s, d) for s, d, _ in results],
        in_specs=[V, V, V, V],
        out_specs=[s for _, _, s in results],
        scratch_shapes=[
            vm((UNITS, 512, 256), F32), pltpu.SemaphoreType.DMA((2 * UNITS,)), pltpu.SemaphoreType.DMA((2,)),
        ],
        compiler_params=pltpu.CompilerParams(vmem_limit_bytes=12 << 20),
        name="finish",
    )(*[pltpu.with_memory_space_constraint(v, pltpu.VMEM) for v in (f, s, y, dx)])
    return y, dx, qkv, qvb, out, ob[0], up, ub[0], down, db[0], gg, sh


def matmul_plain(left, right):
    return jnp.dot(left, right, preferred_element_type=jnp.float32)


def contract_rows(left, right):
    return lax.dot_general(
        left, right, (((0,), (0,)), ((), ())), preferred_element_type=jnp.float32
    )


def contract_cols(left, right):
    return lax.dot_general(
        left, right, (((1,), (1,)), ((), ())), preferred_element_type=jnp.float32
    )


def plain_norm_stats(values):
    center = values - jnp.mean(values, axis=-1, keepdims=True)
    inv_std = lax.rsqrt(jnp.mean(center * center, axis=-1, keepdims=True) + EPSILON)
    return (center * inv_std, inv_std)


def plain_norm_back(upstream, normed, inv_std, gain_vec):
    scaled = upstream * gain_vec
    inner_mean = jnp.mean(scaled * normed, axis=-1, keepdims=True)
    result = inv_std * (scaled - jnp.mean(scaled, axis=-1, keepdims=True) - normed * inner_mean)
    return (result, jnp.sum(upstream * normed, axis=0), jnp.sum(upstream, axis=0))


def row_slice(values, row_start, share_rows):
    return lax.dynamic_slice_in_dim(values, row_start, share_rows, 0)


def shards_by_heads(
    tokens,
    lengths,
    qkv_weight,
    qv_bias,
    out_weight,
    out_bias,
    up_weight,
    up_bias,
    down_weight,
    down_bias,
    norm_gain,
    norm_shift,
    cotangent,
):
    tensor_count = lax.axis_size("tensor")
    tensor_index = lax.axis_index("tensor")
    share_rows = tokens.shape[0] // tensor_count
    row_start = tensor_index * share_rows
    gains = norm_gain.astype(jnp.float32)
    shifts = norm_shift.astype(jnp.float32)
    total_rows = tokens.shape[0]
    count = lengths.shape[0]
    slots = total_rows // count
    local_width = qkv_weight.shape[2]
    local_heads = local_width // HD
    score_scale = HD ** (-0.5)
    qv_float = qv_bias.astype(jnp.float32)
    token_f = tokens.astype(jnp.float32)
    normed_one, inv_one = plain_norm_stats(token_f)
    first_in = (normed_one * gains[0] + shifts[0]).astype(jnp.bfloat16)
    queries = (matmul_plain(first_in, qkv_weight[0]) + qv_float[0]).astype(jnp.bfloat16)
    keys_all = matmul_plain(first_in, qkv_weight[1]).astype(jnp.bfloat16)
    values_all = (matmul_plain(first_in, qkv_weight[2]) + qv_float[1]).astype(jnp.bfloat16)
    shape4 = (count, slots, local_heads, HD)
    query_four = queries.reshape(shape4)
    key_four = keys_all.reshape(shape4)
    value_four = values_all.reshape(shape4)
    position = jnp.arange(slots)
    allowed = (position[None, :] <= position[:, None])[None, :, :] & (
        position[None, None, :] < lengths[:, None, None]
    )
    allowed = allowed[:, None, :, :]

    def masked_scores():
        raw = jnp.einsum(
            "cihd,cjhd->chij", query_four, key_four, preferred_element_type=jnp.float32
        )
        return jnp.where(allowed, raw * score_scale, -1e30)

    scores = masked_scores()
    row_max = jnp.max(scores, axis=-1, keepdims=True)
    log_total = row_max + jnp.log(jnp.sum(jnp.exp(scores - row_max), axis=-1, keepdims=True))
    probs_low = jnp.exp(scores - log_total).astype(jnp.bfloat16)
    context = jnp.einsum(
        "chij,cjhd->cihd", probs_low, value_four, preferred_element_type=jnp.float32
    )
    context = context.reshape(total_rows, local_width).astype(jnp.bfloat16)
    attn_part = matmul_plain(context, out_weight)
    attn_out = lax.psum(attn_part, "tensor") + out_bias.astype(jnp.float32)
    hidden_res = token_f + attn_out
    normed_two, inv_two = plain_norm_stats(hidden_res)
    second_in = (normed_two * gains[1] + shifts[1]).astype(jnp.bfloat16)
    upper = matmul_plain(second_in, up_weight) + up_bias.astype(jnp.float32)
    sigma = jax.nn.sigmoid(1.702 * upper)
    hidden = (upper * sigma).astype(jnp.bfloat16)
    mlp_part = matmul_plain(hidden, down_weight)
    result_rows = (
        hidden_res
        + lax.psum(mlp_part.astype(jnp.bfloat16), "tensor").astype(jnp.float32)
        + down_bias.astype(jnp.float32)
    )
    layer_out = row_slice(result_rows, row_start, share_rows).astype(jnp.bfloat16)
    grad_f = cotangent.astype(jnp.float32)
    down_grad = contract_rows(hidden, cotangent)
    down_bias_grad = jnp.sum(grad_f, axis=0)
    hidden_grad = contract_cols(cotangent, down_weight)
    upper_grad = (hidden_grad * (sigma + 1.702 * upper * sigma * (1.0 - sigma))).astype(
        jnp.bfloat16
    )
    up_grad = contract_rows(second_in, upper_grad)
    up_bias_grad = jnp.sum(upper_grad.astype(jnp.float32), axis=0)
    second_part = contract_cols(upper_grad, up_weight)
    second_grad = lax.psum(second_part, "tensor")
    residual_back, gain_two, shift_two = plain_norm_back(second_grad, normed_two, inv_two, gains[1])
    residual_full = grad_f + residual_back
    branch_grad = residual_full.astype(jnp.bfloat16)
    out_bias_grad = jnp.sum(branch_grad.astype(jnp.float32), axis=0)
    out_grad = contract_rows(context, branch_grad)
    context_grad = contract_cols(branch_grad, out_weight).astype(jnp.bfloat16).reshape(shape4)
    probs = jnp.exp(masked_scores() - log_total)
    probs_low = probs.astype(jnp.bfloat16)
    value_grad = jnp.einsum(
        "chij,cihd->cjhd", probs_low, context_grad, preferred_element_type=jnp.float32
    )
    prob_grad = jnp.einsum(
        "cihd,cjhd->chij", context_grad, value_four, preferred_element_type=jnp.float32
    )
    score_grad = probs * (prob_grad - jnp.sum(prob_grad * probs, axis=-1, keepdims=True))
    score_grad = score_grad.astype(jnp.bfloat16)
    query_grad = (
        jnp.einsum("chij,cjhd->cihd", score_grad, key_four, preferred_element_type=jnp.float32)
        * score_scale
    )
    key_grad = (
        jnp.einsum("chij,cihd->cjhd", score_grad, query_four, preferred_element_type=jnp.float32)
        * score_scale
    )
    query_grad = query_grad.reshape(total_rows, local_width).astype(jnp.bfloat16)
    key_grad = key_grad.reshape(total_rows, local_width).astype(jnp.bfloat16)
    value_grad = value_grad.reshape(total_rows, local_width).astype(jnp.bfloat16)
    qkv_grad = jnp.stack(
        [
            contract_rows(first_in, query_grad),
            contract_rows(first_in, key_grad),
            contract_rows(first_in, value_grad),
        ]
    )
    qv_bias_grad = jnp.stack(
        [
            jnp.sum(query_grad.astype(jnp.float32), axis=0),
            jnp.sum(value_grad.astype(jnp.float32), axis=0),
        ]
    )
    first_part = (
        contract_cols(query_grad, qkv_weight[0])
        + contract_cols(key_grad, qkv_weight[1])
        + contract_cols(value_grad, qkv_weight[2])
    )
    first_grad = lax.psum(first_part.astype(jnp.bfloat16), "tensor").astype(jnp.float32)
    input_back, gain_one, shift_one = plain_norm_back(first_grad, normed_one, inv_one, gains[0])
    input_grad = row_slice(residual_full + input_back, row_start, share_rows)
    gain_grads = jnp.stack([gain_one, gain_two])
    shift_grads = jnp.stack([shift_one, shift_two])
    summed = (
        lax.psum(qkv_grad.astype(jnp.bfloat16), "dp").astype(jnp.float32),
        lax.psum(qv_bias_grad.astype(jnp.bfloat16), "dp").astype(jnp.float32),
        lax.psum(out_grad.astype(jnp.bfloat16), "dp").astype(jnp.float32),
        lax.psum(out_bias_grad.astype(jnp.bfloat16), "dp").astype(jnp.float32),
        lax.psum(up_grad.astype(jnp.bfloat16), "dp").astype(jnp.float32),
        lax.psum(up_bias_grad.astype(jnp.bfloat16), "dp").astype(jnp.float32),
        lax.psum(down_grad.astype(jnp.bfloat16), "dp").astype(jnp.float32),
        lax.psum(down_bias_grad.astype(jnp.bfloat16), "dp").astype(jnp.float32),
        lax.psum(gain_grads.astype(jnp.bfloat16), "dp").astype(jnp.float32),
        lax.psum(shift_grads.astype(jnp.bfloat16), "dp").astype(jnp.float32),
    )
    return (
        layer_out,
        input_grad,
        summed[0],
        summed[1],
        summed[2],
        summed[3],
        summed[4],
        summed[5],
        summed[6],
        summed[7],
        summed[8],
        summed[9],
    )


def solution(mesh):
    dp, tensor = mesh.shape["dp"], mesh.shape["tensor"]
    if tensor == 2 and dp == 16:
        body = functools.partial(shards, dp // 4)
    else:
        body = shards_by_heads
    return jax.shard_map(
        body,
        mesh=mesh,
        in_specs=(P("dp", None), P("dp"), P(None, None, "tensor"), P(None, "tensor"), P("tensor", None), P(), P(None, "tensor"), P("tensor"), P("tensor", None), P(), P(), P(), P("dp", None)),
        out_specs=(P(("dp", "tensor"), None), P(("dp", "tensor"), None), P(None, None, "tensor"), P(None, "tensor"), P("tensor", None), P(), P(None, "tensor"), P("tensor"), P("tensor", None), P(), P(), P()),
        check_vma=False,
    )
```

```python
import functools

import jax
import jax.numpy as jnp
from jax import lax
from jax.experimental import pallas as pl
from jax.experimental.pallas import tpu as pltpu
from jax.sharding import PartitionSpec as P

HD = 64
EPSILON = 1e-05
F32 = jnp.float32
BF16 = jnp.bfloat16
LOG2E = 1.4426950408889634
UNITS = 12
BIG = 11
FINAL = 14
VLIM = 54 << 20
MESH = pl.DeviceIdType.MESH


def nn(left, right):
    return lax.dot_general(left, right, (((1,), (0,)), ((), ())), preferred_element_type=F32)


def nt(left, right):
    return lax.dot_general(left, right, (((1,), (1,)), ((), ())), preferred_element_type=F32)


def tn(left, right):
    return lax.dot_general(left, right, (((0,), (0,)), ((), ())), preferred_element_type=F32)


def loop(count, body):
    lax.fori_loop(0, count, lambda i, c: (body(i), c)[1], 0)


def norm(rows):
    center = rows - jnp.mean(rows, axis=-1, keepdims=True)
    inv = lax.rsqrt(jnp.mean(center * center, axis=-1, keepdims=True) + EPSILON)
    return center * inv, inv


def norm_back(grad, normed, inv, gain):
    t = grad * gain
    inner = jnp.mean(t * normed, axis=-1, keepdims=True)
    return inv * (t - jnp.mean(t, axis=-1, keepdims=True) - normed * inner)


def colsum(x):
    return jnp.sum(x, axis=0, keepdims=True)


class Layer:
    def __init__(self, caps, slots, pad, refs):
        self.caps, self.slots, self.pad = caps, slots, pad
        self.rows = caps * pad
        self.__dict__.update(refs)

    def head_mask(self, h, rows):
        lane = lax.broadcasted_iota(jnp.int32, (rows, 256), 1)
        return (lane >= h * HD) & (lane < (h + 1) * HD)

    def stack(self, block):
        parts = []
        for h in range(4):
            parts.append(jnp.where(self.head_mask(h, self.pad), block, jnp.zeros_like(block)))
        return jnp.concatenate(parts, axis=0)

    def unstack(self, block):
        out = None
        for h in range(4):
            part = block[h * self.pad : (h + 1) * self.pad]
            out = part if out is None else jnp.where(self.head_mask(h, self.pad), part, out)
        return out

    def widen(self, src, base, dst):
        total = src.shape[0]
        tile = self.slots * 2 if total % (self.slots * 2) == 0 else self.slots
        tile = 176 if total % 176 == 0 else total
        def conv(i):
            r = pl.ds(pl.multiple_of(i * tile, 16), tile)
            self.stage[r, :] = src[r, :].astype(F32)
        loop(total // tile, conv)
        self.stage[total : total + 16, :] = jnp.zeros((16, self.stage.shape[1]), F32)
        for c in range(self.caps):
            off = c * self.slots
            low = off // 8 * 8
            v = self.stage[pl.ds(pl.multiple_of(base + low, 8), self.pad + 8), :]
            v = v[off - low : off - low + self.pad]
            row = lax.broadcasted_iota(jnp.int32, v.shape, 0)
            v = jnp.where(row < self.slots, v, 0.0)
            dst[c * self.pad : (c + 1) * self.pad, :] = v.astype(BF16)

    def crows(self, c):
        return pl.ds(pl.multiple_of(c * self.pad, self.pad), self.pad)

    def norm_one(self):
        gain, shift = self.gains[0:1, :].astype(F32), self.shifts[0:1, :].astype(F32)
        def cap(c):
            r = self.crows(c)
            n, inv = norm(self.xs[r, :].astype(F32))
            self.n1[r, :] = n
            self.r1[r, :] = jnp.broadcast_to(inv, (self.pad, 128))
            self.a1[r, :] = (n * gain + shift).astype(BF16)
        loop(self.caps, cap)

    def biases(self, s, qvb, ub):
        for j in range(3):
            if j == 1:
                self.bias_qkv[s * 3 + j] = jnp.zeros((1, 256), F32)
            else:
                self.bias_qkv[s * 3 + j] = qvb[j // 2 : j // 2 + 1, :].astype(F32)
        up = ub[...].astype(F32).reshape(1, -1)
        for n in range(4):
            self.bias_up[s * 4 + n] = up[:, n * 256 : (n + 1) * 256]

    def qkv(self, i):
        s, j = i // 3, lax.rem(i, 3)
        out = nn(self.a1[...], self.w[s * UNITS + j]) + self.bias_qkv[i]
        self.pqkv[i] = out.astype(BF16)

    def attention(self, i):
        s, c = i // self.caps, lax.rem(i, self.caps)
        r = self.crows(c)
        q = self.pqkv[s * 3, r, :]
        km = self.stack(self.pqkv[s * 3 + 1, r, :])
        vm = self.stack(self.pqkv[s * 3 + 2, r, :])
        st = nt(km, q)
        length = self.lengths[self.cap_base + c]
        jj = lax.broadcasted_iota(jnp.int32, (self.pad, self.pad), 0)
        ii = lax.broadcasted_iota(jnp.int32, (self.pad, self.pad), 1)
        allowed = (jj <= ii) & (jj < length)
        blocks = []
        for h in range(4):
            blk = jnp.where(allowed, st[h * self.pad : (h + 1) * self.pad], -1e30)
            top = jnp.max(blk, axis=0, keepdims=True)
            e = jnp.exp2((blk - top) * (HD**-0.5 * LOG2E))
            blocks.append(e * (1.0 / jnp.sum(e, axis=0, keepdims=True)))
        p = jnp.concatenate(blocks, axis=0)
        self.probs[i] = p
        self.ctx[s, r, :] = tn(p.astype(BF16), vm).astype(BF16)

    def attention_back(self, i):
        s, c = i // self.caps, lax.rem(i, self.caps)
        r = self.crows(c)
        q = self.pqkv[s * 3, r, :]
        k = self.pqkv[s * 3 + 1, r, :]
        v = self.pqkv[s * 3 + 2, r, :]
        d = self.ctx[s, r, :]
        p = self.probs[i]
        self.dqkv[s * 3 + 2, r, :] = self.unstack(nn(p.astype(BF16), d)).astype(BF16)
        dp = nt(self.stack(v), d)
        blocks = []
        for h in range(4):
            rr = slice(h * self.pad, (h + 1) * self.pad)
            blocks.append(p[rr] * (dp[rr] - jnp.sum(dp[rr] * p[rr], axis=0, keepdims=True)))
        ds = jnp.concatenate(blocks, axis=0).astype(BF16)
        self.dqkv[s * 3 + 1, r, :] = (self.unstack(nn(ds, q)) * HD**-0.5).astype(BF16)
        self.dqkv[s * 3, r, :] = (tn(ds, self.stack(k)) * HD**-0.5).astype(BF16)

    def half_rows(self, i):
        tile = self.rows // 4
        return pl.ds(pl.multiple_of(i * tile, 16), tile)

    def out_product(self, slot, r):
        c = self.ctx[slot, r, :]
        return jnp.concatenate([nn(c, self.w[slot * UNITS + 3, k * 256 : (k + 1) * 256, :]) for k in range(2)], axis=1)

    def project_own(self, i):
        r = self.half_rows(i)
        self.h1[r, :] = self.xs[r, :].astype(F32) + self.out_product(0, r) + self.ob[...].astype(F32).reshape(1, -1)

    def project(self, i):
        r = self.half_rows(i)
        gain, shift = self.gains[1:2, :].astype(F32), self.shifts[1:2, :].astype(F32)
        h1 = self.h1[r, :] + self.out_product(1, r)
        self.h1[r, :] = h1
        n, inv = norm(h1)
        self.n2[r, :] = n
        self.r2[r, :] = jnp.broadcast_to(inv, (n.shape[0], 128))
        self.a2[r, :] = (n * gain + shift).astype(BF16)

    def wup(self, m):
        return (m // 4) * UNITS + 4 + lax.rem(m, 4)

    def wdown(self, m):
        return (m // 4) * UNITS + 8 + lax.rem(m, 4)

    def up(self, m):
        u = nn(self.a2[...], self.w[self.wup(m)]) + self.bias_up[m]
        sg = 0.5 * jnp.tanh(0.851 * u) + 0.5
        h = u * sg
        self.hid[m] = h.astype(BF16)
        self.act[m] = sg + 1.702 * h * (1.0 - sg)

    def down_grad(self, m):
        w = tn(self.hid[m], self.g[...]).astype(BF16)
        s, n = m // 4, lax.rem(m, 4)
        self.grads[n, s, 0:256, :] = w[:, :256]
        self.grads[n, s, 256:512, :] = w[:, 256:]

    def hidden_back(self, m):
        w = self.wdown(m)
        back = nt(self.g[:, 0:256], self.w[w, 0:256, :]) + nt(self.g[:, 256:512], self.w[w, 256:512, :])
        du = (back * self.act[m]).astype(BF16)
        self.du[m] = du
        self.small_up[m] = colsum(du.astype(F32))

    def up_grad(self, m):
        s, n = m // 4, lax.rem(m, 4)
        self.grads[4 + n, s] = tn(self.a2[...], self.du[m]).astype(BF16)

    def half_tile(self, i):
        tile = self.rows // 2
        r = pl.ds(pl.multiple_of((i // 2) * tile, 16), tile)
        return r, lax.rem(i, 2)

    def second_grad(self, i):
        r, n = self.half_tile(i)
        w = pl.ds(pl.multiple_of(n * 256, 256), 256)
        acc = None
        for m in range(8):
            part = nt(self.du[m, r, :], self.w[(m // 4) * UNITS + 4 + m % 4, w, :])
            acc = part if acc is None else acc + part
        self.e[r, w] = acc

    def mlp_out(self, i):
        r, n = self.half_tile(i)
        w = pl.ds(pl.multiple_of(n * 256, 256), 256)
        acc = self.h1[r, w] + self.db[w].astype(F32).reshape(1, -1)
        for m in range(8):
            acc = acc + nn(self.hid[m, r, :], self.w[(m // 4) * UNITS + 8 + m % 4, w, :])
        self.h1[r, w] = acc

    def norm_two_back(self):
        gain = self.gains[1:2, :].astype(F32)
        zero = jnp.zeros((1, gain.shape[1]), F32)
        def cap(c, carry):
            gg, sg, ob, db = carry
            r = self.crows(c)
            e, n, g = self.e[r, :], self.n2[r, :], self.g[r, :].astype(F32)
            dh = g + norm_back(e, n, self.r2[r, 0:1], gain)
            self.n2[r, :] = dh
            dob = dh.astype(BF16)
            self.dob[r, :] = dob
            return (gg + colsum(e * n), sg + colsum(e), ob + colsum(dob.astype(F32)), db + colsum(g))
        gg, sg, ob, db = lax.fori_loop(0, self.caps, cap, (zero, zero, zero, zero))
        self.small[1:2, :], self.small[3:4, :], self.small[4:5, :], self.small[5:6, :] = gg, sg, ob, db

    def out_back(self, s):
        w = tn(self.ctx[s], self.dob[...]).astype(BF16)
        self.grads[8, s, 0:256, :] = w[:, :256]
        self.grads[8, s, 256:512, :] = w[:, 256:]
        wo = s * UNITS + 3
        back = nt(self.dob[:, 0:256], self.w[wo, 0:256, :]) + nt(self.dob[:, 256:512], self.w[wo, 256:512, :])
        self.ctx[s] = back.astype(BF16)

    def qkv_grad(self, i):
        s, j = i // 3, i % 3
        d = self.dqkv[i]
        w = tn(self.a1[...], d).astype(BF16)
        if j < 2:
            self.grads[9 + j, s] = w
        else:
            self.hg[0, s], self.hg[1, s] = w[:256], w[256:]
        self.small_qkv[i] = colsum(d.astype(F32))

    def first_grad(self, i):
        r, n = self.half_tile(i)
        w = pl.ds(pl.multiple_of(n * 256, 256), 256)
        acc = None
        for m in range(6):
            part = nt(self.dqkv[m, r, :], self.w[(m // 3) * UNITS + m % 3, w, :])
            acc = part if acc is None else acc + part
        self.e[r, w] = acc

    def norm_one_back(self, out):
        gain = self.gains[0:1, :].astype(F32)
        zero = jnp.zeros((1, gain.shape[1]), F32)
        gg, sg = zero, zero
        for c in range(self.caps):
            r = slice(c * self.pad, (c + 1) * self.pad)
            e, n = self.e[r, :], self.n1[r, :]
            dx = self.n2[r, :] + norm_back(e, n, self.r1[r, 0:1], gain)
            out[c * self.slots : (c + 1) * self.slots, :] = dx[: self.slots]
            gg, sg = gg + colsum(e * n), sg + colsum(e)
        self.small[0:1, :], self.small[2:3, :] = gg, sg

    def layer_out(self, flat, out):
        for c in range(self.caps):
            flat[c * self.slots : (c + 1) * self.slots, :] = self.h1[c * self.pad : c * self.pad + self.slots, :]
        out[...] = flat[0 : self.caps * self.slots, :].astype(BF16)

    def pack_small(self, out):
        def put(slot, row, value):
            for i in range(value.shape[1] // 128):
                out[slot, row + i : row + i + 1, :] = value[:, i * 128 : (i + 1) * 128]
        for slot in range(2):
            out[slot] = jnp.zeros(out.shape[1:], F32)
            put(slot, 0, self.small_qkv[slot * 3])
            put(slot, 2, self.small_qkv[slot * 3 + 2])
            for n in range(4):
                put(slot, 4 + 2 * n, self.small_up[slot * 4 + n])
            for i, k in enumerate((4, 5, 0, 1, 2, 3)):
                put(slot, 12 + 4 * i, self.small[k : k + 1, :])


class Peers:
    def __init__(self):
        dp, t = lax.axis_index("dp"), lax.axis_index("tensor")
        depth = lax.axis_size("dp") // 4
        self.core = lax.rem(dp, 2)
        self.x = lax.rem(dp // 2, 2)
        self.z = dp // 4
        self.t = t
        self.to_y = (dp, 1 - t)
        self.to_x = (dp + 2 - 4 * self.x, t)
        self.to_core = (dp + 1 - 2 * self.core, t)
        self.depth = depth
        self.to_z = [(lax.rem(self.z + k, depth) * 4 + lax.rem(dp, 4), t) for k in range(1, depth)]
        self.z_of = [lax.rem(self.z + k, depth) for k in range(1, depth)]
        self.to_far = [(z * 4 + (1 - self.x) * 2 + self.core, t) for z in self.z_of]

    def all(self):
        return [self.to_y, self.to_x, self.to_core] + self.to_z + self.to_far

    def greet(self):
        barrier = pltpu.get_barrier_semaphore()
        for peer in self.all():
            pl.semaphore_signal(barrier, inc=1, device_id=peer, device_id_type=MESH)

    def meet(self):
        pl.semaphore_wait(pltpu.get_barrier_semaphore(), len(self.all()))


def rows(index, size):
    return pl.ds(pl.multiple_of(index * size, size), size)


def remote(src, dst, send, recv, peer):
    return pltpu.make_async_remote_copy(src_ref=src, dst_ref=dst, send_sem=send, recv_sem=recv, device_id=peer, device_id_type=MESH)


class Weights:
    def __init__(self, peers, w, send, recv):
        self.p, self.w, self.send, self.recv = peers, w, send, recv
        self.quarter = peers.core * 2 + peers.x
        self.size = w.shape[1] // 4

    def y(self, u):
        r = rows(self.quarter, self.size)
        return remote(self.w.at[u, r], self.w.at[UNITS + u, r], self.send.at[u, 0], self.recv.at[u, 0], self.p.to_y)

    def x(self, u):
        part = self.w.at[UNITS + u, rows(self.quarter, self.size)]
        return remote(part, part, self.send.at[u, 1], self.recv.at[u, 1], self.p.to_x)

    def c(self, u):
        part = self.w.at[UNITS + u, rows(self.p.core, self.size * 2)]
        return remote(part, part, self.send.at[u, 2], self.recv.at[u, 2], self.p.to_core)

    def relay_x(self, u):
        self.y(u).wait_recv()
        self.x(u).start()

    def relay_c(self, u):
        self.x(u).wait_recv()
        self.c(u).start()

    def ready(self, u):
        self.c(u).wait_recv()

    def drain(self, u):
        self.y(u).wait_send()
        self.x(u).wait_send()
        self.c(u).wait_send()


class Reduce:
    def __init__(self, peers, refs, sem0, send, recv, wide=False):
        self.p = peers
        self.wide = wide
        self.g, self.cr, self.yr, self.xr, self.zr, self.f = refs
        self.sem0, self.send, self.recv = sem0, send, recv
        self.count = self.g.shape[0]
        self.full = self.g.shape[2]
        self.half, self.quarter = self.full // 2, self.full // 4
        self.shard = self.quarter // peers.depth

    def sems(self, n, k):
        return self.send.at[self.sem0 + n, k], self.recv.at[self.sem0 + n, k]

    def c(self, n, slot):
        theirs = self.g.at[n, slot, rows(1 - self.p.core, self.half)]
        return remote(theirs, self.cr.at[n, slot], *self.sems(n, (5 + 2 * self.p.depth - 2) if slot == 0 else 0), self.p.to_core)

    def y(self, n):
        return remote(self.cr.at[n, 1], self.yr.at[n], *self.sems(n, 1), self.p.to_y)

    def x(self, n):
        return remote(self.cr.at[n, 0, rows(1 - self.p.x, self.quarter)], self.xr.at[n], *self.sems(n, 2), self.p.to_x)

    def z(self, n):
        return [
            remote(
                self.cr.at[n, 0, pl.ds(pl.multiple_of(self.p.x * self.quarter + self.p.z_of[k] * self.shard, self.shard), self.shard)],
                self.zr.at[n, k],
                *self.sems(n, 5 + k),
                self.p.to_z[k],
            )
            for k in range(self.p.depth - 1)
        ]

    def own_shard(self):
        p = self.p
        return pl.ds(pl.multiple_of(p.core * self.half + p.x * self.quarter + p.z * self.shard, self.shard), self.shard)

    def za(self, n):
        part = self.f.at[n, self.own_shard()]
        depth = self.p.depth
        copies = [remote(part, part, *self.sems(n, 4 + depth + k), self.p.to_z[k]) for k in range(depth - 1)]
        if self.wide:
            copies.append(remote(part, part, *self.sems(n, 3), self.p.to_x))
            copies += [remote(part, part, *self.sems(n, 4 + 2 * depth + k), self.p.to_far[k]) for k in range(depth - 1)]
        return copies

    def xa(self, n):
        part = self.f.at[n, pl.ds(pl.multiple_of(self.p.core * self.half + self.p.x * self.quarter, self.quarter), self.quarter)]
        return remote(part, part, *self.sems(n, 3), self.p.to_x)

    def ca(self, n):
        part = self.f.at[n, rows(self.p.core, self.half)]
        return remote(part, part, *self.sems(n, 4), self.p.to_core)

    def c_start(self, n):
        self.c(n, 1).start()

    def c_start_own(self, n):
        self.c(n, 0).start()

    def c_done(self, n):
        self.c(n, 1).wait_recv()
        self.cr[n, 1] = self.cr[n, 1] + self.g[n, 1, rows(self.p.core, self.half), :]
        self.y(n).start()

    def y_done(self, n):
        self.c(n, 0).wait_recv()
        self.y(n).wait_recv()
        self.cr[n, 0] = self.cr[n, 0] + self.g[n, 0, rows(self.p.core, self.half), :] + self.yr[n]
        self.x(n).start()

    def x_done(self, n):
        self.x(n).wait_recv()
        r = rows(self.p.x, self.quarter)
        self.cr[n, 0, r, :] = self.cr[n, 0, r, :] + self.xr[n]
        for copy in self.z(n):
            copy.start()

    def z_done(self, n):
        for copy in self.z(n):
            copy.wait_recv()
        mine = pl.ds(pl.multiple_of(self.p.x * self.quarter + self.p.z * self.shard, self.shard), self.shard)
        total = self.cr[n, 0, mine, :].astype(F32)
        for k in range(self.p.depth - 1):
            total = total + self.zr[n, k].astype(F32)
        self.f[n, self.own_shard(), :] = total.astype(self.f.dtype)
        for copy in self.za(n):
            copy.start()

    def za_done(self, n):
        for copy in self.za(n):
            copy.wait_recv()
        self.xa(n).start()

    def xza_done(self, n):
        for copy in self.za(n):
            copy.wait_recv()
        self.ca(n).start()

    def xa_done(self, n):
        self.xa(n).wait_recv()
        self.ca(n).start()

    def ca_done(self, n):
        self.ca(n).wait_recv()

    def drain(self, n):
        across = [] if self.wide else [self.xa(n)]
        for copy in across + [self.c(n, 0), self.c(n, 1), self.y(n), self.x(n), self.ca(n)] + self.z(n) + self.za(n):
            copy.wait_send()


def when(condition, body):
    if isinstance(condition, bool):
        if condition:
            body()
    else:
        pl.when(condition)(body)


ON_WEIGHTS = ("relay_x", "relay_c", "ready")
ON_GRADS = ("c_start", "c_done", "y_done", "x_done", "z_done", "za_done", "xa_done", "ca_done", "xza_done")
PLAN = {
    "norm_one": (),
    "qkv_own": (),
    "att_own": ((1, 0, (0,)), ),
    "widen_g": ((0, 0, (1,)), ),
    "pown": ((3, 0, (2,)), ),
    "qkv_other": ((0, 0, (100, 3, 200,)), (1, 0, (101, 4, 201,)), (2, 0, (102, 5, 202,)), ),
    "att_other": ((0, 0, (103,)), (1, 0, (104, 6, 7,)), ),
    "proj": ((0, 0, (105, 8, 203,)), ),
    "updown": ((0, 0, (204,)), (0, 1, (9,)), (0, 2, (1000, 106,)), (1, 0, (10, 205,)), (1, 1, (107, 1100,)), (1, 2, (1001, 11,)), (2, 0, (108, 206,)), (2, 1, (1101,)), (2, 2, (1002, 109,)), (3, 0, (207,)), (3, 1, (110,)), (3, 2, (1003, 1102, 1200,)), ),
    "hbug": ((0, 0, (111, 208,)), (0, 2, (1004,)), (1, 0, (1201, 1103, 209,)), (1, 1, (1300,)), (1, 2, (1005,)), (2, 0, (210,)), (2, 1, (1202, 1104,)), (2, 2, (1006,)), (2, 3, (1301,)), (3, 0, (211,)), (3, 1, (1400,)), (3, 2, (1007, 1203, 1105,)), (3, 3, (1302,)), ),
    "sg": ((2, 0, (1401,)), (3, 0, (1204, 1106,)), ),
    "ntb": ((0, 0, (1500, 1303,)), ),
    "ob1": ((0, 0, (1402, 1205, 1107,)), ),
    "ob0": ((0, 0, (1008,)), ),
    "ab": ((0, 0, (1501, 1304,)), (1, 0, (1600, 1403, 1206, 1108,)), (2, 0, (1700, 1502, 1305,)), (3, 0, (1601, 1404, 1207,)), ),
    "qg3": ((0, 0, (1701, 1503, 1306,)), ),
    "qg0": ((0, 0, (1009, 1602,)), ),
    "qg4": ((0, 0, (1405, 1208,)), ),
    "qg1": ((0, 0, (1010, 1109, 1702,)), ),
    "qg5": ((0, 0, (1504, 1307,)), ),
    "qg2": ((0, 0, (1011, 1012,)), ),
    "fg": ((0, 0, (1603, 1110,)), (1, 0, (1406,)), (2, 0, (1703,)), (3, 0, (1308,)), ),
    "nob": ((0, 0, (1505,)), ),
    "mo": ((0, 0, (1013, 1604, 1209, 1111,)), (1, 0, (1407,)), (2, 0, (1704, 1112,)), (3, 0, (1506,)), ),
    "lo": ((0, 0, (1605, 1210, 1113,)), ),
    "tail": ((0, 0, (1408, 1705, 1309, 1211, 1507, 1606, 1212, 1706, 1213, 1310, 1508, 1311, 1409, 1607, 1312, 1707, 1313, 1410, 1608, 1411, 1708, 1509, 1412, 1413, 1510, 1609, 1811, 1709, 1711, 1812, 1610, 1813, 1712, 1710, 1713,)), ),
}


def kernel(caps, slots, pad, names_in, *all_refs):
    L = Layer(caps, slots, pad, dict(zip(names_in, all_refs)))
    peers = Peers()
    peers.greet()
    L.cap_base = peers.t * caps
    weights = Weights(peers, L.w, L.wsend, L.wrecv)
    big = Reduce(peers, (L.grads, L.cr, L.yr, L.xr, L.zr, L.f), 0, L.gsend, L.grecv)
    half = Reduce(peers, (L.hg, L.hcr, L.hyr, L.hxr, L.hzr, L.hf), BIG, L.gsend, L.grecv, wide=True)
    small = Reduce(peers, (L.sg, L.scr, L.syr, L.sxr, L.szr, L.sf), BIG + 2, L.gsend, L.grecv, wide=True)

    def at(stage, unit):
        if unit < BIG:
            getattr(big, stage)(unit)
        elif unit < BIG + 2:
            getattr(half, stage)(unit - BIG)
        else:
            getattr(small, stage)(0)

    def arrive(codes):
        for code in codes:
            stage, unit = code // 100, code % 100
            if stage < 10:
                getattr(weights, ON_WEIGHTS[stage])(unit)
            else:
                at(ON_GRADS[stage - 10], unit)

    def run(name, count, *parts):
        def body(i):
            for k, part in enumerate(parts):
                for when_i, when_k, codes in PLAN[name]:
                    if when_k == k:
                        when(i == when_i, functools.partial(arrive, codes))
                part(i)

        if count == 1:
            body(0)
        else:
            loop(count, body)

    local = []

    def load(a, b):
        copy = pltpu.make_async_copy(a, b, L.lsem.at[len(local)])
        copy.start()
        local.append(copy)

    for j in range(3):
        load(L.wqkv_a.at[j], L.w.at[j])
    for n in range(2):
        load(L.wo_a.at[:, pl.ds(n * 256, 256)], L.w.at[3, pl.ds(n * 256, 256)])
    load(L.tok, L.tok_v)
    for n in range(4):
        load(L.wu_a.at[:, pl.ds(n * 256, 256)], L.w.at[4 + n])
    for n in range(4):
        for k in range(2):
            load(L.wd_a.at[pl.ds(n * 256, 256), pl.ds(k * 256, 256)], L.w.at[8 + n, pl.ds(k * 256, 256)])
    load(L.cot, L.cot_v)
    for name in ("qvb", "ub", "ob", "db", "gains", "shifts", "lengths"):
        load(getattr(L, name + "_h"), getattr(L, name))
    local[5].wait()
    L.widen(L.tok_v, peers.t * caps * slots, L.xs)
    for copy in local[:5] + local[6:]:
        copy.wait()
    peers.meet()
    bias_send = [
        remote(L.qvb, L.qvb_b, L.bsem.at[0], L.bsem.at[1], peers.to_y),
        remote(L.ub, L.ub_b, L.bsem.at[2], L.bsem.at[3], peers.to_y),
    ]
    for copy in bias_send:
        copy.start()
    loop(UNITS, lambda u: weights.y(u).start())
    attend = lambda i: [L.attention(4 * i + k) for k in range(4)]

    def rows_and_biases():
        L.widen(L.cot_v, peers.t * caps * slots, L.g)
        for copy in bias_send:
            copy.wait()
        L.biases(1, L.qvb_b, L.ub_b)

    def input_rows():
        L.norm_one_back(L.dx_out)
        L.pack_small(L.sg.at[0])

    def output_rows():
        L.layer_out(L.stage, L.y_out)

    def own(part, unit):
        return lambda n: (part(n), big.c_start_own(unit + n))

    run("norm_one", 1, lambda i: (L.norm_one(), L.biases(0, L.qvb, L.ub)))
    run("qkv_own", 3, L.qkv)
    run("att_own", caps // 4, attend)
    run("widen_g", 1, lambda i: rows_and_biases())
    run("pown", 4, L.project_own)
    run("qkv_other", 3, lambda j: L.qkv(3 + j))
    run("att_other", caps // 4, lambda i: attend(caps // 4 + i))
    run("proj", 4, L.project)
    run("updown", 4, lambda n: L.up(4 + n), lambda n: L.down_grad(4 + n), L.up, own(L.down_grad, 0))
    run("hbug", 4, lambda n: L.hidden_back(4 + n), lambda n: L.up_grad(4 + n), L.hidden_back, own(L.up_grad, 4))
    run("sg", 4, L.second_grad)
    run("ntb", 1, lambda i: L.norm_two_back())
    run("ob1", 1, lambda i: L.out_back(1))
    run("ob0", 1, lambda i: (L.out_back(0), big.c_start_own(8)))
    run("ab", caps // 2, lambda i: [L.attention_back(4 * i + k) for k in range(4)])
    for j in range(3):
        run(f"qg{3 + j}", 1, lambda i: L.qkv_grad(3 + j))
        run(f"qg{j}", 1, lambda i: L.qkv_grad(j))
        for unit in (9 + j,) if j < 2 else (11, 12):
            at("c_start_own", unit)
    run("fg", 4, L.first_grad)
    run("nob", 1, lambda i: (input_rows(), small.c_start_own(0)))
    run("mo", 4, L.mlp_out)
    run("lo", 1, lambda i: output_rows())
    tail = PLAN["tail"][0][2]
    arrive(tail[:-FINAL])
    loop(UNITS, weights.drain)
    loop(6, big.drain)
    arrive(tail[-FINAL:])

    loop(BIG - 6, lambda n: big.drain(6 + n))
    loop(2, half.drain)
    small.drain(0)


def finish(f, hf, s, y, dx, y_out, dx_out, qkv, out, up, down, qvb, ob, ub, db, gg, sh, wide, v1, v2, v3, v4, v5, v6, sem_out, sem_io):
    io = []

    def send(a, b, sem):
        copy = pltpu.make_async_copy(a, b, sem)
        copy.start()
        io.append(copy)

    send(y, y_out, sem_io.at[0])
    send(dx, dx_out, sem_io.at[1])

    def row(first, count):
        return jnp.concatenate([s[0, first + i : first + i + 1, :] for i in range(count)], axis=1)

    for n in range(UNITS):
        if n < BIG:
            wide[n] = f[n].astype(F32)
        else:
            for k in range(2):
                wide[n, k * 256 : (k + 1) * 256, :] = hf[k].astype(F32)
        if n < 4 or n == 8:
            for k in range(2):
                c = pl.ds(k * 256, 256)
                send(wide.at[n, c], down.at[pl.ds(n * 256, 256), c] if n < 4 else out.at[:, c], sem_out.at[2 * n + k])
        elif n < 8:
            send(wide.at[n], up.at[:, pl.ds((n - 4) * 256, 256)], sem_out.at[2 * n])
        else:
            send(wide.at[n], qkv.at[n - 9], sem_out.at[2 * n])
        if n == 1:
            v1[0:1, :], v1[1:2, :] = row(0, 2), row(2, 2)
            v3[...] = row(4, 8)
            v2[...], v4[...] = row(12, 4), row(16, 4)
            v5[0:1, :], v5[1:2, :] = row(20, 4), row(24, 4)
            v6[0:1, :], v6[1:2, :] = row(28, 4), row(32, 4)
            for k, (a, b) in enumerate(((v1, qvb), (v2, ob), (v3, ub), (v4, db), (v5, gg), (v6, sh))):
                send(a, b, sem_io.at[2 + k])
    for copy in io:
        copy.wait()


def shards(depth, tokens, lengths, qkv_weight, qv_bias, out_weight, out_bias, up_weight, up_bias, down_weight, down_bias, norm_gain, norm_shift, cotangent):
    total, width = tokens.shape
    count = lengths.shape[0]
    slots = total // count
    caps = count // 2
    pad = (slots + 15) // 16 * 16
    rws = caps * pad
    V = pl.BlockSpec(memory_space=pltpu.VMEM)
    A = pl.BlockSpec(memory_space=pl.ANY)
    ins = [
        ("tok", tokens, A), ("cot", cotangent, A), ("lengths_h", lengths, A),
        ("wqkv_a", qkv_weight, A), ("wo_a", out_weight, A), ("wu_a", up_weight, A), ("wd_a", down_weight, A),
        ("qvb_h", qv_bias, A), ("ub_h", up_bias, A),
        ("ob_h", out_bias, A), ("db_h", down_bias, A), ("gains_h", norm_gain, A), ("shifts_h", norm_shift, A),
    ]
    outs = [
        ("y_out", (caps * slots, 512), BF16), ("dx_out", (caps * slots, 512), F32),
        ("f", (BIG, 512, 256), BF16), ("hf", (2, 256, 256), BF16), ("sf", (1, 128, 128), F32),
    ]
    vm = pltpu.VMEM
    sems = UNITS + 2, 3 + 3 * depth
    held = [("qvb", qv_bias), ("ub", up_bias), ("ob", out_bias), ("db", down_bias), ("gains", norm_gain), ("shifts", norm_shift)]
    scr = [(n, vm(v.shape, v.dtype)) for n, v in held] + [
        ("lengths", pltpu.SMEM(lengths.shape, jnp.int32)),
        ("tok_v", vm((total, 512), BF16)), ("cot_v", vm((total, 512), BF16)),
        ("stage", vm((total + 16, 512), F32)), ("xs", vm((rws, 512), BF16)), ("g", vm((rws, 512), BF16)),
        ("n1", vm((rws, 512), F32)), ("r1", vm((rws, 128), F32)), ("a1", vm((rws, 512), BF16)),
        ("w", vm((2 * UNITS, 512, 256), BF16)), ("qvb_b", vm((2, 256), BF16)), ("ub_b", vm(up_bias.shape, BF16)),
        ("bias_qkv", vm((6, 1, 256), F32)), ("bias_up", vm((8, 1, 256), F32)),
        ("pqkv", vm((6, rws, 256), BF16)), ("probs", vm((2 * caps, 4 * pad, pad), F32)), ("ctx", vm((2, rws, 256), BF16)),
        ("h1", vm((rws, 512), F32)), ("n2", vm((rws, 512), F32)), ("r2", vm((rws, 128), F32)), ("a2", vm((rws, 512), BF16)),
        ("hid", vm((8, rws, 256), BF16)), ("act", vm((8, rws, 256), F32)), ("du", vm((8, rws, 256), BF16)),
        ("e", vm((rws, 512), F32)), ("dob", vm((rws, 512), BF16)),
        ("dqkv", vm((6, rws, 256), BF16)),
        ("small", vm((8, 512), F32)), ("small_up", vm((8, 1, 256), F32)), ("small_qkv", vm((6, 1, 256), F32)),
        ("grads", vm((BIG, 2, 512, 256), BF16)), ("cr", vm((BIG, 2, 256, 256), BF16)), ("yr", vm((BIG, 256, 256), BF16)),
        ("xr", vm((BIG, 128, 256), BF16)), ("zr", vm((BIG, depth - 1, 128 // depth, 256), BF16)),
        ("hg", vm((2, 2, 256, 256), BF16)), ("hcr", vm((2, 2, 128, 256), BF16)), ("hyr", vm((2, 128, 256), BF16)),
        ("hxr", vm((2, 64, 256), BF16)), ("hzr", vm((2, depth - 1, 64 // depth, 256), BF16)),
        ("sg", vm((1, 2, 128, 128), F32)), ("scr", vm((1, 2, 64, 128), F32)), ("syr", vm((1, 64, 128), F32)),
        ("sxr", vm((1, 32, 128), F32)), ("szr", vm((1, depth - 1, 32 // depth, 128), F32)),
        ("lsem", pltpu.SemaphoreType.DMA((28,))), ("bsem", pltpu.SemaphoreType.DMA((4,))),
        ("wsend", pltpu.SemaphoreType.DMA((UNITS, 3))), ("wrecv", pltpu.SemaphoreType.DMA((UNITS, 3))),
        ("gsend", pltpu.SemaphoreType.DMA(sems)), ("grecv", pltpu.SemaphoreType.DMA(sems)),
    ]
    names = [n for n, _, _ in ins] + [n for n, _, _ in outs] + [n for n, _ in scr]
    y, dx, f, hf, s = pl.pallas_call(
        functools.partial(kernel, caps, slots, pad, names),
        out_shape=[vm(s, d) for _, s, d in outs],
        in_specs=[s for _, _, s in ins],
        out_specs=[V] * len(outs),
        scratch_shapes=[s for _, s in scr],
        compiler_params=pltpu.CompilerParams(vmem_limit_bytes=VLIM, collective_id=0, has_side_effects=True),
        name="layer",
    )(*[v for _, v, _ in ins])
    results = [
        (y.shape, BF16, A), (dx.shape, F32, A), (qkv_weight.shape, F32, A), (out_weight.shape, F32, A),
        (up_weight.shape, F32, A), (down_weight.shape, F32, A),
        (qv_bias.shape, F32, A), ((1, 512), F32, A), ((1, up_bias.shape[0]), F32, A), ((1, 512), F32, A), ((2, 512), F32, A), ((2, 512), F32, A),
    ]
    y, dx, qkv, out, up, down, qvb, ob, ub, db, gg, sh = pl.pallas_call(
        finish,
        out_shape=[jax.ShapeDtypeStruct(s, d) for s, d, _ in results],
        in_specs=[V] * 5,
        out_specs=[s for _, _, s in results],
        scratch_shapes=[
            vm((UNITS, 512, 256), F32), *[vm(s, F32) for s, _, _ in results[6:]], pltpu.SemaphoreType.DMA((2 * UNITS,)), pltpu.SemaphoreType.DMA((8,)),
        ],
        compiler_params=pltpu.CompilerParams(vmem_limit_bytes=12 << 20),
        name="finish",
    )(*[pltpu.with_memory_space_constraint(v, pltpu.VMEM) for v in (f, hf, s, y, dx)])
    return y, dx, qkv, qvb, out, ob[0], up, ub[0], down, db[0], gg, sh


def matmul_plain(left, right):
    return jnp.dot(left, right, preferred_element_type=jnp.float32)


def contract_rows(left, right):
    return lax.dot_general(
        left, right, (((0,), (0,)), ((), ())), preferred_element_type=jnp.float32
    )


def contract_cols(left, right):
    return lax.dot_general(
        left, right, (((1,), (1,)), ((), ())), preferred_element_type=jnp.float32
    )


def plain_norm_stats(values):
    center = values - jnp.mean(values, axis=-1, keepdims=True)
    inv_std = lax.rsqrt(jnp.mean(center * center, axis=-1, keepdims=True) + EPSILON)
    return (center * inv_std, inv_std)


def plain_norm_back(upstream, normed, inv_std, gain_vec):
    scaled = upstream * gain_vec
    inner_mean = jnp.mean(scaled * normed, axis=-1, keepdims=True)
    result = inv_std * (scaled - jnp.mean(scaled, axis=-1, keepdims=True) - normed * inner_mean)
    return (result, jnp.sum(upstream * normed, axis=0), jnp.sum(upstream, axis=0))


def row_slice(values, row_start, share_rows):
    return lax.dynamic_slice_in_dim(values, row_start, share_rows, 0)


def shards_by_heads(
    tokens,
    lengths,
    qkv_weight,
    qv_bias,
    out_weight,
    out_bias,
    up_weight,
    up_bias,
    down_weight,
    down_bias,
    norm_gain,
    norm_shift,
    cotangent,
):
    tensor_count = lax.axis_size("tensor")
    tensor_index = lax.axis_index("tensor")
    share_rows = tokens.shape[0] // tensor_count
    row_start = tensor_index * share_rows
    gains = norm_gain.astype(jnp.float32)
    shifts = norm_shift.astype(jnp.float32)
    total_rows = tokens.shape[0]
    count = lengths.shape[0]
    slots = total_rows // count
    local_width = qkv_weight.shape[2]
    local_heads = local_width // HD
    score_scale = HD ** (-0.5)
    qv_float = qv_bias.astype(jnp.float32)
    token_f = tokens.astype(jnp.float32)
    normed_one, inv_one = plain_norm_stats(token_f)
    first_in = (normed_one * gains[0] + shifts[0]).astype(jnp.bfloat16)
    queries = (matmul_plain(first_in, qkv_weight[0]) + qv_float[0]).astype(jnp.bfloat16)
    keys_all = matmul_plain(first_in, qkv_weight[1]).astype(jnp.bfloat16)
    values_all = (matmul_plain(first_in, qkv_weight[2]) + qv_float[1]).astype(jnp.bfloat16)
    shape4 = (count, slots, local_heads, HD)
    query_four = queries.reshape(shape4)
    key_four = keys_all.reshape(shape4)
    value_four = values_all.reshape(shape4)
    position = jnp.arange(slots)
    allowed = (position[None, :] <= position[:, None])[None, :, :] & (
        position[None, None, :] < lengths[:, None, None]
    )
    allowed = allowed[:, None, :, :]

    def masked_scores():
        raw = jnp.einsum(
            "cihd,cjhd->chij", query_four, key_four, preferred_element_type=jnp.float32
        )
        return jnp.where(allowed, raw * score_scale, -1e30)

    scores = masked_scores()
    row_max = jnp.max(scores, axis=-1, keepdims=True)
    log_total = row_max + jnp.log(jnp.sum(jnp.exp(scores - row_max), axis=-1, keepdims=True))
    probs_low = jnp.exp(scores - log_total).astype(jnp.bfloat16)
    context = jnp.einsum(
        "chij,cjhd->cihd", probs_low, value_four, preferred_element_type=jnp.float32
    )
    context = context.reshape(total_rows, local_width).astype(jnp.bfloat16)
    attn_part = matmul_plain(context, out_weight)
    attn_out = lax.psum(attn_part, "tensor") + out_bias.astype(jnp.float32)
    hidden_res = token_f + attn_out
    normed_two, inv_two = plain_norm_stats(hidden_res)
    second_in = (normed_two * gains[1] + shifts[1]).astype(jnp.bfloat16)
    upper = matmul_plain(second_in, up_weight) + up_bias.astype(jnp.float32)
    sigma = jax.nn.sigmoid(1.702 * upper)
    hidden = (upper * sigma).astype(jnp.bfloat16)
    mlp_part = matmul_plain(hidden, down_weight)
    result_rows = (
        hidden_res
        + lax.psum(mlp_part.astype(jnp.bfloat16), "tensor").astype(jnp.float32)
        + down_bias.astype(jnp.float32)
    )
    layer_out = row_slice(result_rows, row_start, share_rows).astype(jnp.bfloat16)
    grad_f = cotangent.astype(jnp.float32)
    down_grad = contract_rows(hidden, cotangent)
    down_bias_grad = jnp.sum(grad_f, axis=0)
    hidden_grad = contract_cols(cotangent, down_weight)
    upper_grad = (hidden_grad * (sigma + 1.702 * upper * sigma * (1.0 - sigma))).astype(
        jnp.bfloat16
    )
    up_grad = contract_rows(second_in, upper_grad)
    up_bias_grad = jnp.sum(upper_grad.astype(jnp.float32), axis=0)
    second_part = contract_cols(upper_grad, up_weight)
    second_grad = lax.psum(second_part, "tensor")
    residual_back, gain_two, shift_two = plain_norm_back(second_grad, normed_two, inv_two, gains[1])
    residual_full = grad_f + residual_back
    branch_grad = residual_full.astype(jnp.bfloat16)
    out_bias_grad = jnp.sum(branch_grad.astype(jnp.float32), axis=0)
    out_grad = contract_rows(context, branch_grad)
    context_grad = contract_cols(branch_grad, out_weight).astype(jnp.bfloat16).reshape(shape4)
    probs = jnp.exp(masked_scores() - log_total)
    probs_low = probs.astype(jnp.bfloat16)
    value_grad = jnp.einsum(
        "chij,cihd->cjhd", probs_low, context_grad, preferred_element_type=jnp.float32
    )
    prob_grad = jnp.einsum(
        "cihd,cjhd->chij", context_grad, value_four, preferred_element_type=jnp.float32
    )
    score_grad = probs * (prob_grad - jnp.sum(prob_grad * probs, axis=-1, keepdims=True))
    score_grad = score_grad.astype(jnp.bfloat16)
    query_grad = (
        jnp.einsum("chij,cjhd->cihd", score_grad, key_four, preferred_element_type=jnp.float32)
        * score_scale
    )
    key_grad = (
        jnp.einsum("chij,cihd->cjhd", score_grad, query_four, preferred_element_type=jnp.float32)
        * score_scale
    )
    query_grad = query_grad.reshape(total_rows, local_width).astype(jnp.bfloat16)
    key_grad = key_grad.reshape(total_rows, local_width).astype(jnp.bfloat16)
    value_grad = value_grad.reshape(total_rows, local_width).astype(jnp.bfloat16)
    qkv_grad = jnp.stack(
        [
            contract_rows(first_in, query_grad),
            contract_rows(first_in, key_grad),
            contract_rows(first_in, value_grad),
        ]
    )
    qv_bias_grad = jnp.stack(
        [
            jnp.sum(query_grad.astype(jnp.float32), axis=0),
            jnp.sum(value_grad.astype(jnp.float32), axis=0),
        ]
    )
    first_part = (
        contract_cols(query_grad, qkv_weight[0])
        + contract_cols(key_grad, qkv_weight[1])
        + contract_cols(value_grad, qkv_weight[2])
    )
    first_grad = lax.psum(first_part.astype(jnp.bfloat16), "tensor").astype(jnp.float32)
    input_back, gain_one, shift_one = plain_norm_back(first_grad, normed_one, inv_one, gains[0])
    input_grad = row_slice(residual_full + input_back, row_start, share_rows)
    gain_grads = jnp.stack([gain_one, gain_two])
    shift_grads = jnp.stack([shift_one, shift_two])
    summed = (
        lax.psum(qkv_grad.astype(jnp.bfloat16), "dp").astype(jnp.float32),
        lax.psum(qv_bias_grad.astype(jnp.bfloat16), "dp").astype(jnp.float32),
        lax.psum(out_grad.astype(jnp.bfloat16), "dp").astype(jnp.float32),
        lax.psum(out_bias_grad.astype(jnp.bfloat16), "dp").astype(jnp.float32),
        lax.psum(up_grad.astype(jnp.bfloat16), "dp").astype(jnp.float32),
        lax.psum(up_bias_grad.astype(jnp.bfloat16), "dp").astype(jnp.float32),
        lax.psum(down_grad.astype(jnp.bfloat16), "dp").astype(jnp.float32),
        lax.psum(down_bias_grad.astype(jnp.bfloat16), "dp").astype(jnp.float32),
        lax.psum(gain_grads.astype(jnp.bfloat16), "dp").astype(jnp.float32),
        lax.psum(shift_grads.astype(jnp.bfloat16), "dp").astype(jnp.float32),
    )
    return (
        layer_out,
        input_grad,
        summed[0],
        summed[1],
        summed[2],
        summed[3],
        summed[4],
        summed[5],
        summed[6],
        summed[7],
        summed[8],
        summed[9],
    )


def solution(mesh):
    dp, tensor = mesh.shape["dp"], mesh.shape["tensor"]
    if tensor == 2 and dp == 16:
        body = functools.partial(shards, dp // 4)
    else:
        body = shards_by_heads
    return jax.shard_map(
        body,
        mesh=mesh,
        in_specs=(P("dp", None), P("dp"), P(None, None, "tensor"), P(None, "tensor"), P("tensor", None), P(), P(None, "tensor"), P("tensor"), P("tensor", None), P(), P(), P(), P("dp", None)),
        out_specs=(P(("dp", "tensor"), None), P(("dp", "tensor"), None), P(None, None, "tensor"), P(None, "tensor"), P("tensor", None), P(), P(None, "tensor"), P("tensor"), P("tensor", None), P(), P(), P()),
        check_vma=False,
    )
```

```python
import functools

import jax
import jax.numpy as jnp
from jax import lax
from jax.experimental import pallas as pl
from jax.experimental.pallas import tpu as pltpu
from jax.sharding import PartitionSpec as P

HD = 64
EPSILON = 1e-05
F32 = jnp.float32
BF16 = jnp.bfloat16
LOG2E = 1.4426950408889634
UNITS = 12
BIG = 11
FINAL = 14
VLIM = 54 << 20
MESH = pl.DeviceIdType.MESH


def nn(left, right):
    return lax.dot_general(left, right, (((1,), (0,)), ((), ())), preferred_element_type=F32)


def nt(left, right):
    return lax.dot_general(left, right, (((1,), (1,)), ((), ())), preferred_element_type=F32)


def tn(left, right):
    return lax.dot_general(left, right, (((0,), (0,)), ((), ())), preferred_element_type=F32)


def loop(count, body):
    lax.fori_loop(0, count, lambda i, c: (body(i), c)[1], 0)


def norm(rows):
    center = rows - jnp.mean(rows, axis=-1, keepdims=True)
    inv = lax.rsqrt(jnp.mean(center * center, axis=-1, keepdims=True) + EPSILON)
    return center * inv, inv


def norm_back(grad, normed, inv, gain):
    t = grad * gain
    inner = jnp.mean(t * normed, axis=-1, keepdims=True)
    return inv * (t - jnp.mean(t, axis=-1, keepdims=True) - normed * inner)


def colsum(x):
    return jnp.sum(x, axis=0, keepdims=True)


class Layer:
    def __init__(self, caps, slots, pad, refs):
        self.caps, self.slots, self.pad = caps, slots, pad
        self.rows = caps * pad
        self.__dict__.update(refs)

    def head_mask(self, h, rows):
        lane = lax.broadcasted_iota(jnp.int32, (rows, 256), 1)
        return (lane >= h * HD) & (lane < (h + 1) * HD)

    def stack(self, block):
        parts = []
        for h in range(4):
            parts.append(jnp.where(self.head_mask(h, self.pad), block, jnp.zeros_like(block)))
        return jnp.concatenate(parts, axis=0)

    def unstack(self, block):
        out = None
        for h in range(4):
            part = block[h * self.pad : (h + 1) * self.pad]
            out = part if out is None else jnp.where(self.head_mask(h, self.pad), part, out)
        return out

    def widen(self, src, base, dst):
        total = src.shape[0]
        tile = self.slots * 2 if total % (self.slots * 2) == 0 else self.slots
        tile = 176 if total % 176 == 0 else total
        def conv(i):
            r = pl.ds(pl.multiple_of(i * tile, 16), tile)
            self.stage[r, :] = src[r, :].astype(F32)
        loop(total // tile, conv)
        self.stage[total : total + 16, :] = jnp.zeros((16, self.stage.shape[1]), F32)
        for c in range(self.caps):
            off = c * self.slots
            low = off // 8 * 8
            v = self.stage[pl.ds(pl.multiple_of(base + low, 8), self.pad + 8), :]
            v = v[off - low : off - low + self.pad]
            row = lax.broadcasted_iota(jnp.int32, v.shape, 0)
            v = jnp.where(row < self.slots, v, 0.0)
            dst[c * self.pad : (c + 1) * self.pad, :] = v.astype(BF16)

    def crows(self, c):
        return pl.ds(pl.multiple_of(c * self.pad, self.pad), self.pad)

    def norm_one(self):
        gain, shift = self.gains[0:1, :].astype(F32), self.shifts[0:1, :].astype(F32)
        def cap(c):
            r = self.crows(c)
            n, inv = norm(self.xs[r, :].astype(F32))
            self.n1[r, :] = n
            self.r1[r, :] = jnp.broadcast_to(inv, (self.pad, 128))
            self.a1[r, :] = (n * gain + shift).astype(BF16)
        loop(self.caps, cap)

    def biases(self, s, qvb, ub):
        for j in range(3):
            if j == 1:
                self.bias_qkv[s * 3 + j] = jnp.zeros((1, 256), F32)
            else:
                self.bias_qkv[s * 3 + j] = qvb[j // 2 : j // 2 + 1, :].astype(F32)
        up = ub[...].astype(F32).reshape(1, -1)
        for n in range(4):
            self.bias_up[s * 4 + n] = up[:, n * 256 : (n + 1) * 256]

    def qkv(self, i):
        s, j = i // 3, lax.rem(i, 3)
        out = nn(self.a1[...], self.w[s * UNITS + j]) + self.bias_qkv[i]
        self.pqkv[i] = out.astype(BF16)

    def attention(self, i):
        s, c = i // self.caps, lax.rem(i, self.caps)
        r = self.crows(c)
        scores = nt(self.stack(self.pqkv[s * 3, r, :]), self.pqkv[s * 3 + 1, r, :])
        length = self.lengths[self.cap_base + c]
        ii = lax.broadcasted_iota(jnp.int32, (self.pad, self.pad), 0)
        jj = lax.broadcasted_iota(jnp.int32, (self.pad, self.pad), 1)
        allowed = (jj <= ii) & (jj < length)
        blocks = []
        for h in range(4):
            blk = jnp.where(allowed, scores[h * self.pad : (h + 1) * self.pad], -1e30)
            top = jnp.max(blk, axis=1, keepdims=True)
            e = jnp.exp2((blk - top) * (HD**-0.5 * LOG2E))
            blocks.append(e * (1.0 / jnp.sum(e, axis=1, keepdims=True)))
        p = jnp.concatenate(blocks, axis=0)
        self.probs[i] = p
        self.ctx[s, r, :] = self.unstack(nn(p.astype(BF16), self.pqkv[s * 3 + 2, r, :])).astype(BF16)

    def attention_back(self, i):
        s, c = i // self.caps, lax.rem(i, self.caps)
        r = self.crows(c)
        q = self.stack(self.pqkv[s * 3, r, :])
        d = self.stack(self.ctx[s, r, :])
        p = self.probs[i]
        self.dqkv[s * 3 + 2, r, :] = tn(p.astype(BF16), d).astype(BF16)
        dp = nt(d, self.pqkv[s * 3 + 2, r, :])
        ds = (p * (dp - jnp.sum(dp * p, axis=1, keepdims=True))).astype(BF16)
        self.dqkv[s * 3 + 1, r, :] = (tn(ds, q) * HD**-0.5).astype(BF16)
        self.dqkv[s * 3, r, :] = (self.unstack(nn(ds, self.pqkv[s * 3 + 1, r, :])) * HD**-0.5).astype(BF16)

    def half_rows(self, i):
        tile = self.rows // 2
        return pl.ds(pl.multiple_of(i * tile, 16), tile)

    def out_product(self, slot, r):
        c = self.ctx[slot, r, :]
        return jnp.concatenate([nn(c, self.w[slot * UNITS + 3, k * 256 : (k + 1) * 256, :]) for k in range(2)], axis=1)

    def project_own(self, i):
        r = self.half_rows(i)
        self.h1[r, :] = self.xs[r, :].astype(F32) + self.out_product(0, r) + self.ob[...].astype(F32).reshape(1, -1)

    def project(self, i):
        r = self.half_rows(i)
        gain, shift = self.gains[1:2, :].astype(F32), self.shifts[1:2, :].astype(F32)
        h1 = self.h1[r, :] + self.out_product(1, r)
        self.h1[r, :] = h1
        n, inv = norm(h1)
        self.n2[r, :] = n
        self.r2[r, :] = jnp.broadcast_to(inv, (n.shape[0], 128))
        self.a2[r, :] = (n * gain + shift).astype(BF16)

    def wup(self, m):
        return (m // 4) * UNITS + 4 + lax.rem(m, 4)

    def wdown(self, m):
        return (m // 4) * UNITS + 8 + lax.rem(m, 4)

    def up(self, m):
        u = nn(self.a2[...], self.w[self.wup(m)]) + self.bias_up[m]
        sg = 0.5 * jnp.tanh(0.851 * u) + 0.5
        h = u * sg
        self.hid[m] = h.astype(BF16)
        self.act[m] = sg + 1.702 * h * (1.0 - sg)

    def down_grad(self, m):
        w = tn(self.hid[m], self.g[...]).astype(BF16)
        s, n = m // 4, lax.rem(m, 4)
        self.grads[n, s, 0:256, :] = w[:, :256]
        self.grads[n, s, 256:512, :] = w[:, 256:]

    def hidden_back(self, m):
        w = self.wdown(m)
        back = nt(self.g[:, 0:256], self.w[w, 0:256, :]) + nt(self.g[:, 256:512], self.w[w, 256:512, :])
        du = (back * self.act[m]).astype(BF16)
        self.du[m] = du
        self.small_up[m] = colsum(du.astype(F32))

    def up_grad(self, m):
        s, n = m // 4, lax.rem(m, 4)
        self.grads[4 + n, s] = tn(self.a2[...], self.du[m]).astype(BF16)

    def half_tile(self, i):
        tile = self.rows // 2
        r = pl.ds(pl.multiple_of((i // 2) * tile, 16), tile)
        return r, lax.rem(i, 2)

    def second_grad(self, i):
        r, n = self.half_tile(i)
        w = pl.ds(pl.multiple_of(n * 256, 256), 256)
        acc = None
        for m in range(8):
            part = nt(self.du[m, r, :], self.w[(m // 4) * UNITS + 4 + m % 4, w, :])
            acc = part if acc is None else acc + part
        self.e[r, w] = acc

    def mlp_out(self, i):
        r, n = self.half_tile(i)
        w = pl.ds(pl.multiple_of(n * 256, 256), 256)
        acc = self.h1[r, w] + self.db[w].astype(F32).reshape(1, -1)
        for m in range(8):
            acc = acc + nn(self.hid[m, r, :], self.w[(m // 4) * UNITS + 8 + m % 4, w, :])
        self.h1[r, w] = acc

    def norm_two_back(self):
        gain = self.gains[1:2, :].astype(F32)
        zero = jnp.zeros((1, gain.shape[1]), F32)
        def cap(c, carry):
            gg, sg, ob, db = carry
            r = self.crows(c)
            e, n, g = self.e[r, :], self.n2[r, :], self.g[r, :].astype(F32)
            dh = g + norm_back(e, n, self.r2[r, 0:1], gain)
            self.n2[r, :] = dh
            dob = dh.astype(BF16)
            self.dob[r, :] = dob
            return (gg + colsum(e * n), sg + colsum(e), ob + colsum(dob.astype(F32)), db + colsum(g))
        gg, sg, ob, db = lax.fori_loop(0, self.caps, cap, (zero, zero, zero, zero))
        self.small[1:2, :], self.small[3:4, :], self.small[4:5, :], self.small[5:6, :] = gg, sg, ob, db

    def out_back(self, s):
        w = tn(self.ctx[s], self.dob[...]).astype(BF16)
        self.grads[8, s, 0:256, :] = w[:, :256]
        self.grads[8, s, 256:512, :] = w[:, 256:]
        wo = s * UNITS + 3
        back = nt(self.dob[:, 0:256], self.w[wo, 0:256, :]) + nt(self.dob[:, 256:512], self.w[wo, 256:512, :])
        self.ctx[s] = back.astype(BF16)

    def qkv_grad(self, i):
        s, j = i // 3, i % 3
        d = self.dqkv[i]
        w = tn(self.a1[...], d).astype(BF16)
        if j < 2:
            self.grads[9 + j, s] = w
        else:
            self.hg[0, s], self.hg[1, s] = w[:256], w[256:]
        self.small_qkv[i] = colsum(d.astype(F32))

    def first_grad(self, i):
        r, n = self.half_tile(i)
        w = pl.ds(pl.multiple_of(n * 256, 256), 256)
        acc = None
        for m in range(6):
            part = nt(self.dqkv[m, r, :], self.w[(m // 3) * UNITS + m % 3, w, :])
            acc = part if acc is None else acc + part
        self.e[r, w] = acc

    def norm_one_back(self, out):
        gain = self.gains[0:1, :].astype(F32)
        zero = jnp.zeros((1, gain.shape[1]), F32)
        gg, sg = zero, zero
        for c in range(self.caps):
            r = slice(c * self.pad, (c + 1) * self.pad)
            e, n = self.e[r, :], self.n1[r, :]
            dx = self.n2[r, :] + norm_back(e, n, self.r1[r, 0:1], gain)
            out[c * self.slots : (c + 1) * self.slots, :] = dx[: self.slots]
            gg, sg = gg + colsum(e * n), sg + colsum(e)
        self.small[0:1, :], self.small[2:3, :] = gg, sg

    def layer_out(self, flat, out):
        for c in range(self.caps):
            flat[c * self.slots : (c + 1) * self.slots, :] = self.h1[c * self.pad : c * self.pad + self.slots, :]
        out[...] = flat[0 : self.caps * self.slots, :].astype(BF16)

    def pack_small(self, out):
        def put(slot, row, value):
            for i in range(value.shape[1] // 128):
                out[slot, row + i : row + i + 1, :] = value[:, i * 128 : (i + 1) * 128]
        for slot in range(2):
            out[slot] = jnp.zeros(out.shape[1:], F32)
            put(slot, 0, self.small_qkv[slot * 3])
            put(slot, 2, self.small_qkv[slot * 3 + 2])
            for n in range(4):
                put(slot, 4 + 2 * n, self.small_up[slot * 4 + n])
            for i, k in enumerate((4, 5, 0, 1, 2, 3)):
                put(slot, 12 + 4 * i, self.small[k : k + 1, :])


class Peers:
    def __init__(self):
        dp, t = lax.axis_index("dp"), lax.axis_index("tensor")
        depth = lax.axis_size("dp") // 4
        self.core = lax.rem(dp, 2)
        self.x = lax.rem(dp // 2, 2)
        self.z = dp // 4
        self.t = t
        self.to_y = (dp, 1 - t)
        self.to_x = (dp + 2 - 4 * self.x, t)
        self.to_core = (dp + 1 - 2 * self.core, t)
        self.depth = depth
        self.to_z = [(lax.rem(self.z + k, depth) * 4 + lax.rem(dp, 4), t) for k in range(1, depth)]
        self.z_of = [lax.rem(self.z + k, depth) for k in range(1, depth)]
        self.to_far = [(z * 4 + (1 - self.x) * 2 + self.core, t) for z in self.z_of]

    def all(self):
        return [self.to_y, self.to_x, self.to_core] + self.to_z + self.to_far

    def greet(self):
        barrier = pltpu.get_barrier_semaphore()
        for peer in self.all():
            pl.semaphore_signal(barrier, inc=1, device_id=peer, device_id_type=MESH)

    def meet(self):
        pl.semaphore_wait(pltpu.get_barrier_semaphore(), len(self.all()))


def rows(index, size):
    return pl.ds(pl.multiple_of(index * size, size), size)


def remote(src, dst, send, recv, peer):
    return pltpu.make_async_remote_copy(src_ref=src, dst_ref=dst, send_sem=send, recv_sem=recv, device_id=peer, device_id_type=MESH)


class Weights:
    def __init__(self, peers, w, send, recv):
        self.p, self.w, self.send, self.recv = peers, w, send, recv
        self.quarter = peers.core * 2 + peers.x
        self.size = w.shape[1] // 4

    def y(self, u):
        r = rows(self.quarter, self.size)
        return remote(self.w.at[u, r], self.w.at[UNITS + u, r], self.send.at[u, 0], self.recv.at[u, 0], self.p.to_y)

    def x(self, u):
        part = self.w.at[UNITS + u, rows(self.quarter, self.size)]
        return remote(part, part, self.send.at[u, 1], self.recv.at[u, 1], self.p.to_x)

    def c(self, u):
        part = self.w.at[UNITS + u, rows(self.p.core, self.size * 2)]
        return remote(part, part, self.send.at[u, 2], self.recv.at[u, 2], self.p.to_core)

    def relay_x(self, u):
        self.y(u).wait_recv()
        self.x(u).start()

    def relay_c(self, u):
        self.x(u).wait_recv()
        self.c(u).start()

    def ready(self, u):
        self.c(u).wait_recv()

    def drain(self, u):
        self.y(u).wait_send()
        self.x(u).wait_send()
        self.c(u).wait_send()


class Reduce:
    def __init__(self, peers, refs, sem0, send, recv, wide=False):
        self.p = peers
        self.wide = wide
        self.g, self.cr, self.yr, self.xr, self.zr, self.f = refs
        self.sem0, self.send, self.recv = sem0, send, recv
        self.count = self.g.shape[0]
        self.full = self.g.shape[2]
        self.half, self.quarter = self.full // 2, self.full // 4
        self.shard = self.quarter // peers.depth

    def sems(self, n, k):
        return self.send.at[self.sem0 + n, k], self.recv.at[self.sem0 + n, k]

    def c(self, n, slot):
        theirs = self.g.at[n, slot, rows(1 - self.p.core, self.half)]
        return remote(theirs, self.cr.at[n, slot], *self.sems(n, (5 + 2 * self.p.depth - 2) if slot == 0 else 0), self.p.to_core)

    def y(self, n):
        return remote(self.cr.at[n, 1], self.yr.at[n], *self.sems(n, 1), self.p.to_y)

    def x(self, n):
        return remote(self.cr.at[n, 0, rows(1 - self.p.x, self.quarter)], self.xr.at[n], *self.sems(n, 2), self.p.to_x)

    def z(self, n):
        return [
            remote(
                self.cr.at[n, 0, pl.ds(pl.multiple_of(self.p.x * self.quarter + self.p.z_of[k] * self.shard, self.shard), self.shard)],
                self.zr.at[n, k],
                *self.sems(n, 5 + k),
                self.p.to_z[k],
            )
            for k in range(self.p.depth - 1)
        ]

    def own_shard(self):
        p = self.p
        return pl.ds(pl.multiple_of(p.core * self.half + p.x * self.quarter + p.z * self.shard, self.shard), self.shard)

    def za(self, n):
        part = self.f.at[n, self.own_shard()]
        depth = self.p.depth
        copies = [remote(part, part, *self.sems(n, 4 + depth + k), self.p.to_z[k]) for k in range(depth - 1)]
        if self.wide:
            copies.append(remote(part, part, *self.sems(n, 3), self.p.to_x))
            copies += [remote(part, part, *self.sems(n, 4 + 2 * depth + k), self.p.to_far[k]) for k in range(depth - 1)]
        return copies

    def xa(self, n):
        part = self.f.at[n, pl.ds(pl.multiple_of(self.p.core * self.half + self.p.x * self.quarter, self.quarter), self.quarter)]
        return remote(part, part, *self.sems(n, 3), self.p.to_x)

    def ca(self, n):
        part = self.f.at[n, rows(self.p.core, self.half)]
        return remote(part, part, *self.sems(n, 4), self.p.to_core)

    def c_start(self, n):
        self.c(n, 1).start()

    def c_start_own(self, n):
        self.c(n, 0).start()

    def c_done(self, n):
        self.c(n, 1).wait_recv()
        self.cr[n, 1] = self.cr[n, 1] + self.g[n, 1, rows(self.p.core, self.half), :]
        self.y(n).start()

    def y_done(self, n):
        self.c(n, 0).wait_recv()
        self.y(n).wait_recv()
        self.cr[n, 0] = self.cr[n, 0] + self.g[n, 0, rows(self.p.core, self.half), :] + self.yr[n]
        self.x(n).start()

    def x_done(self, n):
        self.x(n).wait_recv()
        r = rows(self.p.x, self.quarter)
        self.cr[n, 0, r, :] = self.cr[n, 0, r, :] + self.xr[n]
        for copy in self.z(n):
            copy.start()

    def z_done(self, n):
        for copy in self.z(n):
            copy.wait_recv()
        mine = pl.ds(pl.multiple_of(self.p.x * self.quarter + self.p.z * self.shard, self.shard), self.shard)
        total = self.cr[n, 0, mine, :].astype(F32)
        for k in range(self.p.depth - 1):
            total = total + self.zr[n, k].astype(F32)
        self.f[n, self.own_shard(), :] = total.astype(self.f.dtype)
        for copy in self.za(n):
            copy.start()

    def za_done(self, n):
        for copy in self.za(n):
            copy.wait_recv()
        self.xa(n).start()

    def xza_done(self, n):
        for copy in self.za(n):
            copy.wait_recv()
        self.ca(n).start()

    def xa_done(self, n):
        self.xa(n).wait_recv()
        self.ca(n).start()

    def ca_done(self, n):
        self.ca(n).wait_recv()

    def drain(self, n):
        across = [] if self.wide else [self.xa(n)]
        for copy in across + [self.c(n, 0), self.c(n, 1), self.y(n), self.x(n), self.ca(n)] + self.z(n) + self.za(n):
            copy.wait_send()


def when(condition, body):
    if isinstance(condition, bool):
        if condition:
            body()
    else:
        pl.when(condition)(body)


ON_WEIGHTS = ("relay_x", "relay_c", "ready")
ON_GRADS = ("c_start", "c_done", "y_done", "x_done", "z_done", "za_done", "xa_done", "ca_done", "xza_done")
PLAN = {
    "norm_one": (),
    "qkv_own": (),
    "att_own": ((1, 0, (0,)), ),
    "widen_g": ((0, 0, (1,)), ),
    "pown": (),
    "qkv_other": ((0, 0, (2, 100, 3, 200,)), (1, 0, (101, 4, 201,)), (2, 0, (102, 5, 202,)), ),
    "att_other": ((0, 0, (103,)), (1, 0, (104, 6, 7,)), ),
    "proj": ((0, 0, (105, 8, 203,)), ),
    "updown": ((0, 0, (204,)), (0, 1, (9,)), (0, 2, (1000, 106,)), (1, 0, (10, 205,)), (1, 1, (107, 1100,)), (1, 2, (1001,)), (1, 3, (11,)), (2, 0, (108, 206,)), (2, 1, (1101,)), (2, 2, (1002,)), (2, 3, (109,)), (3, 0, (207,)), (3, 1, (1102, 110,)), (3, 2, (1003, 1200,)), ),
    "hbug": ((0, 0, (111, 208,)), (0, 1, (1103,)), (0, 2, (1004,)), (1, 0, (1201, 209,)), (1, 1, (1300,)), (1, 2, (1005, 1104,)), (2, 0, (210,)), (2, 1, (1202,)), (2, 2, (1006,)), (2, 3, (1301, 1105,)), (3, 0, (211,)), (3, 1, (1400,)), (3, 2, (1007, 1203,)), ),
    "sg": ((0, 0, (1302, 1106,)), (2, 0, (1401,)), (3, 0, (1204,)), ),
    "ntb": ((0, 0, (1500, 1303, 1107,)), ),
    "ob1": ((0, 0, (1402, 1205,)), ),
    "ob0": ((0, 0, (1008,)), ),
    "ab": ((0, 0, (1501, 1304,)), (1, 0, (1600, 1403, 1206, 1108,)), (2, 0, (1700, 1502, 1305,)), (3, 0, (1601, 1404, 1207,)), ),
    "qg3": ((0, 0, (1701, 1503, 1306,)), ),
    "qg0": ((0, 0, (1009,)), ),
    "qg4": ((0, 0, (1602, 1405, 1208,)), ),
    "qg1": ((0, 0, (1010, 1109,)), ),
    "qg5": ((0, 0, (1702, 1504, 1307,)), ),
    "qg2": ((0, 0, (1011, 1012, 1110,)), ),
    "fg": ((0, 0, (1603,)), (1, 0, (1406,)), (2, 0, (1111, 1703,)), (3, 0, (1308,)), ),
    "nob": ((0, 0, (1505,)), ),
    "mo": ((0, 0, (1013, 1604, 1209, 1112, 1407,)), (2, 0, (1704, 1113,)), (3, 0, (1506,)), ),
    "lo": ((0, 0, (1605, 1210,)), ),
    "tail": ((0, 0, (1408, 1705, 1309, 1211, 1507, 1606, 1212, 1706, 1213, 1310, 1508, 1311, 1409, 1607, 1312, 1707, 1313, 1410, 1608, 1411, 1708, 1509, 1412, 1413, 1510, 1609, 1811, 1709, 1711, 1812, 1610, 1813, 1712, 1710, 1713,)), ),
}


def kernel(caps, slots, pad, names_in, *all_refs):
    L = Layer(caps, slots, pad, dict(zip(names_in, all_refs)))
    peers = Peers()
    peers.greet()
    L.cap_base = peers.t * caps
    weights = Weights(peers, L.w, L.wsend, L.wrecv)
    big = Reduce(peers, (L.grads, L.cr, L.yr, L.xr, L.zr, L.f), 0, L.gsend, L.grecv)
    half = Reduce(peers, (L.hg, L.hcr, L.hyr, L.hxr, L.hzr, L.hf), BIG, L.gsend, L.grecv, wide=True)
    small = Reduce(peers, (L.sg, L.scr, L.syr, L.sxr, L.szr, L.sf), BIG + 2, L.gsend, L.grecv, wide=True)

    def at(stage, unit):
        if unit < BIG:
            getattr(big, stage)(unit)
        elif unit < BIG + 2:
            getattr(half, stage)(unit - BIG)
        else:
            getattr(small, stage)(0)

    def arrive(codes):
        for code in codes:
            stage, unit = code // 100, code % 100
            if stage < 10:
                getattr(weights, ON_WEIGHTS[stage])(unit)
            else:
                at(ON_GRADS[stage - 10], unit)

    def run(name, count, *parts):
        def body(i):
            for k, part in enumerate(parts):
                for when_i, when_k, codes in PLAN[name]:
                    if when_k == k:
                        when(i == when_i, functools.partial(arrive, codes))
                part(i)

        if count == 1:
            body(0)
        else:
            loop(count, body)

    local = []

    def load(a, b):
        copy = pltpu.make_async_copy(a, b, L.lsem.at[len(local)])
        copy.start()
        local.append(copy)

    for j in range(3):
        load(L.wqkv_a.at[j], L.w.at[j])
    for n in range(2):
        load(L.wo_a.at[:, pl.ds(n * 256, 256)], L.w.at[3, pl.ds(n * 256, 256)])
    load(L.tok, L.tok_v)
    for n in range(4):
        load(L.wu_a.at[:, pl.ds(n * 256, 256)], L.w.at[4 + n])
    for n in range(4):
        for k in range(2):
            load(L.wd_a.at[pl.ds(n * 256, 256), pl.ds(k * 256, 256)], L.w.at[8 + n, pl.ds(k * 256, 256)])
    load(L.cot, L.cot_v)
    for name in ("qvb", "ub", "ob", "db", "gains", "shifts", "lengths"):
        load(getattr(L, name + "_h"), getattr(L, name))
    local[5].wait()
    L.widen(L.tok_v, peers.t * caps * slots, L.xs)
    for copy in local[:5] + local[6:]:
        copy.wait()
    peers.meet()
    bias_send = [
        remote(L.qvb, L.qvb_b, L.bsem.at[0], L.bsem.at[1], peers.to_y),
        remote(L.ub, L.ub_b, L.bsem.at[2], L.bsem.at[3], peers.to_y),
    ]
    for copy in bias_send:
        copy.start()
    loop(UNITS, lambda u: weights.y(u).start())
    attend = lambda i: [L.attention(4 * i + k) for k in range(4)]

    def rows_and_biases():
        L.widen(L.cot_v, peers.t * caps * slots, L.g)
        for copy in bias_send:
            copy.wait()
        L.biases(1, L.qvb_b, L.ub_b)

    def input_rows():
        L.norm_one_back(L.dx_out)
        L.pack_small(L.sg.at[0])

    def output_rows():
        L.layer_out(L.stage, L.y_out)

    def own(part, unit):
        return lambda n: (part(n), big.c_start_own(unit + n))

    run("norm_one", 1, lambda i: (L.norm_one(), L.biases(0, L.qvb, L.ub)))
    run("qkv_own", 3, L.qkv)
    run("att_own", caps // 4, attend)
    run("widen_g", 1, lambda i: rows_and_biases())
    run("pown", 2, L.project_own)
    run("qkv_other", 3, lambda j: L.qkv(3 + j))
    run("att_other", caps // 4, lambda i: attend(caps // 4 + i))
    run("proj", 2, L.project)
    run("updown", 4, lambda n: L.up(4 + n), lambda n: L.down_grad(4 + n), L.up, own(L.down_grad, 0))
    run("hbug", 4, lambda n: L.hidden_back(4 + n), lambda n: L.up_grad(4 + n), L.hidden_back, own(L.up_grad, 4))
    run("sg", 4, L.second_grad)
    run("ntb", 1, lambda i: L.norm_two_back())
    run("ob1", 1, lambda i: L.out_back(1))
    run("ob0", 1, lambda i: (L.out_back(0), big.c_start_own(8)))
    run("ab", caps // 2, lambda i: [L.attention_back(4 * i + k) for k in range(4)])
    for j in range(3):
        run(f"qg{3 + j}", 1, lambda i: L.qkv_grad(3 + j))
        run(f"qg{j}", 1, lambda i: L.qkv_grad(j))
        for unit in (9 + j,) if j < 2 else (11, 12):
            at("c_start_own", unit)
    run("fg", 4, L.first_grad)
    run("nob", 1, lambda i: (input_rows(), small.c_start_own(0)))
    run("mo", 4, L.mlp_out)
    run("lo", 1, lambda i: output_rows())
    tail = PLAN["tail"][0][2]
    arrive(tail[:-FINAL])
    loop(UNITS, weights.drain)
    loop(6, big.drain)
    arrive(tail[-FINAL:])

    loop(BIG - 6, lambda n: big.drain(6 + n))
    loop(2, half.drain)
    small.drain(0)


def finish(f, hf, s, y, dx, y_out, dx_out, qkv, out, up, down, qvb, ob, ub, db, gg, sh, wide, v1, v2, v3, v4, v5, v6, sem_out, sem_io):
    io = []

    def send(a, b, sem):
        copy = pltpu.make_async_copy(a, b, sem)
        copy.start()
        io.append(copy)

    send(y, y_out, sem_io.at[0])
    send(dx, dx_out, sem_io.at[1])

    def row(first, count):
        return jnp.concatenate([s[0, first + i : first + i + 1, :] for i in range(count)], axis=1)

    for n in range(UNITS):
        if n < BIG:
            wide[n] = f[n].astype(F32)
        else:
            for k in range(2):
                wide[n, k * 256 : (k + 1) * 256, :] = hf[k].astype(F32)
        if n < 4 or n == 8:
            for k in range(2):
                c = pl.ds(k * 256, 256)
                send(wide.at[n, c], down.at[pl.ds(n * 256, 256), c] if n < 4 else out.at[:, c], sem_out.at[2 * n + k])
        elif n < 8:
            send(wide.at[n], up.at[:, pl.ds((n - 4) * 256, 256)], sem_out.at[2 * n])
        else:
            send(wide.at[n], qkv.at[n - 9], sem_out.at[2 * n])
        if n == 1:
            v1[0:1, :], v1[1:2, :] = row(0, 2), row(2, 2)
            v3[...] = row(4, 8)
            v2[...], v4[...] = row(12, 4), row(16, 4)
            v5[0:1, :], v5[1:2, :] = row(20, 4), row(24, 4)
            v6[0:1, :], v6[1:2, :] = row(28, 4), row(32, 4)
            for k, (a, b) in enumerate(((v1, qvb), (v2, ob), (v3, ub), (v4, db), (v5, gg), (v6, sh))):
                send(a, b, sem_io.at[2 + k])
    for copy in io:
        copy.wait()


def shards(depth, tokens, lengths, qkv_weight, qv_bias, out_weight, out_bias, up_weight, up_bias, down_weight, down_bias, norm_gain, norm_shift, cotangent):
    total, width = tokens.shape
    count = lengths.shape[0]
    slots = total // count
    caps = count // 2
    pad = (slots + 15) // 16 * 16
    rws = caps * pad
    V = pl.BlockSpec(memory_space=pltpu.VMEM)
    A = pl.BlockSpec(memory_space=pl.ANY)
    ins = [
        ("tok", tokens, A), ("cot", cotangent, A), ("lengths_h", lengths, A),
        ("wqkv_a", qkv_weight, A), ("wo_a", out_weight, A), ("wu_a", up_weight, A), ("wd_a", down_weight, A),
        ("qvb_h", qv_bias, A), ("ub_h", up_bias, A),
        ("ob_h", out_bias, A), ("db_h", down_bias, A), ("gains_h", norm_gain, A), ("shifts_h", norm_shift, A),
    ]
    outs = [
        ("y_out", (caps * slots, 512), BF16), ("dx_out", (caps * slots, 512), F32),
        ("f", (BIG, 512, 256), BF16), ("hf", (2, 256, 256), BF16), ("sf", (1, 128, 128), F32),
    ]
    vm = pltpu.VMEM
    sems = UNITS + 2, 3 + 3 * depth
    held = [("qvb", qv_bias), ("ub", up_bias), ("ob", out_bias), ("db", down_bias), ("gains", norm_gain), ("shifts", norm_shift)]
    scr = [(n, vm(v.shape, v.dtype)) for n, v in held] + [
        ("lengths", pltpu.SMEM(lengths.shape, jnp.int32)),
        ("tok_v", vm((total, 512), BF16)), ("cot_v", vm((total, 512), BF16)),
        ("stage", vm((total + 16, 512), F32)), ("xs", vm((rws, 512), BF16)), ("g", vm((rws, 512), BF16)),
        ("n1", vm((rws, 512), F32)), ("r1", vm((rws, 128), F32)), ("a1", vm((rws, 512), BF16)),
        ("w", vm((2 * UNITS, 512, 256), BF16)), ("qvb_b", vm((2, 256), BF16)), ("ub_b", vm(up_bias.shape, BF16)),
        ("bias_qkv", vm((6, 1, 256), F32)), ("bias_up", vm((8, 1, 256), F32)),
        ("pqkv", vm((6, rws, 256), BF16)), ("probs", vm((2 * caps, 4 * pad, pad), F32)), ("ctx", vm((2, rws, 256), BF16)),
        ("h1", vm((rws, 512), F32)), ("n2", vm((rws, 512), F32)), ("r2", vm((rws, 128), F32)), ("a2", vm((rws, 512), BF16)),
        ("hid", vm((8, rws, 256), BF16)), ("act", vm((8, rws, 256), F32)), ("du", vm((8, rws, 256), BF16)),
        ("e", vm((rws, 512), F32)), ("dob", vm((rws, 512), BF16)),
        ("dqkv", vm((6, rws, 256), BF16)),
        ("small", vm((8, 512), F32)), ("small_up", vm((8, 1, 256), F32)), ("small_qkv", vm((6, 1, 256), F32)),
        ("grads", vm((BIG, 2, 512, 256), BF16)), ("cr", vm((BIG, 2, 256, 256), BF16)), ("yr", vm((BIG, 256, 256), BF16)),
        ("xr", vm((BIG, 128, 256), BF16)), ("zr", vm((BIG, depth - 1, 128 // depth, 256), BF16)),
        ("hg", vm((2, 2, 256, 256), BF16)), ("hcr", vm((2, 2, 128, 256), BF16)), ("hyr", vm((2, 128, 256), BF16)),
        ("hxr", vm((2, 64, 256), BF16)), ("hzr", vm((2, depth - 1, 64 // depth, 256), BF16)),
        ("sg", vm((1, 2, 128, 128), F32)), ("scr", vm((1, 2, 64, 128), F32)), ("syr", vm((1, 64, 128), F32)),
        ("sxr", vm((1, 32, 128), F32)), ("szr", vm((1, depth - 1, 32 // depth, 128), F32)),
        ("lsem", pltpu.SemaphoreType.DMA((28,))), ("bsem", pltpu.SemaphoreType.DMA((4,))),
        ("wsend", pltpu.SemaphoreType.DMA((UNITS, 3))), ("wrecv", pltpu.SemaphoreType.DMA((UNITS, 3))),
        ("gsend", pltpu.SemaphoreType.DMA(sems)), ("grecv", pltpu.SemaphoreType.DMA(sems)),
    ]
    names = [n for n, _, _ in ins] + [n for n, _, _ in outs] + [n for n, _ in scr]
    y, dx, f, hf, s = pl.pallas_call(
        functools.partial(kernel, caps, slots, pad, names),
        out_shape=[vm(s, d) for _, s, d in outs],
        in_specs=[s for _, _, s in ins],
        out_specs=[V] * len(outs),
        scratch_shapes=[s for _, s in scr],
        compiler_params=pltpu.CompilerParams(vmem_limit_bytes=VLIM, collective_id=0, has_side_effects=True),
        name="layer",
    )(*[v for _, v, _ in ins])
    results = [
        (y.shape, BF16, A), (dx.shape, F32, A), (qkv_weight.shape, F32, A), (out_weight.shape, F32, A),
        (up_weight.shape, F32, A), (down_weight.shape, F32, A),
        (qv_bias.shape, F32, A), ((1, 512), F32, A), ((1, up_bias.shape[0]), F32, A), ((1, 512), F32, A), ((2, 512), F32, A), ((2, 512), F32, A),
    ]
    y, dx, qkv, out, up, down, qvb, ob, ub, db, gg, sh = pl.pallas_call(
        finish,
        out_shape=[jax.ShapeDtypeStruct(s, d) for s, d, _ in results],
        in_specs=[V] * 5,
        out_specs=[s for _, _, s in results],
        scratch_shapes=[
            vm((UNITS, 512, 256), F32), *[vm(s, F32) for s, _, _ in results[6:]], pltpu.SemaphoreType.DMA((2 * UNITS,)), pltpu.SemaphoreType.DMA((8,)),
        ],
        compiler_params=pltpu.CompilerParams(vmem_limit_bytes=12 << 20),
        name="finish",
    )(*[pltpu.with_memory_space_constraint(v, pltpu.VMEM) for v in (f, hf, s, y, dx)])
    return y, dx, qkv, qvb, out, ob[0], up, ub[0], down, db[0], gg, sh


def matmul_plain(left, right):
    return jnp.dot(left, right, preferred_element_type=jnp.float32)


def contract_rows(left, right):
    return lax.dot_general(
        left, right, (((0,), (0,)), ((), ())), preferred_element_type=jnp.float32
    )


def contract_cols(left, right):
    return lax.dot_general(
        left, right, (((1,), (1,)), ((), ())), preferred_element_type=jnp.float32
    )


def plain_norm_stats(values):
    center = values - jnp.mean(values, axis=-1, keepdims=True)
    inv_std = lax.rsqrt(jnp.mean(center * center, axis=-1, keepdims=True) + EPSILON)
    return (center * inv_std, inv_std)


def plain_norm_back(upstream, normed, inv_std, gain_vec):
    scaled = upstream * gain_vec
    inner_mean = jnp.mean(scaled * normed, axis=-1, keepdims=True)
    result = inv_std * (scaled - jnp.mean(scaled, axis=-1, keepdims=True) - normed * inner_mean)
    return (result, jnp.sum(upstream * normed, axis=0), jnp.sum(upstream, axis=0))


def row_slice(values, row_start, share_rows):
    return lax.dynamic_slice_in_dim(values, row_start, share_rows, 0)


def shards_by_heads(
    tokens,
    lengths,
    qkv_weight,
    qv_bias,
    out_weight,
    out_bias,
    up_weight,
    up_bias,
    down_weight,
    down_bias,
    norm_gain,
    norm_shift,
    cotangent,
):
    tensor_count = lax.axis_size("tensor")
    tensor_index = lax.axis_index("tensor")
    share_rows = tokens.shape[0] // tensor_count
    row_start = tensor_index * share_rows
    gains = norm_gain.astype(jnp.float32)
    shifts = norm_shift.astype(jnp.float32)
    total_rows = tokens.shape[0]
    count = lengths.shape[0]
    slots = total_rows // count
    local_width = qkv_weight.shape[2]
    local_heads = local_width // HD
    score_scale = HD ** (-0.5)
    qv_float = qv_bias.astype(jnp.float32)
    token_f = tokens.astype(jnp.float32)
    normed_one, inv_one = plain_norm_stats(token_f)
    first_in = (normed_one * gains[0] + shifts[0]).astype(jnp.bfloat16)
    queries = (matmul_plain(first_in, qkv_weight[0]) + qv_float[0]).astype(jnp.bfloat16)
    keys_all = matmul_plain(first_in, qkv_weight[1]).astype(jnp.bfloat16)
    values_all = (matmul_plain(first_in, qkv_weight[2]) + qv_float[1]).astype(jnp.bfloat16)
    shape4 = (count, slots, local_heads, HD)
    query_four = queries.reshape(shape4)
    key_four = keys_all.reshape(shape4)
    value_four = values_all.reshape(shape4)
    position = jnp.arange(slots)
    allowed = (position[None, :] <= position[:, None])[None, :, :] & (
        position[None, None, :] < lengths[:, None, None]
    )
    allowed = allowed[:, None, :, :]

    def masked_scores():
        raw = jnp.einsum(
            "cihd,cjhd->chij", query_four, key_four, preferred_element_type=jnp.float32
        )
        return jnp.where(allowed, raw * score_scale, -1e30)

    scores = masked_scores()
    row_max = jnp.max(scores, axis=-1, keepdims=True)
    log_total = row_max + jnp.log(jnp.sum(jnp.exp(scores - row_max), axis=-1, keepdims=True))
    probs_low = jnp.exp(scores - log_total).astype(jnp.bfloat16)
    context = jnp.einsum(
        "chij,cjhd->cihd", probs_low, value_four, preferred_element_type=jnp.float32
    )
    context = context.reshape(total_rows, local_width).astype(jnp.bfloat16)
    attn_part = matmul_plain(context, out_weight)
    attn_out = lax.psum(attn_part, "tensor") + out_bias.astype(jnp.float32)
    hidden_res = token_f + attn_out
    normed_two, inv_two = plain_norm_stats(hidden_res)
    second_in = (normed_two * gains[1] + shifts[1]).astype(jnp.bfloat16)
    upper = matmul_plain(second_in, up_weight) + up_bias.astype(jnp.float32)
    sigma = jax.nn.sigmoid(1.702 * upper)
    hidden = (upper * sigma).astype(jnp.bfloat16)
    mlp_part = matmul_plain(hidden, down_weight)
    result_rows = (
        hidden_res
        + lax.psum(mlp_part.astype(jnp.bfloat16), "tensor").astype(jnp.float32)
        + down_bias.astype(jnp.float32)
    )
    layer_out = row_slice(result_rows, row_start, share_rows).astype(jnp.bfloat16)
    grad_f = cotangent.astype(jnp.float32)
    down_grad = contract_rows(hidden, cotangent)
    down_bias_grad = jnp.sum(grad_f, axis=0)
    hidden_grad = contract_cols(cotangent, down_weight)
    upper_grad = (hidden_grad * (sigma + 1.702 * upper * sigma * (1.0 - sigma))).astype(
        jnp.bfloat16
    )
    up_grad = contract_rows(second_in, upper_grad)
    up_bias_grad = jnp.sum(upper_grad.astype(jnp.float32), axis=0)
    second_part = contract_cols(upper_grad, up_weight)
    second_grad = lax.psum(second_part, "tensor")
    residual_back, gain_two, shift_two = plain_norm_back(second_grad, normed_two, inv_two, gains[1])
    residual_full = grad_f + residual_back
    branch_grad = residual_full.astype(jnp.bfloat16)
    out_bias_grad = jnp.sum(branch_grad.astype(jnp.float32), axis=0)
    out_grad = contract_rows(context, branch_grad)
    context_grad = contract_cols(branch_grad, out_weight).astype(jnp.bfloat16).reshape(shape4)
    probs = jnp.exp(masked_scores() - log_total)
    probs_low = probs.astype(jnp.bfloat16)
    value_grad = jnp.einsum(
        "chij,cihd->cjhd", probs_low, context_grad, preferred_element_type=jnp.float32
    )
    prob_grad = jnp.einsum(
        "cihd,cjhd->chij", context_grad, value_four, preferred_element_type=jnp.float32
    )
    score_grad = probs * (prob_grad - jnp.sum(prob_grad * probs, axis=-1, keepdims=True))
    score_grad = score_grad.astype(jnp.bfloat16)
    query_grad = (
        jnp.einsum("chij,cjhd->cihd", score_grad, key_four, preferred_element_type=jnp.float32)
        * score_scale
    )
    key_grad = (
        jnp.einsum("chij,cihd->cjhd", score_grad, query_four, preferred_element_type=jnp.float32)
        * score_scale
    )
    query_grad = query_grad.reshape(total_rows, local_width).astype(jnp.bfloat16)
    key_grad = key_grad.reshape(total_rows, local_width).astype(jnp.bfloat16)
    value_grad = value_grad.reshape(total_rows, local_width).astype(jnp.bfloat16)
    qkv_grad = jnp.stack(
        [
            contract_rows(first_in, query_grad),
            contract_rows(first_in, key_grad),
            contract_rows(first_in, value_grad),
        ]
    )
    qv_bias_grad = jnp.stack(
        [
            jnp.sum(query_grad.astype(jnp.float32), axis=0),
            jnp.sum(value_grad.astype(jnp.float32), axis=0),
        ]
    )
    first_part = (
        contract_cols(query_grad, qkv_weight[0])
        + contract_cols(key_grad, qkv_weight[1])
        + contract_cols(value_grad, qkv_weight[2])
    )
    first_grad = lax.psum(first_part.astype(jnp.bfloat16), "tensor").astype(jnp.float32)
    input_back, gain_one, shift_one = plain_norm_back(first_grad, normed_one, inv_one, gains[0])
    input_grad = row_slice(residual_full + input_back, row_start, share_rows)
    gain_grads = jnp.stack([gain_one, gain_two])
    shift_grads = jnp.stack([shift_one, shift_two])
    summed = (
        lax.psum(qkv_grad.astype(jnp.bfloat16), "dp").astype(jnp.float32),
        lax.psum(qv_bias_grad.astype(jnp.bfloat16), "dp").astype(jnp.float32),
        lax.psum(out_grad.astype(jnp.bfloat16), "dp").astype(jnp.float32),
        lax.psum(out_bias_grad.astype(jnp.bfloat16), "dp").astype(jnp.float32),
        lax.psum(up_grad.astype(jnp.bfloat16), "dp").astype(jnp.float32),
        lax.psum(up_bias_grad.astype(jnp.bfloat16), "dp").astype(jnp.float32),
        lax.psum(down_grad.astype(jnp.bfloat16), "dp").astype(jnp.float32),
        lax.psum(down_bias_grad.astype(jnp.bfloat16), "dp").astype(jnp.float32),
        lax.psum(gain_grads.astype(jnp.bfloat16), "dp").astype(jnp.float32),
        lax.psum(shift_grads.astype(jnp.bfloat16), "dp").astype(jnp.float32),
    )
    return (
        layer_out,
        input_grad,
        summed[0],
        summed[1],
        summed[2],
        summed[3],
        summed[4],
        summed[5],
        summed[6],
        summed[7],
        summed[8],
        summed[9],
    )


def solution(mesh):
    dp, tensor = mesh.shape["dp"], mesh.shape["tensor"]
    if tensor == 2 and dp == 16:
        body = functools.partial(shards, dp // 4)
    else:
        body = shards_by_heads
    return jax.shard_map(
        body,
        mesh=mesh,
        in_specs=(P("dp", None), P("dp"), P(None, None, "tensor"), P(None, "tensor"), P("tensor", None), P(), P(None, "tensor"), P("tensor"), P("tensor", None), P(), P(), P(), P("dp", None)),
        out_specs=(P(("dp", "tensor"), None), P(("dp", "tensor"), None), P(None, None, "tensor"), P(None, "tensor"), P("tensor", None), P(), P(None, "tensor"), P("tensor"), P("tensor", None), P(), P(), P()),
        check_vma=False,
    )
```

```python
import functools

import jax
import jax.numpy as jnp
from jax import lax
from jax.experimental import pallas as pl
from jax.experimental.pallas import tpu as pltpu
from jax.sharding import PartitionSpec as P

HD = 64
EPSILON = 1e-05
F32 = jnp.float32
BF16 = jnp.bfloat16
LOG2E = 1.4426950408889634
UNITS = 12
BIG = 11
FINAL = 9
VLIM = 54 << 20
MESH = pl.DeviceIdType.MESH


def nn(left, right):
    return lax.dot_general(left, right, (((1,), (0,)), ((), ())), preferred_element_type=F32)


def nt(left, right):
    return lax.dot_general(left, right, (((1,), (1,)), ((), ())), preferred_element_type=F32)


def tn(left, right):
    return lax.dot_general(left, right, (((0,), (0,)), ((), ())), preferred_element_type=F32)


def loop(count, body):
    lax.fori_loop(0, count, lambda i, c: (body(i), c)[1], 0)


def norm(rows):
    center = rows - jnp.mean(rows, axis=-1, keepdims=True)
    inv = lax.rsqrt(jnp.mean(center * center, axis=-1, keepdims=True) + EPSILON)
    return center * inv, inv


def norm_back(grad, normed, inv, gain):
    t = grad * gain
    inner = jnp.mean(t * normed, axis=-1, keepdims=True)
    return inv * (t - jnp.mean(t, axis=-1, keepdims=True) - normed * inner)


def colsum(x):
    return jnp.sum(x, axis=0, keepdims=True)


class Layer:
    def __init__(self, caps, slots, pad, refs):
        self.caps, self.slots, self.pad = caps, slots, pad
        self.rows = caps * pad
        self.__dict__.update(refs)

    def head_mask(self, h, rows):
        lane = lax.broadcasted_iota(jnp.int32, (rows, 256), 1)
        return (lane >= h * HD) & (lane < (h + 1) * HD)

    def stack(self, block):
        parts = []
        for h in range(4):
            parts.append(jnp.where(self.head_mask(h, self.pad), block, jnp.zeros_like(block)))
        return jnp.concatenate(parts, axis=0)

    def unstack(self, block):
        out = None
        for h in range(4):
            part = block[h * self.pad : (h + 1) * self.pad]
            out = part if out is None else jnp.where(self.head_mask(h, self.pad), part, out)
        return out

    def widen(self, src, base, dst):
        total = src.shape[0]
        tile = self.slots * 2 if total % (self.slots * 2) == 0 else self.slots
        tile = 176 if total % 176 == 0 else total
        def conv(i):
            r = pl.ds(pl.multiple_of(i * tile, 16), tile)
            self.stage[r, :] = src[r, :].astype(F32)
        loop(total // tile, conv)
        self.stage[total : total + 16, :] = jnp.zeros((16, self.stage.shape[1]), F32)
        for c in range(self.caps):
            off = c * self.slots
            low = off // 8 * 8
            v = self.stage[pl.ds(pl.multiple_of(base + low, 8), self.pad + 8), :]
            v = v[off - low : off - low + self.pad]
            row = lax.broadcasted_iota(jnp.int32, v.shape, 0)
            v = jnp.where(row < self.slots, v, 0.0)
            dst[c * self.pad : (c + 1) * self.pad, :] = v.astype(BF16)

    def crows(self, c):
        return pl.ds(pl.multiple_of(c * self.pad, self.pad), self.pad)

    def norm_one(self):
        gain, shift = self.gains[0:1, :].astype(F32), self.shifts[0:1, :].astype(F32)
        def cap(c):
            r = self.crows(c)
            n, inv = norm(self.xs[r, :].astype(F32))
            self.n1[r, :] = n
            self.r1[r, :] = jnp.broadcast_to(inv, (self.pad, 128))
            self.a1[r, :] = (n * gain + shift).astype(BF16)
        loop(self.caps, cap)

    def biases(self, s, qvb, ub):
        for j in range(3):
            if j == 1:
                self.bias_qkv[s * 3 + j] = jnp.zeros((1, 256), F32)
            else:
                self.bias_qkv[s * 3 + j] = qvb[j // 2 : j // 2 + 1, :].astype(F32)
        up = ub[...].astype(F32).reshape(1, -1)
        for n in range(4):
            self.bias_up[s * 4 + n] = up[:, n * 256 : (n + 1) * 256]

    def qkv(self, i):
        s, j = i // 3, lax.rem(i, 3)
        out = nn(self.a1[...], self.w[s * UNITS + j]) + self.bias_qkv[i]
        self.pqkv[i] = out.astype(BF16)

    def attention(self, i):
        s, c = i // self.caps, lax.rem(i, self.caps)
        r = self.crows(c)
        scores = nt(self.stack(self.pqkv[s * 3, r, :]), self.pqkv[s * 3 + 1, r, :])
        length = self.lengths[self.cap_base + c]
        ii = lax.broadcasted_iota(jnp.int32, (self.pad, self.pad), 0)
        jj = lax.broadcasted_iota(jnp.int32, (self.pad, self.pad), 1)
        allowed = (jj <= ii) & (jj < length)
        blocks = []
        for h in range(4):
            blk = jnp.where(allowed, scores[h * self.pad : (h + 1) * self.pad], -1e30)
            top = jnp.max(blk, axis=1, keepdims=True)
            e = jnp.exp2((blk - top) * (HD**-0.5 * LOG2E))
            blocks.append(e * (1.0 / jnp.sum(e, axis=1, keepdims=True)))
        p = jnp.concatenate(blocks, axis=0)
        self.probs[i] = p
        self.ctx[s, r, :] = self.unstack(nn(p.astype(BF16), self.pqkv[s * 3 + 2, r, :])).astype(BF16)

    def attention_back(self, i):
        s, c = i // self.caps, lax.rem(i, self.caps)
        r = self.crows(c)
        q = self.stack(self.pqkv[s * 3, r, :])
        d = self.stack(self.ctx[s, r, :])
        p = self.probs[i]
        self.dqkv[s * 3 + 2, r, :] = tn(p.astype(BF16), d).astype(BF16)
        dp = nt(d, self.pqkv[s * 3 + 2, r, :])
        ds = (p * (dp - jnp.sum(dp * p, axis=1, keepdims=True))).astype(BF16)
        self.dqkv[s * 3 + 1, r, :] = (tn(ds, q) * HD**-0.5).astype(BF16)
        self.dqkv[s * 3, r, :] = (self.unstack(nn(ds, self.pqkv[s * 3 + 1, r, :])) * HD**-0.5).astype(BF16)

    def half_rows(self, i):
        tile = self.rows // 2
        return pl.ds(pl.multiple_of(i * tile, 16), tile)

    def out_product(self, slot, r):
        c = self.ctx[slot, r, :]
        return jnp.concatenate([nn(c, self.w[slot * UNITS + 3, k * 256 : (k + 1) * 256, :]) for k in range(2)], axis=1)

    def project_own(self, i):
        r = self.half_rows(i)
        self.h1[r, :] = self.xs[r, :].astype(F32) + self.out_product(0, r) + self.ob[...].astype(F32).reshape(1, -1)

    def project(self, i):
        r = self.half_rows(i)
        gain, shift = self.gains[1:2, :].astype(F32), self.shifts[1:2, :].astype(F32)
        h1 = self.h1[r, :] + self.out_product(1, r)
        self.h1[r, :] = h1
        n, inv = norm(h1)
        self.n2[r, :] = n
        self.r2[r, :] = jnp.broadcast_to(inv, (n.shape[0], 128))
        self.a2[r, :] = (n * gain + shift).astype(BF16)

    def wup(self, m):
        return (m // 4) * UNITS + 4 + lax.rem(m, 4)

    def wdown(self, m):
        return (m // 4) * UNITS + 8 + lax.rem(m, 4)

    def up(self, m):
        u = nn(self.a2[...], self.w[self.wup(m)]) + self.bias_up[m]
        sg = 0.5 * jnp.tanh(0.851 * u) + 0.5
        h = u * sg
        self.hid[m] = h.astype(BF16)
        self.act[m] = sg + 1.702 * h * (1.0 - sg)

    def down_grad(self, m):
        w = tn(self.hid[m], self.g[...]).astype(BF16)
        s, n = m // 4, lax.rem(m, 4)
        self.grads[n, s, 0:256, :] = w[:, :256]
        self.grads[n, s, 256:512, :] = w[:, 256:]

    def hidden_back(self, m):
        w = self.wdown(m)
        back = nt(self.g[:, 0:256], self.w[w, 0:256, :]) + nt(self.g[:, 256:512], self.w[w, 256:512, :])
        du = (back * self.act[m]).astype(BF16)
        self.du[m] = du
        self.small_up[m] = colsum(du.astype(F32))

    def up_grad(self, m):
        s, n = m // 4, lax.rem(m, 4)
        self.grads[4 + n, s] = tn(self.a2[...], self.du[m]).astype(BF16)

    def half_tile(self, i):
        tile = self.rows // 2
        r = pl.ds(pl.multiple_of((i // 2) * tile, 16), tile)
        return r, lax.rem(i, 2)

    def second_grad(self, i):
        r, n = self.half_tile(i)
        w = pl.ds(pl.multiple_of(n * 256, 256), 256)
        acc = None
        for m in range(8):
            part = nt(self.du[m, r, :], self.w[(m // 4) * UNITS + 4 + m % 4, w, :])
            acc = part if acc is None else acc + part
        self.e[r, w] = acc

    def mlp_out(self, i):
        r, n = self.half_tile(i)
        w = pl.ds(pl.multiple_of(n * 256, 256), 256)
        acc = self.h1[r, w] + self.db[w].astype(F32).reshape(1, -1)
        for m in range(8):
            acc = acc + nn(self.hid[m, r, :], self.w[(m // 4) * UNITS + 8 + m % 4, w, :])
        self.h1[r, w] = acc

    def norm_two_back(self):
        gain = self.gains[1:2, :].astype(F32)
        zero = jnp.zeros((1, gain.shape[1]), F32)
        def cap(c, carry):
            gg, sg, ob, db = carry
            r = self.crows(c)
            e, n, g = self.e[r, :], self.n2[r, :], self.g[r, :].astype(F32)
            dh = g + norm_back(e, n, self.r2[r, 0:1], gain)
            self.n2[r, :] = dh
            dob = dh.astype(BF16)
            self.dob[r, :] = dob
            return (gg + colsum(e * n), sg + colsum(e), ob + colsum(dob.astype(F32)), db + colsum(g))
        gg, sg, ob, db = lax.fori_loop(0, self.caps, cap, (zero, zero, zero, zero))
        self.small[1:2, :], self.small[3:4, :], self.small[4:5, :], self.small[5:6, :] = gg, sg, ob, db

    def out_back(self, s):
        w = tn(self.ctx[s], self.dob[...]).astype(BF16)
        self.grads[8, s, 0:256, :] = w[:, :256]
        self.grads[8, s, 256:512, :] = w[:, 256:]
        wo = s * UNITS + 3
        back = nt(self.dob[:, 0:256], self.w[wo, 0:256, :]) + nt(self.dob[:, 256:512], self.w[wo, 256:512, :])
        self.ctx[s] = back.astype(BF16)

    def qkv_grad(self, i):
        s, j = i // 3, i % 3
        d = self.dqkv[i]
        w = tn(self.a1[...], d).astype(BF16)
        if j < 2:
            self.grads[9 + j, s] = w
        else:
            self.hg[0, s], self.hg[1, s] = w[:256], w[256:]
        self.small_qkv[i] = colsum(d.astype(F32))

    def first_grad(self, i):
        r, n = self.half_tile(i)
        w = pl.ds(pl.multiple_of(n * 256, 256), 256)
        acc = None
        for m in range(6):
            part = nt(self.dqkv[m, r, :], self.w[(m // 3) * UNITS + m % 3, w, :])
            acc = part if acc is None else acc + part
        self.e[r, w] = acc

    def norm_one_back(self, out):
        gain = self.gains[0:1, :].astype(F32)
        zero = jnp.zeros((1, gain.shape[1]), F32)
        gg, sg = zero, zero
        for c in range(self.caps):
            r = slice(c * self.pad, (c + 1) * self.pad)
            e, n = self.e[r, :], self.n1[r, :]
            dx = self.n2[r, :] + norm_back(e, n, self.r1[r, 0:1], gain)
            out[c * self.slots : (c + 1) * self.slots, :] = dx[: self.slots]
            gg, sg = gg + colsum(e * n), sg + colsum(e)
        self.small[0:1, :], self.small[2:3, :] = gg, sg

    def layer_out(self, flat, out):
        for c in range(self.caps):
            flat[c * self.slots : (c + 1) * self.slots, :] = self.h1[c * self.pad : c * self.pad + self.slots, :]
        out[...] = flat[0 : self.caps * self.slots, :].astype(BF16)

    def pack_small(self, out):
        def put(slot, row, value):
            for i in range(value.shape[1] // 128):
                out[slot, row + i : row + i + 1, :] = value[:, i * 128 : (i + 1) * 128]
        for slot in range(2):
            out[slot] = jnp.zeros(out.shape[1:], F32)
            put(slot, 0, self.small_qkv[slot * 3])
            put(slot, 2, self.small_qkv[slot * 3 + 2])
            for n in range(4):
                put(slot, 4 + 2 * n, self.small_up[slot * 4 + n])
            for i, k in enumerate((4, 5, 0, 1, 2, 3)):
                put(slot, 12 + 4 * i, self.small[k : k + 1, :])


class Peers:
    def __init__(self):
        dp, t = lax.axis_index("dp"), lax.axis_index("tensor")
        depth = lax.axis_size("dp") // 4
        self.core = lax.rem(dp, 2)
        self.x = lax.rem(dp // 2, 2)
        self.z = dp // 4
        self.t = t
        self.to_y = (dp, 1 - t)
        self.to_x = (dp + 2 - 4 * self.x, t)
        self.to_core = (dp + 1 - 2 * self.core, t)
        self.depth = depth
        self.to_z = [(lax.rem(self.z + k, depth) * 4 + lax.rem(dp, 4), t) for k in range(1, depth)]
        self.z_of = [lax.rem(self.z + k, depth) for k in range(1, depth)]
        self.to_far = [(z * 4 + (1 - self.x) * 2 + self.core, t) for z in self.z_of]

    def all(self):
        return [self.to_y, self.to_x, self.to_core] + self.to_z + self.to_far

    def greet(self):
        barrier = pltpu.get_barrier_semaphore()
        for peer in self.all():
            pl.semaphore_signal(barrier, inc=1, device_id=peer, device_id_type=MESH)

    def meet(self):
        pl.semaphore_wait(pltpu.get_barrier_semaphore(), len(self.all()))


def rows(index, size):
    return pl.ds(pl.multiple_of(index * size, size), size)


def remote(src, dst, send, recv, peer):
    return pltpu.make_async_remote_copy(src_ref=src, dst_ref=dst, send_sem=send, recv_sem=recv, device_id=peer, device_id_type=MESH)


class Weights:
    def __init__(self, peers, w, send, recv):
        self.p, self.w, self.send, self.recv = peers, w, send, recv
        self.quarter = peers.core * 2 + peers.x
        self.size = w.shape[1] // 4

    def y(self, u):
        r = rows(self.quarter, self.size)
        return remote(self.w.at[u, r], self.w.at[UNITS + u, r], self.send.at[u, 0], self.recv.at[u, 0], self.p.to_y)

    def x(self, u):
        part = self.w.at[UNITS + u, rows(self.quarter, self.size)]
        return remote(part, part, self.send.at[u, 1], self.recv.at[u, 1], self.p.to_x)

    def c(self, u):
        part = self.w.at[UNITS + u, rows(self.p.core, self.size * 2)]
        return remote(part, part, self.send.at[u, 2], self.recv.at[u, 2], self.p.to_core)

    def relay_x(self, u):
        self.y(u).wait_recv()
        self.x(u).start()

    def relay_c(self, u):
        self.x(u).wait_recv()
        self.c(u).start()

    def ready(self, u):
        self.c(u).wait_recv()

    def drain(self, u):
        self.y(u).wait_send()
        self.x(u).wait_send()
        self.c(u).wait_send()


class Reduce:
    def __init__(self, peers, refs, sem0, send, recv, wide=False):
        self.p = peers
        self.wide = wide
        self.g, self.cr, self.yr, self.xr, self.zr, self.f = refs
        self.sem0, self.send, self.recv = sem0, send, recv
        self.count = self.g.shape[0]
        self.full = self.g.shape[2]
        self.half, self.quarter = self.full // 2, self.full // 4
        self.shard = self.quarter // peers.depth

    def sems(self, n, k):
        return self.send.at[self.sem0 + n, k], self.recv.at[self.sem0 + n, k]

    def c(self, n, slot):
        theirs = self.g.at[n, slot, rows(1 - self.p.core, self.half)]
        return remote(theirs, self.cr.at[n, slot], *self.sems(n, (5 + 2 * self.p.depth - 2) if slot == 0 else 0), self.p.to_core)

    def y(self, n):
        return remote(self.cr.at[n, 1], self.yr.at[n], *self.sems(n, 1), self.p.to_y)

    def x(self, n):
        return remote(self.cr.at[n, 0, rows(1 - self.p.x, self.quarter)], self.xr.at[n], *self.sems(n, 2), self.p.to_x)

    def z(self, n):
        return [
            remote(
                self.cr.at[n, 0, pl.ds(pl.multiple_of(self.p.x * self.quarter + self.p.z_of[k] * self.shard, self.shard), self.shard)],
                self.zr.at[n, k],
                *self.sems(n, 5 + k),
                self.p.to_z[k],
            )
            for k in range(self.p.depth - 1)
        ]

    def own_shard(self):
        p = self.p
        return pl.ds(pl.multiple_of(p.core * self.half + p.x * self.quarter + p.z * self.shard, self.shard), self.shard)

    def za(self, n):
        part = self.f.at[n, self.own_shard()]
        depth = self.p.depth
        copies = [remote(part, part, *self.sems(n, 4 + depth + k), self.p.to_z[k]) for k in range(depth - 1)]
        if self.wide:
            copies.append(remote(part, part, *self.sems(n, 3), self.p.to_x))
            copies += [remote(part, part, *self.sems(n, 4 + 2 * depth + k), self.p.to_far[k]) for k in range(depth - 1)]
        return copies

    def xa(self, n):
        part = self.f.at[n, pl.ds(pl.multiple_of(self.p.core * self.half + self.p.x * self.quarter, self.quarter), self.quarter)]
        return remote(part, part, *self.sems(n, 3), self.p.to_x)

    def ca(self, n):
        part = self.f.at[n, rows(self.p.core, self.half)]
        return remote(part, part, *self.sems(n, 4), self.p.to_core)

    def c_start(self, n):
        self.c(n, 1).start()

    def c_start_own(self, n):
        self.c(n, 0).start()

    def c_done(self, n):
        self.c(n, 1).wait_recv()
        self.cr[n, 1] = self.cr[n, 1] + self.g[n, 1, rows(self.p.core, self.half), :]
        self.y(n).start()

    def y_done(self, n):
        self.c(n, 0).wait_recv()
        self.y(n).wait_recv()
        self.cr[n, 0] = self.cr[n, 0] + self.g[n, 0, rows(self.p.core, self.half), :] + self.yr[n]
        self.x(n).start()

    def x_done(self, n):
        self.x(n).wait_recv()
        r = rows(self.p.x, self.quarter)
        self.cr[n, 0, r, :] = self.cr[n, 0, r, :] + self.xr[n]
        for copy in self.z(n):
            copy.start()

    def z_done(self, n):
        for copy in self.z(n):
            copy.wait_recv()
        mine = pl.ds(pl.multiple_of(self.p.x * self.quarter + self.p.z * self.shard, self.shard), self.shard)
        total = self.cr[n, 0, mine, :].astype(F32)
        for k in range(self.p.depth - 1):
            total = total + self.zr[n, k].astype(F32)
        self.f[n, self.own_shard(), :] = total.astype(self.f.dtype)
        for copy in self.za(n):
            copy.start()

    def za_done(self, n):
        for copy in self.za(n):
            copy.wait_recv()
        self.xa(n).start()

    def xza_done(self, n):
        for copy in self.za(n):
            copy.wait_recv()
        self.ca(n).start()

    def xa_done(self, n):
        self.xa(n).wait_recv()
        self.ca(n).start()

    def ca_done(self, n):
        self.ca(n).wait_recv()

    def drain(self, n):
        across = [] if self.wide else [self.xa(n)]
        for copy in across + [self.c(n, 0), self.c(n, 1), self.y(n), self.x(n), self.ca(n)] + self.z(n) + self.za(n):
            copy.wait_send()


def when(condition, body):
    if isinstance(condition, bool):
        if condition:
            body()
    else:
        pl.when(condition)(body)


ON_WEIGHTS = ("relay_x", "relay_c", "ready")
ON_GRADS = ("c_start", "c_done", "y_done", "x_done", "z_done", "za_done", "xa_done", "ca_done", "xza_done")
PLAN = {
    "norm_one": (),
    "qkv_own": (),
    "att_own": ((1, 0, (0,)), ),
    "widen_g": ((0, 0, (1,)), ),
    "pown": (),
    "qkv_other": ((0, 0, (2, 100, 3, 200,)), (1, 0, (101, 4, 201,)), (2, 0, (102, 5, 202,)), ),
    "att_other": ((0, 0, (103,)), (1, 0, (104, 6, 7,)), ),
    "proj": ((0, 0, (105, 8, 203,)), ),
    "updown": ((0, 0, (204,)), (0, 1, (9,)), (0, 2, (1000, 106,)), (1, 0, (10, 205,)), (1, 1, (107, 1100,)), (1, 2, (1001,)), (1, 3, (11,)), (2, 0, (108, 206,)), (2, 1, (1101,)), (2, 2, (1002,)), (2, 3, (109,)), (3, 0, (207,)), (3, 1, (1102, 110,)), (3, 2, (1003, 1200,)), ),
    "hbug": ((0, 0, (111, 208,)), (0, 1, (1103,)), (0, 2, (1004,)), (1, 0, (1201, 209,)), (1, 1, (1300,)), (1, 2, (1005, 1104,)), (2, 0, (210,)), (2, 1, (1202,)), (2, 2, (1006,)), (2, 3, (1301, 1105,)), (3, 0, (211,)), (3, 1, (1400,)), (3, 2, (1007, 1203,)), ),
    "sg": ((0, 0, (1302, 1106,)), (2, 0, (1401,)), (3, 0, (1204,)), ),
    "ntb": ((0, 0, (1500, 1303, 1107,)), ),
    "ob1": ((0, 0, (1402, 1205,)), ),
    "ob0": ((0, 0, (1008,)), ),
    "ab": ((0, 0, (1501, 1304,)), (1, 0, (1600, 1403, 1206, 1108,)), (2, 0, (1700, 1502, 1305,)), (3, 0, (1601, 1404, 1207,)), ),
    "qg3": ((0, 0, (1701, 1503, 1306,)), ),
    "qg0": ((0, 0, (1009,)), ),
    "qg4": ((0, 0, (1602, 1405, 1208,)), ),
    "qg1": ((0, 0, (1010, 1109,)), ),
    "qg5": ((0, 0, (1702, 1504, 1307,)), ),
    "qg2": ((0, 0, (1011, 1012, 1110,)), ),
    "fg": ((0, 0, (1603,)), (1, 0, (1406,)), (2, 0, (1111, 1703,)), (3, 0, (1308,)), ),
    "nob": ((0, 0, (1505,)), ),
    "mo": ((0, 0, (1013, 1604, 1209, 1112, 1407,)), (2, 0, (1704, 1113,)), (3, 0, (1506,)), ),
    "lo": ((0, 0, (1605, 1210,)), ),
    "tail": ((0, 0, (1408, 1705, 1309, 1211, 1507, 1606, 1212, 1706, 1213, 1310, 1508, 1311, 1409, 1607, 1312, 1707, 1313, 1410, 1608, 1411, 1708, 1509, 1412, 1413, 1510, 1609, 1811, 1709, 1711, 1812, 1610, 1813, 1712, 1710, 1713,)), ),
}


def kernel(caps, slots, pad, names_in, *all_refs):
    L = Layer(caps, slots, pad, dict(zip(names_in, all_refs)))
    peers = Peers()
    peers.greet()
    L.cap_base = peers.t * caps
    weights = Weights(peers, L.w, L.wsend, L.wrecv)
    big = Reduce(peers, (L.grads, L.cr, L.yr, L.xr, L.zr, L.f), 0, L.gsend, L.grecv)
    half = Reduce(peers, (L.hg, L.hcr, L.hyr, L.hxr, L.hzr, L.hf), BIG, L.gsend, L.grecv, wide=True)
    small = Reduce(peers, (L.sg, L.scr, L.syr, L.sxr, L.szr, L.sf), BIG + 2, L.gsend, L.grecv, wide=True)

    def at(stage, unit):
        if unit < BIG:
            getattr(big, stage)(unit)
        elif unit < BIG + 2:
            getattr(half, stage)(unit - BIG)
        else:
            getattr(small, stage)(0)

    def arrive(codes):
        for code in codes:
            stage, unit = code // 100, code % 100
            if stage < 10:
                getattr(weights, ON_WEIGHTS[stage])(unit)
            else:
                at(ON_GRADS[stage - 10], unit)

    def run(name, count, *parts):
        def body(i):
            for k, part in enumerate(parts):
                for when_i, when_k, codes in PLAN[name]:
                    if when_k == k:
                        when(i == when_i, functools.partial(arrive, codes))
                part(i)

        if count == 1:
            body(0)
        else:
            loop(count, body)

    local = []

    def load(a, b):
        copy = pltpu.make_async_copy(a, b, L.lsem.at[len(local)])
        copy.start()
        local.append(copy)

    for j in range(3):
        load(L.wqkv_a.at[j], L.w.at[j])
    for n in range(2):
        load(L.wo_a.at[:, pl.ds(n * 256, 256)], L.w.at[3, pl.ds(n * 256, 256)])
    load(L.tok, L.tok_v)
    for n in range(4):
        load(L.wu_a.at[:, pl.ds(n * 256, 256)], L.w.at[4 + n])
    for n in range(4):
        for k in range(2):
            load(L.wd_a.at[pl.ds(n * 256, 256), pl.ds(k * 256, 256)], L.w.at[8 + n, pl.ds(k * 256, 256)])
    load(L.cot, L.cot_v)
    for name in ("qvb", "ub", "ob", "db", "gains", "shifts", "lengths"):
        load(getattr(L, name + "_h"), getattr(L, name))
    for copy in local[:5] + local[6:18] + local[19:21]:
        copy.wait()
    peers.meet()
    bias_send = [
        remote(L.qvb, L.qvb_b, L.bsem.at[0], L.bsem.at[1], peers.to_y),
        remote(L.ub, L.ub_b, L.bsem.at[2], L.bsem.at[3], peers.to_y),
    ]
    for copy in bias_send:
        copy.start()
    loop(UNITS, lambda u: weights.y(u).start())
    local[5].wait()
    L.widen(L.tok_v, peers.t * caps * slots, L.xs)
    for copy in local[18:19] + local[21:]:
        copy.wait()
    attend = lambda i: [L.attention(4 * i + k) for k in range(4)]

    def rows_and_biases():
        L.widen(L.cot_v, peers.t * caps * slots, L.g)
        for copy in bias_send:
            copy.wait()
        L.biases(1, L.qvb_b, L.ub_b)

    def input_rows():
        L.norm_one_back(L.dx_out)
        L.pack_small(L.sg.at[0])

    def output_rows():
        L.layer_out(L.stage, L.y_out)

    def own(part, unit):
        return lambda n: (part(n), big.c_start_own(unit + n))

    run("norm_one", 1, lambda i: (L.norm_one(), L.biases(0, L.qvb, L.ub)))
    run("qkv_own", 3, L.qkv)
    run("att_own", caps // 4, attend)
    run("widen_g", 1, lambda i: rows_and_biases())
    run("pown", 2, L.project_own)
    run("qkv_other", 3, lambda j: L.qkv(3 + j))
    run("att_other", caps // 4, lambda i: attend(caps // 4 + i))
    run("proj", 2, L.project)
    run("updown", 4, lambda n: L.up(4 + n), lambda n: L.down_grad(4 + n), L.up, own(L.down_grad, 0))
    run("hbug", 4, lambda n: L.hidden_back(4 + n), lambda n: L.up_grad(4 + n), L.hidden_back, own(L.up_grad, 4))
    run("sg", 4, L.second_grad)
    run("ntb", 1, lambda i: L.norm_two_back())
    run("ob1", 1, lambda i: L.out_back(1))
    run("ob0", 1, lambda i: (L.out_back(0), big.c_start_own(8)))
    run("ab", caps // 2, lambda i: [L.attention_back(4 * i + k) for k in range(4)])
    for j in range(3):
        run(f"qg{3 + j}", 1, lambda i: L.qkv_grad(3 + j))
        run(f"qg{j}", 1, lambda i: L.qkv_grad(j))
        for unit in (9 + j,) if j < 2 else (11, 12):
            at("c_start_own", unit)
    run("fg", 4, L.first_grad)
    run("nob", 1, lambda i: (input_rows(), small.c_start_own(0)))
    run("mo", 4, L.mlp_out)
    run("lo", 1, lambda i: output_rows())
    tail = PLAN["tail"][0][2]
    arrive(tail[:-FINAL])
    loop(UNITS, weights.drain)
    loop(9, big.drain)
    arrive(tail[-FINAL:])

    loop(BIG - 9, lambda n: big.drain(9 + n))
    loop(2, half.drain)
    small.drain(0)


def finish(f, hf, s, y, dx, y_out, dx_out, qkv, out, up, down, qvb, ob, ub, db, gg, sh, wide, v1, v2, v3, v4, v5, v6, sem_out, sem_io):
    io = []

    def send(a, b, sem):
        copy = pltpu.make_async_copy(a, b, sem)
        copy.start()
        io.append(copy)

    send(y, y_out, sem_io.at[0])
    send(dx, dx_out, sem_io.at[1])

    def row(first, count):
        return jnp.concatenate([s[0, first + i : first + i + 1, :] for i in range(count)], axis=1)

    for n in range(UNITS):
        if n < BIG:
            wide[n] = f[n].astype(F32)
        else:
            for k in range(2):
                wide[n, k * 256 : (k + 1) * 256, :] = hf[k].astype(F32)
        if n < 4 or n == 8:
            for k in range(2):
                c = pl.ds(k * 256, 256)
                send(wide.at[n, c], down.at[pl.ds(n * 256, 256), c] if n < 4 else out.at[:, c], sem_out.at[2 * n + k])
        elif n < 8:
            send(wide.at[n], up.at[:, pl.ds((n - 4) * 256, 256)], sem_out.at[2 * n])
        else:
            send(wide.at[n], qkv.at[n - 9], sem_out.at[2 * n])
        if n == 1:
            v1[0:1, :], v1[1:2, :] = row(0, 2), row(2, 2)
            v3[...] = row(4, 8)
            v2[...], v4[...] = row(12, 4), row(16, 4)
            v5[0:1, :], v5[1:2, :] = row(20, 4), row(24, 4)
            v6[0:1, :], v6[1:2, :] = row(28, 4), row(32, 4)
            for k, (a, b) in enumerate(((v1, qvb), (v2, ob), (v3, ub), (v4, db), (v5, gg), (v6, sh))):
                send(a, b, sem_io.at[2 + k])
    for copy in io:
        copy.wait()


def shards(depth, tokens, lengths, qkv_weight, qv_bias, out_weight, out_bias, up_weight, up_bias, down_weight, down_bias, norm_gain, norm_shift, cotangent):
    total, width = tokens.shape
    count = lengths.shape[0]
    slots = total // count
    caps = count // 2
    pad = (slots + 15) // 16 * 16
    rws = caps * pad
    V = pl.BlockSpec(memory_space=pltpu.VMEM)
    A = pl.BlockSpec(memory_space=pl.ANY)
    ins = [
        ("tok", tokens, A), ("cot", cotangent, A), ("lengths_h", lengths, A),
        ("wqkv_a", qkv_weight, A), ("wo_a", out_weight, A), ("wu_a", up_weight, A), ("wd_a", down_weight, A),
        ("qvb_h", qv_bias, A), ("ub_h", up_bias, A),
        ("ob_h", out_bias, A), ("db_h", down_bias, A), ("gains_h", norm_gain, A), ("shifts_h", norm_shift, A),
    ]
    outs = [
        ("y_out", (caps * slots, 512), BF16), ("dx_out", (caps * slots, 512), F32),
        ("f", (BIG, 512, 256), BF16), ("hf", (2, 256, 256), BF16), ("sf", (1, 128, 128), F32),
    ]
    vm = pltpu.VMEM
    sems = UNITS + 2, 3 + 3 * depth
    held = [("qvb", qv_bias), ("ub", up_bias), ("ob", out_bias), ("db", down_bias), ("gains", norm_gain), ("shifts", norm_shift)]
    scr = [(n, vm(v.shape, v.dtype)) for n, v in held] + [
        ("lengths", pltpu.SMEM(lengths.shape, jnp.int32)),
        ("tok_v", vm((total, 512), BF16)), ("cot_v", vm((total, 512), BF16)),
        ("stage", vm((total + 16, 512), F32)), ("xs", vm((rws, 512), BF16)), ("g", vm((rws, 512), BF16)),
        ("n1", vm((rws, 512), F32)), ("r1", vm((rws, 128), F32)), ("a1", vm((rws, 512), BF16)),
        ("w", vm((2 * UNITS, 512, 256), BF16)), ("qvb_b", vm((2, 256), BF16)), ("ub_b", vm(up_bias.shape, BF16)),
        ("bias_qkv", vm((6, 1, 256), F32)), ("bias_up", vm((8, 1, 256), F32)),
        ("pqkv", vm((6, rws, 256), BF16)), ("probs", vm((2 * caps, 4 * pad, pad), F32)), ("ctx", vm((2, rws, 256), BF16)),
        ("h1", vm((rws, 512), F32)), ("n2", vm((rws, 512), F32)), ("r2", vm((rws, 128), F32)), ("a2", vm((rws, 512), BF16)),
        ("hid", vm((8, rws, 256), BF16)), ("act", vm((8, rws, 256), F32)), ("du", vm((8, rws, 256), BF16)),
        ("e", vm((rws, 512), F32)), ("dob", vm((rws, 512), BF16)),
        ("dqkv", vm((6, rws, 256), BF16)),
        ("small", vm((8, 512), F32)), ("small_up", vm((8, 1, 256), F32)), ("small_qkv", vm((6, 1, 256), F32)),
        ("grads", vm((BIG, 2, 512, 256), BF16)), ("cr", vm((BIG, 2, 256, 256), BF16)), ("yr", vm((BIG, 256, 256), BF16)),
        ("xr", vm((BIG, 128, 256), BF16)), ("zr", vm((BIG, depth - 1, 128 // depth, 256), BF16)),
        ("hg", vm((2, 2, 256, 256), BF16)), ("hcr", vm((2, 2, 128, 256), BF16)), ("hyr", vm((2, 128, 256), BF16)),
        ("hxr", vm((2, 64, 256), BF16)), ("hzr", vm((2, depth - 1, 64 // depth, 256), BF16)),
        ("sg", vm((1, 2, 128, 128), F32)), ("scr", vm((1, 2, 64, 128), F32)), ("syr", vm((1, 64, 128), F32)),
        ("sxr", vm((1, 32, 128), F32)), ("szr", vm((1, depth - 1, 32 // depth, 128), F32)),
        ("lsem", pltpu.SemaphoreType.DMA((28,))), ("bsem", pltpu.SemaphoreType.DMA((4,))),
        ("wsend", pltpu.SemaphoreType.DMA((UNITS, 3))), ("wrecv", pltpu.SemaphoreType.DMA((UNITS, 3))),
        ("gsend", pltpu.SemaphoreType.DMA(sems)), ("grecv", pltpu.SemaphoreType.DMA(sems)),
    ]
    names = [n for n, _, _ in ins] + [n for n, _, _ in outs] + [n for n, _ in scr]
    y, dx, f, hf, s = pl.pallas_call(
        functools.partial(kernel, caps, slots, pad, names),
        out_shape=[vm(s, d) for _, s, d in outs],
        in_specs=[s for _, _, s in ins],
        out_specs=[V] * len(outs),
        scratch_shapes=[s for _, s in scr],
        compiler_params=pltpu.CompilerParams(vmem_limit_bytes=VLIM, collective_id=0, has_side_effects=True),
        name="layer",
    )(*[v for _, v, _ in ins])
    results = [
        (y.shape, BF16, A), (dx.shape, F32, A), (qkv_weight.shape, F32, A), (out_weight.shape, F32, A),
        (up_weight.shape, F32, A), (down_weight.shape, F32, A),
        (qv_bias.shape, F32, A), ((1, 512), F32, A), ((1, up_bias.shape[0]), F32, A), ((1, 512), F32, A), ((2, 512), F32, A), ((2, 512), F32, A),
    ]
    y, dx, qkv, out, up, down, qvb, ob, ub, db, gg, sh = pl.pallas_call(
        finish,
        out_shape=[jax.ShapeDtypeStruct(s, d) for s, d, _ in results],
        in_specs=[V] * 5,
        out_specs=[s for _, _, s in results],
        scratch_shapes=[
            vm((UNITS, 512, 256), F32), *[vm(s, F32) for s, _, _ in results[6:]], pltpu.SemaphoreType.DMA((2 * UNITS,)), pltpu.SemaphoreType.DMA((8,)),
        ],
        compiler_params=pltpu.CompilerParams(vmem_limit_bytes=12 << 20),
        name="finish",
    )(*[pltpu.with_memory_space_constraint(v, pltpu.VMEM) for v in (f, hf, s, y, dx)])
    return y, dx, qkv, qvb, out, ob[0], up, ub[0], down, db[0], gg, sh


def matmul_plain(left, right):
    return jnp.dot(left, right, preferred_element_type=jnp.float32)


def contract_rows(left, right):
    return lax.dot_general(
        left, right, (((0,), (0,)), ((), ())), preferred_element_type=jnp.float32
    )


def contract_cols(left, right):
    return lax.dot_general(
        left, right, (((1,), (1,)), ((), ())), preferred_element_type=jnp.float32
    )


def plain_norm_stats(values):
    center = values - jnp.mean(values, axis=-1, keepdims=True)
    inv_std = lax.rsqrt(jnp.mean(center * center, axis=-1, keepdims=True) + EPSILON)
    return (center * inv_std, inv_std)


def plain_norm_back(upstream, normed, inv_std, gain_vec):
    scaled = upstream * gain_vec
    inner_mean = jnp.mean(scaled * normed, axis=-1, keepdims=True)
    result = inv_std * (scaled - jnp.mean(scaled, axis=-1, keepdims=True) - normed * inner_mean)
    return (result, jnp.sum(upstream * normed, axis=0), jnp.sum(upstream, axis=0))


def row_slice(values, row_start, share_rows):
    return lax.dynamic_slice_in_dim(values, row_start, share_rows, 0)


def shards_by_heads(
    tokens,
    lengths,
    qkv_weight,
    qv_bias,
    out_weight,
    out_bias,
    up_weight,
    up_bias,
    down_weight,
    down_bias,
    norm_gain,
    norm_shift,
    cotangent,
):
    tensor_count = lax.axis_size("tensor")
    tensor_index = lax.axis_index("tensor")
    share_rows = tokens.shape[0] // tensor_count
    row_start = tensor_index * share_rows
    gains = norm_gain.astype(jnp.float32)
    shifts = norm_shift.astype(jnp.float32)
    total_rows = tokens.shape[0]
    count = lengths.shape[0]
    slots = total_rows // count
    local_width = qkv_weight.shape[2]
    local_heads = local_width // HD
    score_scale = HD ** (-0.5)
    qv_float = qv_bias.astype(jnp.float32)
    token_f = tokens.astype(jnp.float32)
    normed_one, inv_one = plain_norm_stats(token_f)
    first_in = (normed_one * gains[0] + shifts[0]).astype(jnp.bfloat16)
    queries = (matmul_plain(first_in, qkv_weight[0]) + qv_float[0]).astype(jnp.bfloat16)
    keys_all = matmul_plain(first_in, qkv_weight[1]).astype(jnp.bfloat16)
    values_all = (matmul_plain(first_in, qkv_weight[2]) + qv_float[1]).astype(jnp.bfloat16)
    shape4 = (count, slots, local_heads, HD)
    query_four = queries.reshape(shape4)
    key_four = keys_all.reshape(shape4)
    value_four = values_all.reshape(shape4)
    position = jnp.arange(slots)
    allowed = (position[None, :] <= position[:, None])[None, :, :] & (
        position[None, None, :] < lengths[:, None, None]
    )
    allowed = allowed[:, None, :, :]

    def masked_scores():
        raw = jnp.einsum(
            "cihd,cjhd->chij", query_four, key_four, preferred_element_type=jnp.float32
        )
        return jnp.where(allowed, raw * score_scale, -1e30)

    scores = masked_scores()
    row_max = jnp.max(scores, axis=-1, keepdims=True)
    log_total = row_max + jnp.log(jnp.sum(jnp.exp(scores - row_max), axis=-1, keepdims=True))
    probs_low = jnp.exp(scores - log_total).astype(jnp.bfloat16)
    context = jnp.einsum(
        "chij,cjhd->cihd", probs_low, value_four, preferred_element_type=jnp.float32
    )
    context = context.reshape(total_rows, local_width).astype(jnp.bfloat16)
    attn_part = matmul_plain(context, out_weight)
    attn_out = lax.psum(attn_part, "tensor") + out_bias.astype(jnp.float32)
    hidden_res = token_f + attn_out
    normed_two, inv_two = plain_norm_stats(hidden_res)
    second_in = (normed_two * gains[1] + shifts[1]).astype(jnp.bfloat16)
    upper = matmul_plain(second_in, up_weight) + up_bias.astype(jnp.float32)
    sigma = jax.nn.sigmoid(1.702 * upper)
    hidden = (upper * sigma).astype(jnp.bfloat16)
    mlp_part = matmul_plain(hidden, down_weight)
    result_rows = (
        hidden_res
        + lax.psum(mlp_part.astype(jnp.bfloat16), "tensor").astype(jnp.float32)
        + down_bias.astype(jnp.float32)
    )
    layer_out = row_slice(result_rows, row_start, share_rows).astype(jnp.bfloat16)
    grad_f = cotangent.astype(jnp.float32)
    down_grad = contract_rows(hidden, cotangent)
    down_bias_grad = jnp.sum(grad_f, axis=0)
    hidden_grad = contract_cols(cotangent, down_weight)
    upper_grad = (hidden_grad * (sigma + 1.702 * upper * sigma * (1.0 - sigma))).astype(
        jnp.bfloat16
    )
    up_grad = contract_rows(second_in, upper_grad)
    up_bias_grad = jnp.sum(upper_grad.astype(jnp.float32), axis=0)
    second_part = contract_cols(upper_grad, up_weight)
    second_grad = lax.psum(second_part, "tensor")
    residual_back, gain_two, shift_two = plain_norm_back(second_grad, normed_two, inv_two, gains[1])
    residual_full = grad_f + residual_back
    branch_grad = residual_full.astype(jnp.bfloat16)
    out_bias_grad = jnp.sum(branch_grad.astype(jnp.float32), axis=0)
    out_grad = contract_rows(context, branch_grad)
    context_grad = contract_cols(branch_grad, out_weight).astype(jnp.bfloat16).reshape(shape4)
    probs = jnp.exp(masked_scores() - log_total)
    probs_low = probs.astype(jnp.bfloat16)
    value_grad = jnp.einsum(
        "chij,cihd->cjhd", probs_low, context_grad, preferred_element_type=jnp.float32
    )
    prob_grad = jnp.einsum(
        "cihd,cjhd->chij", context_grad, value_four, preferred_element_type=jnp.float32
    )
    score_grad = probs * (prob_grad - jnp.sum(prob_grad * probs, axis=-1, keepdims=True))
    score_grad = score_grad.astype(jnp.bfloat16)
    query_grad = (
        jnp.einsum("chij,cjhd->cihd", score_grad, key_four, preferred_element_type=jnp.float32)
        * score_scale
    )
    key_grad = (
        jnp.einsum("chij,cihd->cjhd", score_grad, query_four, preferred_element_type=jnp.float32)
        * score_scale
    )
    query_grad = query_grad.reshape(total_rows, local_width).astype(jnp.bfloat16)
    key_grad = key_grad.reshape(total_rows, local_width).astype(jnp.bfloat16)
    value_grad = value_grad.reshape(total_rows, local_width).astype(jnp.bfloat16)
    qkv_grad = jnp.stack(
        [
            contract_rows(first_in, query_grad),
            contract_rows(first_in, key_grad),
            contract_rows(first_in, value_grad),
        ]
    )
    qv_bias_grad = jnp.stack(
        [
            jnp.sum(query_grad.astype(jnp.float32), axis=0),
            jnp.sum(value_grad.astype(jnp.float32), axis=0),
        ]
    )
    first_part = (
        contract_cols(query_grad, qkv_weight[0])
        + contract_cols(key_grad, qkv_weight[1])
        + contract_cols(value_grad, qkv_weight[2])
    )
    first_grad = lax.psum(first_part.astype(jnp.bfloat16), "tensor").astype(jnp.float32)
    input_back, gain_one, shift_one = plain_norm_back(first_grad, normed_one, inv_one, gains[0])
    input_grad = row_slice(residual_full + input_back, row_start, share_rows)
    gain_grads = jnp.stack([gain_one, gain_two])
    shift_grads = jnp.stack([shift_one, shift_two])
    summed = (
        lax.psum(qkv_grad.astype(jnp.bfloat16), "dp").astype(jnp.float32),
        lax.psum(qv_bias_grad.astype(jnp.bfloat16), "dp").astype(jnp.float32),
        lax.psum(out_grad.astype(jnp.bfloat16), "dp").astype(jnp.float32),
        lax.psum(out_bias_grad.astype(jnp.bfloat16), "dp").astype(jnp.float32),
        lax.psum(up_grad.astype(jnp.bfloat16), "dp").astype(jnp.float32),
        lax.psum(up_bias_grad.astype(jnp.bfloat16), "dp").astype(jnp.float32),
        lax.psum(down_grad.astype(jnp.bfloat16), "dp").astype(jnp.float32),
        lax.psum(down_bias_grad.astype(jnp.bfloat16), "dp").astype(jnp.float32),
        lax.psum(gain_grads.astype(jnp.bfloat16), "dp").astype(jnp.float32),
        lax.psum(shift_grads.astype(jnp.bfloat16), "dp").astype(jnp.float32),
    )
    return (
        layer_out,
        input_grad,
        summed[0],
        summed[1],
        summed[2],
        summed[3],
        summed[4],
        summed[5],
        summed[6],
        summed[7],
        summed[8],
        summed[9],
    )


def solution(mesh):
    dp, tensor = mesh.shape["dp"], mesh.shape["tensor"]
    if tensor == 2 and dp == 16:
        body = functools.partial(shards, dp // 4)
    else:
        body = shards_by_heads
    return jax.shard_map(
        body,
        mesh=mesh,
        in_specs=(P("dp", None), P("dp"), P(None, None, "tensor"), P(None, "tensor"), P("tensor", None), P(), P(None, "tensor"), P("tensor"), P("tensor", None), P(), P(), P(), P("dp", None)),
        out_specs=(P(("dp", "tensor"), None), P(("dp", "tensor"), None), P(None, None, "tensor"), P(None, "tensor"), P("tensor", None), P(), P(None, "tensor"), P("tensor"), P("tensor", None), P(), P(), P()),
        check_vma=False,
    )
```
